32 devices in a mesh: wide: 8 (over y, x, core), narrow: 4 (over z).
Axes of the slice: x: 2, y: 2, z: 4, core: 2. Of those that a mesh axis runs over, the one named last changes fastest.
Arguments:
- hidden_in: bfloat16 [4096, 1024], P(('wide', 'narrow')), may hold values from -6 to 6
- w_qkv: bfloat16 [2, 1024, 3072], P(None, ('wide', 'narrow')), may hold values from -0.1875 to 0.1875
- w_proj: bfloat16 [2, 1024, 1024], P(None, ('wide', 'narrow')), may hold values from -0.1875 to 0.1875
- w_mlp: bfloat16 [2, 4096, 2048], P(None, ('wide', 'narrow')), may hold values from -0.1875 to 0.1875
- norm_params: bfloat16 [2, 1024, 8], P(None, ('wide', 'narrow')), may hold values from -1.2 to 1.7, as said below
- grad_output: bfloat16 [4096, 1024], P(('wide', 'narrow')), may hold values from -6 to 6
- corpus_id: int32 [4096], P(('wide', 'narrow')), may hold values from 0 to 7
- corpus_weight: float32 [8], replicated, may hold values from 0.25 to 4
Outputs:
- hidden_out: bfloat16 [4096, 1024], P(('wide', 'narrow'))
- grad_input: float32 [4096, 1024], P(('wide', 'narrow'))
- grad_qkv: float32 [2, 1024, 3072], P(None, ('wide', 'narrow'))
- grad_proj: float32 [2, 1024, 1024], P(None, ('wide', 'narrow'))
- grad_mlp: float32 [2, 4096, 2048], P(None, ('wide', 'narrow'))
- grad_norms: float32 [2, 1024, 8], P(None, ('wide', 'narrow'))
The draws below stay inside these ranges and needn't reach their ends.
Inputs may be any that keep to these rules, and one draw needn't show every extreme that they name: `norm_params`: columns 0, 2, 4, 6 are gains, columns 1, 3, 5, 7 biases.
All inputs are finite; a program needn't handle non-finite values.
Results may differ from the reference program's by a relative error of at most 0.028.
Values may be sent and summed in bfloat16 or wider, within the bound.
A program may use at most 256 MiB of HBM per device.

```python
import math
import jax
import jax.numpy as jnp
from jax import lax

D = 1024
HEADS = 16
HEAD_DIM = 64
FF = 4096
LAYERS = 2
CORPORA = 8
KEY_BLOCK = 512
LENGTH = 512
SEQS = 8
TOKENS = 4096


def draw_norm_params(key, part):
    gain_key, bias_key = jax.random.split(jax.random.fold_in(key, 11))
    shape = (LAYERS, D, 8)
    gains = jax.random.uniform(gain_key, shape, jnp.float32, 0.6, 1.5)
    biases = jnp.clip(0.3 * jax.random.normal(bias_key, shape, jnp.float32), -1.18, 1.18)
    column = jnp.arange(8, dtype=jnp.int32) % 2
    return jnp.where(column[None, None, :] == 0, gains, biases).astype(jnp.bfloat16)


def place_ends(array, stream_key, least, high):
    shape = array.shape
    index_at = [jax.random.randint(jax.random.fold_in(stream_key, axis), (), 0, shape[axis]) for axis in range(len(shape))]
    array = array.at[tuple(index_at)].set(least)
    longest = shape.index(max(shape))
    index_at[longest] = (index_at[longest] + 1) % shape[longest]
    return array.at[tuple(index_at)].set(high)


def with_spikes(values, key, source, target, shards_of, factor):
    owner, partner = [(jnp.arange(values.shape[dim]) // (values.shape[dim] // shards_of)).reshape([-1 if axis == dim else 1 for axis in range(values.ndim)]) for dim in (source, target)]
    chosen = jax.random.permutation(key, shards_of)[partner]
    strong = (owner == chosen) | (owner == (partner + shards_of // 2) % shards_of)
    return jnp.where(strong, factor * values, values)


def steps_of(key, dims, cuts, low, high):
    level, own = 1.0, jax.random.fold_in(key, 6)
    for dim, blocks in cuts:
        draws = jnp.exp(jax.random.uniform(jax.random.fold_in(own, dim), (blocks,), jnp.float32, low / len(cuts), high / len(cuts)))
        level = level * jnp.repeat(draws, dims[dim] // blocks).reshape([-1 if axis == dim else 1 for axis in range(len(dims))])
    return level


def normal_values(key, shape, scale, most, shards=(), kind=jnp.bfloat16):
    drawn = scale * jax.random.normal(key, shape, jnp.float32)
    if shards:
        drawn = drawn * steps_of(key, shape, shards, -0.22, 0.18)
    return jnp.clip(drawn, -most, most).astype(kind)


def noise_with(rng, shape, deviation, bound, cuts, heavy, kind=jnp.bfloat16):
    array = deviation * jax.random.normal(rng, shape, jnp.float32)
    if cuts:
        array = array * steps_of(rng, shape, cuts, -0.22, 0.18)
    return jnp.clip(with_spikes(array, jax.random.fold_in(rng, 3), *heavy), -bound, bound).astype(kind)


def setup_inputs(seed: int = 0) -> dict:
    seeds = jax.random.split(jax.random.key(seed), 9)
    return {
        "hidden_in": normal_values(seeds[0], (TOKENS, D), 1.0, 6.0, ((0, 32),)),
        "w_qkv": normal_values(seeds[1], (LAYERS, D, 3 * D), D ** -0.5, 0.1875, ((1, 32),)),
        "w_proj": normal_values(seeds[2], (LAYERS, D, D), D ** -0.5, 0.1875, ((1, 32),)),
        "w_mlp": normal_values(seeds[3], (LAYERS, FF, 2 * D), D ** -0.5, 0.1875, ((1, 32),)),
        "norm_params": draw_norm_params(jax.random.fold_in(seeds[8], 71), 0),
        "grad_output": noise_with(seeds[5], (TOKENS, D), 1.0, 6.0, ((0, 32),), (0, 1, 32, 2.75)),
        "corpus_id": place_ends(jax.random.randint(seeds[6], (TOKENS,), 0, CORPORA), jax.random.fold_in(seeds[6], 1), 0, CORPORA - 1).astype(jnp.int32),
        "corpus_weight": jnp.clip(jnp.exp(jax.random.uniform(seeds[7], (CORPORA,), jnp.float32, math.log(0.25), math.log(4.0))), 0.25, 4.0),
    }


EPS = 1e-05
MASKED = -1e+30
ROPE_BASE = 10000.0
HIGH = lax.Precision.HIGHEST

@jax.custom_vjp
def low(v):
    return lax.optimization_barrier(v.astype(jnp.bfloat16)).astype(jnp.float32)

@jax.custom_vjp
def low_back(v):
    return v

def low_keep(v):
    return (low(v), None)

def low_pass(kept, grad):
    return (grad,)

def back_keep(v):
    return (v, None)

def back_low(kept, grad):
    return (low(grad),)
low.defvjp(low_keep, low_pass)
low_back.defvjp(back_keep, back_low)

def standardize(inputs):
    centre = lax.optimization_barrier(jnp.mean(inputs, axis=-1, keepdims=True))
    centered = inputs - centre
    spread = lax.optimization_barrier(jnp.mean(centered * centered, axis=-1, keepdims=True))
    return centered * lax.rsqrt(spread + EPS)

def layer_norm(inputs, gain_vec, bias_vec):
    return standardize(inputs) * gain_vec + bias_vec

def rotate(inputs, positions):
    half = HEAD_DIM // 2
    token_count = inputs.shape[0]
    freqs = ROPE_BASE ** (-jnp.arange(half, dtype=jnp.float32) / half)
    angles = positions.astype(jnp.float32)[:, None] * freqs[None, :]
    cosine = jnp.cos(angles)[:, None, :]
    sine = jnp.sin(angles)[:, None, :]
    shaped = inputs.reshape(token_count, HEADS, HEAD_DIM)
    first = shaped[..., :half]
    second = shaped[..., half:]
    turned = jnp.concatenate([first * cosine - second * sine, second * cosine + first * sine], axis=-1)
    return turned.reshape(token_count, HEADS * HEAD_DIM)

def attend(queries, keys, values):
    length = queries.shape[0]
    query_heads = queries.reshape(length, HEADS, HEAD_DIM)
    key_heads = keys.reshape(length, HEADS, HEAD_DIM)
    value_heads = values.reshape(length, HEADS, HEAD_DIM)
    key_pos = jnp.arange(length, dtype=jnp.int32)

    def one_block(block_number):
        offset = (block_number * KEY_BLOCK).astype(jnp.int32)
        block_query = lax.dynamic_slice_in_dim(query_heads, offset, KEY_BLOCK, 0)
        scores = jnp.einsum('qhd,khd->hqk', block_query, key_heads, precision=HIGH) * HEAD_DIM ** (-0.5)
        scores = low_back(scores)
        query_pos = offset + jnp.arange(KEY_BLOCK, dtype=jnp.int32)
        allowed = key_pos[None, :] <= query_pos[:, None]
        scores = jnp.where(allowed[None], scores, MASKED)
        weights = low(jax.nn.softmax(scores, axis=-1))
        return jnp.einsum('hqk,khd->qhd', weights, value_heads, precision=HIGH)
    blocks = lax.map(jax.checkpoint(one_block), jnp.arange(length // KEY_BLOCK, dtype=jnp.int32))
    return blocks.reshape(length, HEADS * HEAD_DIM)

def peri_layer(state, qkv_weight, proj_weight, mlp_weight, norm_cols):
    positions = jnp.arange(TOKENS, dtype=jnp.int32) % LENGTH
    first_in = low(layer_norm(state, norm_cols[:, 0], norm_cols[:, 1]))
    qkv = low_back(jnp.dot(first_in, qkv_weight, precision=HIGH))
    queries = low(rotate(qkv[:, :D], positions))
    keys = low(rotate(qkv[:, D:2 * D], positions))
    values = low(qkv[:, 2 * D:])
    per_seq = (queries.reshape(SEQS, LENGTH, D), keys.reshape(SEQS, LENGTH, D), values.reshape(SEQS, LENGTH, D))
    attended = lax.map(lambda triple: attend(triple[0], triple[1], triple[2]), per_seq).reshape(TOKENS, D)
    attended = low_back(low(attended))
    branch = low_back(jnp.dot(attended, proj_weight.T, precision=HIGH))
    middle = state + layer_norm(branch, norm_cols[:, 2], norm_cols[:, 3])
    ffn_in = low(layer_norm(middle, norm_cols[:, 4], norm_cols[:, 5]))
    pre = low_back(jnp.dot(ffn_in, mlp_weight[:, :D].T, precision=HIGH))
    hidden = low(jax.nn.gelu(pre, approximate=True))
    mlp_out = low_back(jnp.dot(hidden, mlp_weight[:, D:], precision=HIGH))
    return middle + layer_norm(mlp_out, norm_cols[:, 6], norm_cols[:, 7])

def forward(hidden, qkv_all, proj_all, mlp_all, norm_all):
    state = hidden
    for layer_index in range(LAYERS):
        state = peri_layer(state, qkv_all[layer_index], proj_all[layer_index], mlp_all[layer_index], norm_all[layer_index])
    return state

def reference(hidden_in, w_qkv, w_proj, w_mlp, norm_params, grad_output, corpus_id, corpus_weight):
    hidden = hidden_in.astype(jnp.float32)
    qkv_all = w_qkv.astype(jnp.float32)
    proj_all = w_proj.astype(jnp.float32)
    mlp_all = w_mlp.astype(jnp.float32)
    norm_all = norm_params.astype(jnp.float32)
    result, pullback = jax.vjp(forward, hidden, qkv_all, proj_all, mlp_all, norm_all)
    match = corpus_id[:, None] == jnp.arange(CORPORA, dtype=jnp.int32)[None, :]
    row_scale = lax.optimization_barrier(jnp.sum(jnp.where(match, corpus_weight[None, :], 0.0), axis=1))
    cotangent = grad_output.astype(jnp.float32) * row_scale[:, None]
    grad_hidden, grad_qkv, grad_proj, grad_mlp, grad_norms = pullback(cotangent)
    return (result.astype(jnp.bfloat16), grad_hidden, grad_qkv, grad_proj, grad_mlp, grad_norms)
```

```python
from functools import partial

import jax
import jax.numpy as jnp
from jax import lax
from jax.experimental import pallas as pl
from jax.experimental.pallas import tpu as pltpu
from jax.sharding import PartitionSpec as P

HEADS = 16
HEAD_DIM = 64
FF = 4096
LAYERS = 2
EPS = 1e-05
MASKED = -1e30
ROPE_BASE = 10000.0
MESH = pl.DeviceIdType.MESH
BF = jnp.bfloat16
F32 = jnp.float32
LANES = 128


def dot_nn(left, right):
    return lax.dot_general(left, right, (((1,), (0,)), ((), ())), preferred_element_type=F32)


def dot_nt(left, right):
    return lax.dot_general(left, right, (((1,), (1,)), ((), ())), preferred_element_type=F32)


def dot_tn(left, right):
    return lax.dot_general(left, right, (((0,), (0,)), ((), ())), preferred_element_type=F32)


def normalize(inputs):
    centre = jnp.mean(inputs, axis=-1, keepdims=True)
    centered = inputs - centre
    rstd = lax.rsqrt(jnp.mean(centered * centered, axis=-1, keepdims=True) + EPS)
    return centered * rstd, rstd


def norm_back(nhat, rstd, grad, gain):
    scaled = grad * gain
    mean_f = jnp.mean(scaled, axis=-1, keepdims=True)
    mean_fn = jnp.mean(scaled * nhat, axis=-1, keepdims=True)
    return rstd * (scaled - mean_f - nhat * mean_fn)


GELU_S = 0.7978845608028654
GELU_A = 0.044715


def gelu(pre):
    return 0.5 * pre * (1.0 + jnp.tanh(GELU_S * (pre + GELU_A * pre * pre * pre)))


def gelu_slope(pre):
    square = pre * pre
    turned = jnp.tanh(GELU_S * (pre + GELU_A * pre * square))
    inner = GELU_S * (1.0 + 3.0 * GELU_A * square)
    return 0.5 * (1.0 + turned) + 0.5 * pre * (1.0 - turned * turned) * inner


def kernel_body(
    dims,
    hid_ref, gout_ref, scale_ref, nrm_ref, cos_ref, sin_ref, wa_ref, wm_ref,
    out_h, out_g, out_qkv, out_proj, out_mlp, out_n,
    wa, wm, a1, a3, dm, db, qs_, ks_, vs_, att, st, br, mid, mo,
    pre_s, hid_s, dpre_s, datt, dq_s, dk_s, dv_s, dqkv,
    rs_send, rs_recv, acc, hid_p, g_p, sc_p, outh_s, g,
    gmb, gmr, gmz, stage, gab, gar, gaz, gax_s, gax_r,
    npar, ngrad, n_send, n_x, n_z, n_m,
    perm_s, perm_r, loc, a2a_s, a2a_r, ag_s, ag_r, rs_s, rs_r,
    zw_s, zw_r, mw_s, mw_r, zg_s, zg_r, mg_s, mg_r, xg_s, xg_r,
    nx_s, nx_r, nz_s, nz_r, nm_s, nm_r, credit,
):
    C, N, TB, D, FQ, UQ, RW, US, AW = dims
    T = C * TB
    HPC = FQ // HEAD_DIM
    HALF = N * US
    w = lax.axis_index("wide")
    n = lax.axis_index("narrow")
    c = w // 2
    k = lax.rem(w, 2)
    mate = (2 * c + (1 - k), n)
    swap = (2 * n + k, c)

    def chip(j):
        return lax.rem(c + j, C)

    def xy(j):
        return (2 * chip(j) + k, n)

    def zp(j):
        return (w, lax.rem(n + j, N))

    def zfrom(j):
        return lax.rem(n + N - j, N)

    def cfrom(j):
        return lax.rem(c + C - j, C)

    def remote(src, dst, ssem, rsem, device):
        return pltpu.make_async_remote_copy(
            src_ref=src, dst_ref=dst, send_sem=ssem, recv_sem=rsem,
            device_id=device, device_id_type=MESH,
        )

    barrier = pltpu.get_barrier_semaphore()
    partners = [xy(j) for j in range(1, C)] + [zp(j) for j in range(1, N)] + [mate]
    for device in partners:
        pl.semaphore_signal(barrier, inc=1, device_id=device, device_id_type=MESH)

    @pl.when(c != n)
    def _():
        pl.semaphore_signal(barrier, inc=1, device_id=swap, device_id_type=MESH)

    pl.semaphore_wait(barrier, len(partners) + jnp.where(c != n, 1, 0))

    def a2a(l, j):
        return remote(
            wa_ref.at[chip(j), l], wa.at[l, c, k, n], a2a_s.at[l, j - 1], a2a_r.at[l, j - 1], xy(j)
        )

    def a2a_in(l, j):
        there = wa.at[l, cfrom(j), k, n]
        return remote(there, there, a2a_s.at[l, j - 1], a2a_r.at[l, j - 1], xy(j))

    for l in range(LAYERS):
        for j in range(1, C):
            a2a(l, j).start()

    def own_wa(l):
        return pltpu.make_async_copy(wa_ref.at[c, l], wa.at[l, c, k, n], loc.at[l])

    def own_wm(l):
        return pltpu.make_async_copy(wm_ref.at[l], wm.at[l, k, n], loc.at[LAYERS + l])

    for l in range(LAYERS):
        own_wa(l).start()
        own_wm(l).start()

    perm = [
        remote(hid_ref, hid_p, perm_s.at[0], perm_r.at[0], swap),
        remote(gout_ref, g_p, perm_s.at[1], perm_r.at[1], swap),
        remote(scale_ref, sc_p, perm_s.at[2], perm_r.at[2], swap),
        remote(outh_s, out_h, perm_s.at[3], perm_r.at[3], swap),
        remote(g, out_g, perm_s.at[4], perm_r.at[4], swap),
    ]

    @pl.when(c != n)
    def _():
        for copy in perm[:3]:
            copy.start()

    def n_copy(way, rnd, j):
        if rnd == 0:
            return remote(n_send.at[way, 0], n_x.at[way, j - 1], nx_s.at[way, j - 1], nx_r.at[way, j - 1], xy(j))
        if rnd == 1:
            return remote(n_send.at[way, 1], n_z.at[way, j - 1], nz_s.at[way, j - 1], nz_r.at[way, j - 1], zp(j))
        return remote(n_send.at[way, 2], n_m.at[way], nm_s.at[way], nm_r.at[way], mate)

    n_count = (C, N, 2)

    def n_start(way, rnd, value):
        n_send[way, rnd] = value
        for j in range(1, n_count[rnd]):
            n_copy(way, rnd, j).start()

    def n_finish(way, rnd):
        total = n_send[way, rnd]
        for j in range(1, n_count[rnd]):
            n_copy(way, rnd, j).wait()
            total = total + (n_x[way, j - 1] if rnd == 0 else n_z[way, j - 1] if rnd == 1 else n_m[way])
        return total

    first = (w * N + n) * RW
    spot = lax.broadcasted_iota(jnp.int32, (RW, D), 1) == (
        lax.broadcasted_iota(jnp.int32, (RW, D), 0) + first
    )
    n_start(0, 0, dot_nn(nrm_ref[...].astype(F32), spot.astype(F32)))

    def wref(s):
        return wa.at[s // 2] if s % 2 == 0 else wm.at[s // 2]

    def zslice(s, at):
        return wa.at[s // 2, :, k, at] if s % 2 == 0 else wm.at[s // 2, k, at]

    def half(s, core):
        return wa.at[s // 2, :, core] if s % 2 == 0 else wm.at[s // 2, core]

    def w_send(s):
        for j in range(1, N):
            remote(zslice(s, n), zslice(s, n), zw_s.at[s, j - 1], zw_r.at[s, j - 1], zp(j)).start()

    def w_arrive(s):
        for j in range(1, N):
            there = zslice(s, zfrom(j))
            remote(there, there, zw_s.at[s, j - 1], zw_r.at[s, j - 1], zp(j)).wait_recv()
        remote(half(s, k), half(s, k), mw_s.at[s], mw_r.at[s], mate).start()

    def w_ready(s):
        remote(half(s, 1 - k), half(s, 1 - k), mw_s.at[s], mw_r.at[s], mate).wait_recv()

    def w_drain(s):
        for j in range(1, N):
            remote(zslice(s, n), zslice(s, n), zw_s.at[s, j - 1], zw_r.at[s, j - 1], zp(j)).wait_send()
        remote(half(s, k), half(s, k), mw_s.at[s], mw_r.at[s], mate).wait_send()

    for j in range(1, C):
        a2a_in(0, j).wait_recv()
    own_wa(0).wait()
    w_send(0)

    n_start(0, 1, n_finish(0, 0))
    n_start(0, 2, n_finish(0, 1))
    npar[...] = n_finish(0, 2)
    ngrad[...] = jnp.zeros_like(ngrad)

    def gain(l, col):
        return npar[pl.ds(l * 8 + col, 1), :]

    def ag_start(p, buf, value):
        buf[c] = value
        for j in range(1, C):
            remote(buf.at[c], buf.at[c], ag_s.at[p, j - 1], ag_r.at[p, j - 1], xy(j)).start()

    def ag_wait(p, buf):
        for j in range(1, C):
            there = buf.at[cfrom(j)]
            remote(there, there, ag_s.at[p, j - 1], ag_r.at[p, j - 1], xy(j)).wait_recv()

    def ag_drain(p, buf):
        for j in range(1, C):
            remote(buf.at[c], buf.at[c], ag_s.at[p, j - 1], ag_r.at[p, j - 1], xy(j)).wait_send()

    def rs_copy(p, j):
        return remote(rs_send.at[j - 1], rs_recv.at[j - 1], rs_s.at[p, j - 1], rs_r.at[p, j - 1], xy(j))

    def rs_loop(p, part):
        def step(i, carry):
            value = part(chip(i))

            @pl.when(i < C)
            def _():
                rs_send[i - 1] = value.astype(BF)
                rs_copy(p, i).start()

            @pl.when(i == C)
            def _():
                acc[...] = value

            return carry

        lax.fori_loop(1, C + 1, step, 0)

    def rs_finish(p):
        total = acc[...]
        for j in range(1, C):
            rs_copy(p, j).wait()
            total = total + rs_recv[j - 1].astype(F32)
        return total

    lane = lax.broadcasted_iota(jnp.int32, (TB, FQ), 1)
    low_half = lax.rem(lane, HEAD_DIM) < HEAD_DIM // 2
    head_of = lane // HEAD_DIM

    def tables(b):
        rows = pl.ds(b * TB, TB)
        reps = FQ // LANES
        return (
            jnp.concatenate([cos_ref[rows, :]] * reps, axis=1),
            jnp.concatenate([sin_ref[rows, :]] * reps, axis=1),
        )

    def swapped(u):
        half_dim = HEAD_DIM // 2
        return jnp.where(
            low_half, pltpu.roll(u, FQ - half_dim, 1), pltpu.roll(u, half_dim, 1)
        )

    def w_qkv(l):
        return wa[l, :, :, :, :, 0 : 3 * FQ].reshape(D, 3 * FQ)

    def w_proj(l):
        return wa[l, :, :, :, :, 3 * FQ : 4 * FQ].reshape(D, FQ)

    def w_up(l):
        return wm[l, :, :, :, 0:D].reshape(UQ, D)

    def w_down(l):
        return wm[l, :, :, :, D : 2 * D].reshape(UQ, D)

    def head_probs(l, b, h):
        q = jnp.where(head_of == h, qs_[l, b], jnp.zeros((), BF))
        scores = dot_nt(q, ks_[l].reshape(T, FQ)) * HEAD_DIM ** (-0.5)
        row = lax.broadcasted_iota(jnp.int32, (TB, T), 0) + b * TB
        col = lax.broadcasted_iota(jnp.int32, (TB, T), 1)
        scores = jnp.where(col <= row, scores, MASKED)
        peak = jnp.max(scores, axis=-1, keepdims=True)
        weights = jnp.exp(scores - peak)
        return q, weights * (1.0 / jnp.sum(weights, axis=-1, keepdims=True))

    @pl.when(c != n)
    def _():
        for copy in perm[:3]:
            copy.wait_recv()

    @pl.when(c == n)
    def _():
        hid_p[...] = hid_ref[...]
        g_p[...] = gout_ref[...]
        sc_p[...] = scale_ref[...]

    st[0] = hid_p[...].astype(F32)
    for l in range(LAYERS):
        nhat, unused = normalize(st[l])
        ag_start(2 * l, a1.at[l], (nhat * gain(l, 0) + gain(l, 1)).astype(BF))
        w_arrive(2 * l)
        if l == 0:
            own_wm(0).wait()
        else:
            own_wm(1).wait()
        w_send(2 * l + 1)
        w_ready(2 * l)
        ag_wait(2 * l, a1.at[l])

        def qkv_step(b, carry, l=l):
            u = dot_nn(a1[l, b], w_qkv(l))
            cosine, sine = tables(b)
            uq = u[:, 0:FQ]
            uk = u[:, FQ : 2 * FQ]
            qs_[l, b] = (uq * cosine + swapped(uq) * sine).astype(BF)
            ks_[l, b] = (uk * cosine + swapped(uk) * sine).astype(BF)
            vs_[l, b] = u[:, 2 * FQ :].astype(BF)
            return carry

        lax.fori_loop(0, C, qkv_step, 0)

        def attend(b, l=l):
            def head_step(h, total):
                unused, probs = head_probs(l, b, h)
                mixed = dot_nn(probs.astype(BF), vs_[l].reshape(T, FQ))
                return jnp.where(head_of == h, mixed, total)

            low = lax.fori_loop(0, HPC, head_step, jnp.zeros((TB, FQ), F32)).astype(BF)
            att[l, b] = low
            return dot_nt(low, w_proj(l))

        rs_loop(2 * l, attend)
        branch = rs_finish(2 * l)
        ag_drain(2 * l, a1.at[l])
        br[l] = branch
        nhat, unused = normalize(branch)
        middle = st[l] + nhat * gain(l, 2) + gain(l, 3)
        mid[l] = middle
        nhat, unused = normalize(middle)
        ag_start(2 * l + 1, a3.at[l], (nhat * gain(l, 4) + gain(l, 5)).astype(BF))
        w_arrive(2 * l + 1)
        if l + 1 < LAYERS:
            for j in range(1, C):
                a2a_in(l + 1, j).wait_recv()
            own_wa(l + 1).wait()
            w_send(2 * l + 2)
        w_ready(2 * l + 1)
        ag_wait(2 * l + 1, a3.at[l])

        def feed(b, l=l):
            hidden = gelu(dot_nt(a3[l, b], w_up(l))).astype(BF)
            return dot_nn(hidden, w_down(l))

        rs_loop(2 * l + 1, feed)
        mlp_out = rs_finish(2 * l + 1)
        ag_drain(2 * l + 1, a3.at[l])
        mo[l] = mlp_out
        nhat, unused = normalize(mlp_out)
        new_state = mid[l] + nhat * gain(l, 6) + gain(l, 7)
        if l + 1 < LAYERS:
            st[l + 1] = new_state
        else:
            outh_s[...] = new_state.astype(BF)
            g[...] = g_p[...].astype(F32) * sc_p[:, 0:1]

    @pl.when(c != n)
    def _():
        perm[3].start()

    @pl.when(c == n)
    def _():
        out_h[...] = outh_s[...]

    for s in range(2 * LAYERS):
        w_drain(s)

    def add_norm(l, col, grad, nhat):
        ngrad[pl.ds(l * 8 + col, 1), :] = jnp.sum(grad * nhat, axis=0, keepdims=True)
        ngrad[pl.ds(l * 8 + col + 1, 1), :] = jnp.sum(grad, axis=0, keepdims=True)

    def gm_of(l):
        return gmb if l == LAYERS - 1 else wm.at[LAYERS - 1]

    def ga_of(l):
        return gab if l == LAYERS - 1 else wa.at[LAYERS - 1]

    def gm_half(l, core):
        dst = gm_of(l)
        per = LANES // US

        def chunk(i, carry):
            off = pl.multiple_of(core * HALF + i * LANES, LANES)
            up = dot_tn(dpre_s[:, pl.ds(off, LANES)], a3[l].reshape(T, D))
            down = dot_tn(hid_s[:, pl.ds(off, LANES)], dm[...].reshape(T, D))
            rows = pl.ds(i * per, per)
            dst[core, rows, :, 0:D] = up.astype(BF).reshape(per, US, D)
            dst[core, rows, :, D : 2 * D] = down.astype(BF).reshape(per, US, D)
            return carry

        lax.fori_loop(0, HALF // LANES, chunk, 0)

    def gm_mate(l):
        return remote(gm_of(l).at[1 - k], gmr, mg_s.at[2 * l + 1], mg_r.at[2 * l + 1], mate)

    def gm_z(l, j):
        return remote(
            gm_of(l).at[k, lax.rem(n + j, N)], gmz.at[l, j - 1],
            zg_s.at[2 * l + 1, j - 1], zg_r.at[2 * l + 1, j - 1], zp(j),
        )

    def gm_spread(l):
        gm_mate(l).wait_recv()
        src = gm_of(l)

        def add(i, carry):
            at = lax.rem(n + i, N)
            src[k, at] = (src[k, at].astype(F32) + gmr[at].astype(F32)).astype(BF)

            @pl.when(i < N)
            def _():
                gm_z(l, i).start()

            return carry

        lax.fori_loop(1, N + 1, add, 0)

    def ga_all(l):
        dst = ga_of(l)
        rows = 2 * N * RW

        def chunk(i, carry):
            off = pl.multiple_of(i * rows, LANES)
            grad_a = dot_tn(a1[l, :, :, pl.ds(off, rows)].reshape(T, rows), dqkv[...])
            grad_p = dot_tn(db[:, :, pl.ds(off, rows)].reshape(T, rows), att[l].reshape(T, FQ))
            dst[i, :, :, :, 0 : 3 * FQ] = grad_a.astype(BF).reshape(2, N, RW, 3 * FQ)
            dst[i, :, :, :, 3 * FQ : 4 * FQ] = grad_p.astype(BF).reshape(2, N, RW, FQ)
            return carry

        lax.fori_loop(0, C, chunk, 0)

    def ga_mate(l):
        return remote(ga_of(l).at[:, 1 - k], gar.at[l], mg_s.at[2 * l], mg_r.at[2 * l], mate)

    def ga_z(l, j):
        return remote(
            ga_of(l).at[:, k, lax.rem(n + j, N)], gaz.at[l, j - 1],
            zg_s.at[2 * l, j - 1], zg_r.at[2 * l, j - 1], zp(j),
        )

    def ga_spread(l):
        ga_mate(l).wait_recv()
        src = ga_of(l)
        src[:, k] = (src[:, k].astype(F32) + gar[l].astype(F32)).astype(BF)
        for j in range(1, N):
            ga_z(l, j).start()

    for l in reversed(range(LAYERS)):
        p = 2 * LAYERS + 2 * (LAYERS - 1 - l)
        grad = g[...]
        nhat, rstd = normalize(mo[l])
        ag_start(p, dm, norm_back(nhat, rstd, grad, gain(l, 6)).astype(BF))
        add_norm(l, 6, grad, nhat)
        if l + 1 < LAYERS:
            ga_spread(l + 1)

        def redo(b, carry, l=l):
            pre = dot_nt(a3[l, b], w_up(l))
            rows = pl.ds(b * TB, TB)
            pre_s[rows, :] = pre
            hid_s[rows, :] = gelu(pre).astype(BF)
            return carry

        lax.fori_loop(0, C, redo, 0)
        ag_wait(p, dm)

        def feed_back(b, l=l):
            rows = pl.ds(b * TB, TB)
            slope = (dot_nt(dm[b], w_down(l)) * gelu_slope(pre_s[rows, :])).astype(BF)
            dpre_s[rows, :] = slope
            return dot_nn(slope, w_up(l))

        rs_loop(p, feed_back)
        if l + 1 < LAYERS:
            gm_mate(l + 1).wait_send()
            pl.semaphore_wait(credit, 1)
        gm_half(l, 1 - k)
        gm_mate(l).start()
        gm_half(l, k)
        d_a3 = rs_finish(p)
        ag_drain(p, dm)
        nhat, rstd = normalize(mid[l])
        add_norm(l, 4, d_a3, nhat)
        d_mid = g[...] + norm_back(nhat, rstd, d_a3, gain(l, 4))
        g[...] = d_mid
        nhat, rstd = normalize(br[l])
        ag_start(p + 1, db, norm_back(nhat, rstd, d_mid, gain(l, 2)).astype(BF))
        add_norm(l, 2, d_mid, nhat)
        gm_spread(l)
        if l > 0:
            pl.semaphore_signal(credit, inc=1, device_id=mate, device_id_type=MESH)
        ag_wait(p + 1, db)
        dk_s[...] = jnp.zeros_like(dk_s)
        dv_s[...] = jnp.zeros_like(dv_s)

        def attend_back(b, carry, l=l):
            d_att = dot_nn(db[b], w_proj(l)).astype(BF)

            def head_step(h, total):
                q, probs = head_probs(l, b, h)
                d_head = jnp.where(head_of == h, d_att, jnp.zeros((), BF))
                d_probs = dot_nt(d_head, vs_[l].reshape(T, FQ))
                delta = jnp.sum(probs * d_probs, axis=-1, keepdims=True)
                d_scores = (probs * (d_probs - delta)).astype(BF)
                d_q = dot_nn(d_scores, ks_[l].reshape(T, FQ))
                dk_s[...] += dot_tn(d_scores, q)
                dv_s[...] += dot_tn(probs.astype(BF), d_head)
                return jnp.where(head_of == h, d_q, total)

            d_query = lax.fori_loop(0, HPC, head_step, jnp.zeros((TB, FQ), F32))
            d_query = d_query * HEAD_DIM ** (-0.5)
            cosine, sine = tables(b)
            rows = pl.ds(b * TB, TB)
            dqkv[rows, 0:FQ] = (d_query * cosine - swapped(d_query) * sine).astype(BF)
            return carry

        lax.fori_loop(0, C, attend_back, 0)

        def qkv_back(b, l=l):
            rows = pl.ds(b * TB, TB)
            d_key = dk_s[rows, :] * HEAD_DIM ** (-0.5)
            cosine, sine = tables(b)
            dqkv[rows, FQ : 2 * FQ] = (d_key * cosine - swapped(d_key) * sine).astype(BF)
            dqkv[rows, 2 * FQ : 3 * FQ] = dv_s[rows, :].astype(BF)
            return dot_nt(dqkv[rows, :], w_qkv(l))

        rs_loop(p + 1, qkv_back)
        ga_all(l)
        ga_mate(l).start()
        d_a1 = rs_finish(p + 1)
        ag_drain(p + 1, db)
        nhat, rstd = normalize(st[l])
        add_norm(l, 0, d_a1, nhat)
        g[...] = g[...] + norm_back(nhat, rstd, d_a1, gain(l, 0))

    @pl.when(c != n)
    def _():
        perm[4].start()

    @pl.when(c == n)
    def _():
        out_g[...] = g[...]

    ga_spread(0)
    n_start(1, 0, ngrad[...])

    def gm_finish(l):
        total = gm_of(l)[k, n].astype(F32)
        for j in range(1, N):
            gm_z(l, j).wait()
            total = total + gmz[l, j - 1].astype(F32)
        stage[l] = total
        pltpu.make_async_copy(stage.at[l], out_mlp.at[l], loc.at[2 * LAYERS + l]).start()

    def xg(l, j):
        return remote(gax_s.at[l, j - 1], gax_r.at[l, j - 1], xg_s.at[l, j - 1], xg_r.at[l, j - 1], xy(j))

    def place(l, at, value):
        for part in range(3):
            cols = pl.ds(pl.multiple_of(part * D + at * FQ, LANES), FQ)
            out_qkv[l, :, cols] = value[:, part * FQ : (part + 1) * FQ]
        out_proj[l, :, pl.ds(pl.multiple_of(at * FQ, LANES), FQ)] = value[:, 3 * FQ : 4 * FQ]

    def ga_finish(l):
        for j in range(1, N):
            ga_z(l, j).wait()

        def total(at):
            value = ga_of(l)[at, k, n].astype(F32)
            for j in range(1, N):
                value = value + gaz[l, j - 1, at].astype(F32)
            return value

        for j in range(1, C):
            gax_s[l, j - 1] = total(chip(j)).astype(BF)
            xg(l, j).start()
        place(l, c, total(c))

    n_start(1, 1, n_finish(1, 0))
    gm_finish(1)
    ga_finish(1)
    n_start(1, 2, n_finish(1, 1))
    gm_finish(0)
    out_n[...] = n_finish(1, 2)
    ga_finish(0)
    for l in range(LAYERS):
        for j in range(1, C):
            xg(l, j).wait()
            place(l, cfrom(j), gax_r[l, j - 1].astype(F32))

    for l in range(LAYERS):
        pltpu.make_async_copy(stage.at[l], out_mlp.at[l], loc.at[2 * LAYERS + l]).wait()
        ga_mate(l).wait_send()
        for j in range(1, C):
            a2a(l, j).wait_send()
    gm_mate(0).wait_send()

    @pl.when(c != n)
    def _():
        for copy in perm[:3]:
            copy.wait_send()
        for copy in perm[3:]:
            copy.wait()


def body(mesh, hidden_in, w_qkv, w_proj, w_mlp, norm_params, grad_output, corpus_id, corpus_weight):
    W, N = mesh.shape["wide"], mesh.shape["narrow"]
    C = W // 2
    TB, D = hidden_in.shape
    FQ, UQ, RW, US = D // C, FF // C, D // (W * N), FF // (W * N)
    AW = 4 * FQ
    T = C * TB
    assert C == N and w_mlp.shape[1] == US and w_qkv.shape[1] == RW

    match = corpus_id[:, None] == jnp.arange(corpus_weight.shape[0], dtype=jnp.int32)[None, :]
    row_scale = jnp.sum(jnp.where(match, corpus_weight[None, :], 0.0), axis=1)
    scale = jnp.broadcast_to(row_scale[:, None], (TB, LANES))
    pieces = jnp.concatenate(
        [w_qkv.reshape(LAYERS, RW, 3, C, FQ), w_proj.reshape(LAYERS, RW, 1, C, FQ)], axis=2
    )
    wa = pieces.transpose(3, 0, 1, 2, 4).reshape(C, LAYERS, RW, AW)
    nrm = norm_params.transpose(0, 2, 1).reshape(LAYERS * 8, RW)
    half = HEAD_DIM // 2
    freqs = ROPE_BASE ** (-jnp.arange(half, dtype=F32) / half)
    angles = jnp.arange(T, dtype=F32)[:, None] * freqs[None, :]
    cosine = jnp.tile(jnp.cos(angles), (1, LANES // half))
    sine = jnp.sin(angles)
    sine = jnp.tile(jnp.concatenate([-sine, sine], axis=1), (1, LANES // HEAD_DIM))

    NR = LAYERS * 8
    dma = pltpu.SemaphoreType.DMA
    vm = pltpu.VMEM
    L = LAYERS
    scratch = [
        vm((L, C, 2, N, RW, AW), BF),
        vm((L, 2, N, US, 2 * D), BF),
        vm((L, C, TB, D), BF),
        vm((L, C, TB, D), BF),
        vm((C, TB, D), BF),
        vm((C, TB, D), BF),
        vm((L, C, TB, FQ), BF),
        vm((L, C, TB, FQ), BF),
        vm((L, C, TB, FQ), BF),
        vm((L, C, TB, FQ), BF),
        vm((L, TB, D), F32),
        vm((L, TB, D), F32),
        vm((L, TB, D), F32),
        vm((L, TB, D), F32),
        vm((T, UQ), F32),
        vm((T, UQ), BF),
        vm((T, UQ), BF),
        vm((8, LANES), BF),
        vm((8, LANES), F32),
        vm((T, FQ), F32),
        vm((T, FQ), F32),
        vm((T, 3 * FQ), BF),
        vm((C - 1, TB, D), BF),
        vm((C - 1, TB, D), BF),
        vm((TB, D), F32),
        vm((TB, D), BF),
        vm((TB, D), BF),
        vm((TB, LANES), F32),
        vm((TB, D), BF),
        vm((TB, D), F32),
        vm((2, N, US, 2 * D), BF),
        vm((N, US, 2 * D), BF),
        vm((L, N - 1, US, 2 * D), BF),
        vm((L, US, 2 * D), F32),
        vm((C, 2, N, RW, AW), BF),
        vm((L, C, N, RW, AW), BF),
        vm((L, N - 1, C, RW, AW), BF),
        vm((L, C - 1, RW, AW), BF),
        vm((L, C - 1, RW, AW), BF),
        vm((NR, D), F32),
        vm((NR, D), F32),
        vm((2, 3, NR, D), F32),
        vm((2, C - 1, NR, D), F32),
        vm((2, N - 1, NR, D), F32),
        vm((2, NR, D), F32),
        dma((5,)), dma((5,)),
        dma((3 * L,)),
        dma((L, C - 1)), dma((L, C - 1)),
        dma((4 * L, C - 1)), dma((4 * L, C - 1)),
        dma((4 * L, C - 1)), dma((4 * L, C - 1)),
        dma((2 * L, N - 1)), dma((2 * L, N - 1)),
        dma((2 * L,)), dma((2 * L,)),
        dma((2 * L, N - 1)), dma((2 * L, N - 1)),
        dma((2 * L,)), dma((2 * L,)),
        dma((L, C - 1)), dma((L, C - 1)),
        dma((2, C - 1)), dma((2, C - 1)),
        dma((2, N - 1)), dma((2, N - 1)),
        dma((2,)), dma((2,)),
        pltpu.SemaphoreType.REGULAR,
    ]
    vspec = pl.BlockSpec(memory_space=pltpu.VMEM)
    anyspec = pl.BlockSpec(memory_space=pl.ANY)
    outs = pl.pallas_call(
        partial(kernel_body, (C, N, TB, D, FQ, UQ, RW, US, AW)),
        out_shape=(
            jax.ShapeDtypeStruct((TB, D), BF),
            jax.ShapeDtypeStruct((TB, D), F32),
            jax.ShapeDtypeStruct((L, RW, 3 * D), F32),
            jax.ShapeDtypeStruct((L, RW, D), F32),
            jax.ShapeDtypeStruct((L, US, 2 * D), F32),
            jax.ShapeDtypeStruct((NR, D), F32),
        ),
        in_specs=[vspec] * 6 + [anyspec] * 2,
        out_specs=(vspec, vspec, vspec, vspec, anyspec, vspec),
        scratch_shapes=scratch,
        compiler_params=pltpu.CompilerParams(
            collective_id=0, has_side_effects=True, vmem_limit_bytes=63 << 20
        ),
    )(hidden_in, grad_output, scale, nrm, cosine, sine, wa, w_mlp)
    hidden_out, grad_in, grad_qkv, grad_proj, grad_mlp, norm_sum = outs
    index = lax.axis_index("wide") * N + lax.axis_index("narrow")
    own = lax.dynamic_slice_in_dim(norm_sum, index * RW, RW, 1)
    grad_norms = own.reshape(LAYERS, 8, RW).transpose(0, 2, 1)
    return hidden_out, grad_in, grad_qkv, grad_proj, grad_mlp, grad_norms


def solution(mesh):
    rows = P(("wide", "narrow"), None)
    layered = P(None, ("wide", "narrow"), None)
    return jax.shard_map(
        partial(body, mesh),
        mesh=mesh,
        in_specs=(rows, layered, layered, layered, layered, rows, P(("wide", "narrow")), P()),
        out_specs=(rows, rows, layered, layered, layered, layered),
        check_vma=False,
    )
```

```python
from functools import partial

import jax
import jax.numpy as jnp
import numpy as np
from jax import lax
from jax.experimental import pallas as pl
from jax.experimental.pallas import tpu as pltpu
from jax.sharding import PartitionSpec as P

HEADS = 16
HEAD_DIM = 64
FF = 4096
LAYERS = 2
EPS = 1e-05
MASKED = -1e30
ROPE_BASE = 10000.0
MESH = pl.DeviceIdType.MESH
BF = jnp.bfloat16
F32 = jnp.float32
LANES = 128
UNITS = 256


def dot_nn(left, right):
    return lax.dot_general(left, right, (((1,), (0,)), ((), ())), preferred_element_type=F32)


def dot_nt(left, right):
    return lax.dot_general(left, right, (((1,), (1,)), ((), ())), preferred_element_type=F32)


def dot_tn(left, right):
    return lax.dot_general(left, right, (((0,), (0,)), ((), ())), preferred_element_type=F32)


def normalize(inputs):
    centre = jnp.mean(inputs, axis=-1, keepdims=True)
    centered = inputs - centre
    rstd = lax.rsqrt(jnp.mean(centered * centered, axis=-1, keepdims=True) + EPS)
    return centered * rstd, rstd


def norm_back(nhat, rstd, grad, gain):
    scaled = grad * gain
    mean_f = jnp.mean(scaled, axis=-1, keepdims=True)
    mean_fn = jnp.mean(scaled * nhat, axis=-1, keepdims=True)
    return rstd * (scaled - mean_f - nhat * mean_fn)


GELU_S = 0.7978845608028654
GELU_A = 0.044715


def gelu(pre):
    return 0.5 * pre * (1.0 + jnp.tanh(GELU_S * (pre + GELU_A * pre * pre * pre)))


def gelu_slope(pre):
    square = pre * pre
    turned = jnp.tanh(GELU_S * (pre + GELU_A * pre * square))
    inner = GELU_S * (1.0 + 3.0 * GELU_A * square)
    return 0.5 * (1.0 + turned) + 0.5 * pre * (1.0 - turned * turned) * inner


def kernel_body(
    dims,
    hid_ref, gout_ref, ids_ref, cw_ref, nrm_ref, cos_ref, sin_ref, wq_ref, wp_ref, wm_ref,
    out_h, out_g, out_qkv, out_proj, out_mlp, out_n,
    wa, wm, a1, a3, dm, db, qs_, ks_, vs_, att, st, br, mid, mo,
    pre_s, hid_s, dpre_s, p_s, dk_s, dv_s, dqkv,
    rs_send, rs_recv, acc, hid_p, g_p, sc_own, sc_p, outh_s, g,
    gmb, gmr, gmz, stage, stage_a, gab, gar, gaz, gax_s, gax_r,
    npar, ngrad, nf_send, nf_recv, nb_send, nb_recv,
    perm_s, perm_r, loc, a2a_s, a2a_r, ag_s, ag_r, rs_s, rs_r,
    zw_s, zw_r, mw_s, mw_r, zg_s, zg_r, mga_s, mga_r, mgm_s, mgm_r, xg_s, xg_r,
    nx_s, nx_r, nz_s, nz_r, nm_s, nm_r, credit,
):
    C, N, TB, D, FQ, UQ, RW, US, AW = dims
    T = C * TB
    HPC = FQ // HEAD_DIM
    HALF = N * US
    REACH = N // 2
    w = lax.axis_index("wide")
    n = lax.axis_index("narrow")
    c = w // 2
    k = lax.rem(w, 2)
    mate = (2 * c + (1 - k), n)
    to_chip = n + k * (N - 1 - 2 * n)
    to_plane = c + k * (N - 1 - 2 * c)
    swap = (2 * to_chip + k, to_plane)
    moves = to_chip != c

    def block(at):
        return at + k * (C - 1 - 2 * at)

    mine = block(c)

    def flipped(base, j, count):
        out, bit = 0, 1
        while bit < count:
            ours = lax.rem(base // bit, 2)
            flip = (j // bit) % 2 if isinstance(j, int) else lax.rem(j // bit, 2)
            out = out + bit * (ours + flip - 2 * ours * flip)
            bit *= 2
        return out

    def chip(j):
        return flipped(c, j, C)

    def xy(j):
        return (2 * chip(j) + k, n)

    def zdev(at):
        return (w, at)

    def remote(src, dst, ssem, rsem, device):
        return pltpu.make_async_remote_copy(
            src_ref=src, dst_ref=dst, send_sem=ssem, recv_sem=rsem,
            device_id=device, device_id_type=MESH,
        )

    def local(src, dst, sem):
        return pltpu.make_async_copy(src, dst, sem)

    barrier = pltpu.get_barrier_semaphore()
    partners = [xy(j) for j in range(1, C)] + [mate]
    partners += [zdev(lax.rem(n + j, N)) for j in range(1, N)]
    for device in partners:
        pl.semaphore_signal(barrier, inc=1, device_id=device, device_id_type=MESH)

    @pl.when(moves)
    def _():
        pl.semaphore_signal(barrier, inc=1, device_id=swap, device_id_type=MESH)

    pl.semaphore_wait(barrier, len(partners) + jnp.where(moves, 1, 0))

    def perm(i):
        src, dst = (
            (hid_ref, hid_p), (gout_ref, g_p), (sc_own, sc_p), (outh_s, out_h), (g_p, hid_p)
        )[i]
        return src, dst, perm_s.at[i], perm_r.at[i]

    def perm_start(i):
        src, dst, ssem, rsem = perm(i)

        @pl.when(moves)
        def _():
            remote(src, dst, ssem, rsem, swap).start()

        @pl.when(jnp.logical_not(moves))
        def _():
            local(src, dst, rsem).start()

    def perm_wait(i):
        src, dst, ssem, rsem = perm(i)

        @pl.when(moves)
        def _():
            remote(src, dst, ssem, rsem, swap).wait_recv()

        @pl.when(jnp.logical_not(moves))
        def _():
            local(src, dst, rsem).wait()

    def perm_drain(i):
        src, dst, ssem, rsem = perm(i)

        @pl.when(moves)
        def _():
            remote(src, dst, ssem, rsem, swap).wait_send()

    perm_start(0)

    def n_copy(way, axis, j):
        send, heard = (nf_send, nf_recv) if way == 0 else (nb_send, nb_recv)
        slot = n_slot[axis]
        if axis == "x":
            return remote(send.at[slot], heard.at[slot, j - 1], nx_s.at[way, j - 1], nx_r.at[way, j - 1], xy(j))
        if axis == "z":
            there = zdev(lax.rem(n + j, N))
            return remote(send.at[slot], heard.at[slot, j - 1], nz_s.at[way, j - 1], nz_r.at[way, j - 1], there)
        return remote(send.at[slot], heard.at[slot, j - 1], nm_s.at[way], nm_r.at[way], mate)

    n_count = {"x": C, "z": N, "m": 2}
    n_slot = {"x": 0, "z": 1, "m": 2}

    def n_start(way, axis, value):
        send = nf_send if way == 0 else nb_send
        send[n_slot[axis]] = value.astype(send.dtype)
        for j in range(1, n_count[axis]):
            n_copy(way, axis, j).start()

    def n_finish(way, axis):
        send, heard = (nf_send, nf_recv) if way == 0 else (nb_send, nb_recv)
        total = send[n_slot[axis]].astype(F32)
        for j in range(1, n_count[axis]):
            n_copy(way, axis, j).wait()
            total = total + heard[n_slot[axis], j - 1].astype(F32)
        return total

    first = (w * N + n) * RW
    spot = lax.broadcasted_iota(jnp.int32, (RW, D), 1) == (
        lax.broadcasted_iota(jnp.int32, (RW, D), 0) + first
    )
    spot = spot.astype(F32)
    n_start(0, "x", jnp.concatenate(
        [dot_tn(nrm_ref[l], spot.astype(BF)) for l in range(LAYERS)], axis=0
    ))

    def pieces(l, at):
        for part in range(3):
            cols = pl.ds(pl.multiple_of(part * D + at * FQ, LANES), FQ)
            yield wq_ref.at[l, :, cols], wa.at[l, c, k, n, :, pl.ds(part * FQ, FQ)]
        cols = pl.ds(pl.multiple_of(at * FQ, LANES), FQ)
        yield wp_ref.at[l, :, cols], wa.at[l, c, k, n, :, pl.ds(3 * FQ, FQ)]

    def a2a_start(l):
        for j in range(1, C):
            for src, dst in pieces(l, chip(j)):
                remote(src, dst, a2a_s.at[l, j - 1], a2a_r.at[l, j - 1], xy(j)).start()

    def a2a_all(l, j):
        there = wa.at[l, chip(j), k, n]
        return remote(there, there, a2a_s.at[l, j - 1], a2a_r.at[l, j - 1], xy(j))

    def own_wa(l):
        mine = wa.at[l, c, k, n]
        return local(mine, mine, loc.at[l])

    def own_wm(l):
        return local(wm_ref.at[l], wm.at[l, k, n], loc.at[LAYERS + l])

    a2a_start(0)
    for l in range(LAYERS):
        for src, dst in pieces(l, c):
            local(src, dst, loc.at[l]).start()
        own_wm(l).start()

    def zslice(s, at):
        return wa.at[s // 2, :, k, at] if s % 2 == 0 else wm.at[s // 2, k, at]

    def mslice(s, core, at):
        return wa.at[s // 2, :, core, at] if s % 2 == 0 else wm.at[s // 2, core, at]

    def inside(at):
        return (at >= 0) & (at < N)

    def signed(least, most):
        return [sign * d for d in range(most, least - 1, -1) for sign in (1, -1)]

    def zw_copy(s, origin, at, slot):
        return remote(zslice(s, origin), zslice(s, origin), zw_s.at[s, slot], zw_r.at[s, origin], zdev(at))

    def direct_slot(d):
        return d + REACH

    def relay_slot(sign, q):
        return 2 * REACH + (q if sign > 0 else q + REACH - 1)

    def to_mate(s, at):
        return remote(mslice(s, k, at), mslice(s, k, at), mw_s.at[s, at], mw_r.at[s, at], mate)

    def w_send(s):
        for d in signed(1, REACH):
            @pl.when(inside(n + d))
            def _(d=d):
                zw_copy(s, n, n + d, direct_slot(d)).start()

        to_mate(s, n).start()

    def w_relay(s):
        for sign in (1, -1):
            origin = n - sign * REACH

            @pl.when(inside(origin) & inside(n + sign))
            def _(sign=sign, origin=origin):
                zw_copy(s, origin, n, 0).wait_recv()
                for q in range(1, REACH):
                    @pl.when(inside(n + sign * q))
                    def _(q=q):
                        zw_copy(s, origin, n + sign * q, relay_slot(sign, q)).start()

    def w_arrive(s):
        for d in reversed(signed(1, N - 1)):
            origin = n + d

            @pl.when(inside(origin))
            def _(d=d, origin=origin):
                if abs(d) == REACH:
                    sign = -1 if d > 0 else 1

                    @pl.when(jnp.logical_not(inside(n + sign)))
                    def _():
                        zw_copy(s, origin, n, 0).wait_recv()
                else:
                    zw_copy(s, origin, n, 0).wait_recv()
                to_mate(s, origin).start()

    def w_ready(s):
        for at in range(N):
            there = mslice(s, 1 - k, at)
            remote(there, there, mw_s.at[s, at], mw_r.at[s, at], mate).wait_recv()

    def w_drain(s):
        for d in signed(1, REACH):
            @pl.when(inside(n + d))
            def _(d=d):
                zw_copy(s, n, n + d, direct_slot(d)).wait_send()

        for sign in (1, -1):
            origin = n - sign * REACH
            for q in range(1, REACH):
                @pl.when(inside(origin) & inside(n + sign) & inside(n + sign * q))
                def _(sign=sign, origin=origin, q=q):
                    zw_copy(s, origin, n + sign * q, relay_slot(sign, q)).wait_send()

        for at in range(N):
            to_mate(s, at).wait_send()

    n_start(0, "z", n_finish(0, "x"))
    own_wa(0).wait()
    for j in range(1, C):
        a2a_all(0, j).wait_recv()
    w_send(0)
    n_start(0, "m", n_finish(0, "z"))
    npar[...] = n_finish(0, "m")
    ngrad[...] = jnp.zeros_like(ngrad)

    def gain(l, col):
        return npar[pl.ds(l * 8 + col, 1), :]

    SPLIT = C == 4
    hops = ((1, 0), (1, 1), (2, 1), (2, 0), (2, 0), (1, 1))

    def ag_copy(p, buf, source, slot):
        if not SPLIT:
            rows = buf.at[block(source)]
            return remote(rows, rows, ag_s.at[p, slot], ag_r.at[p, slot], xy(slot + 1))
        j, part = hops[slot]
        rows = buf.at[block(source), pl.ds(part * (TB // 2), TB // 2)]
        return remote(rows, rows, ag_s.at[p, slot], ag_r.at[p, slot], xy(j))

    def ag_start(p, buf, value):
        buf[mine] = value
        for slot in (0, 2, 1, 3) if SPLIT else range(C - 1):
            ag_copy(p, buf, c, slot).start()

    def ag_pass(p, buf):
        if SPLIT:
            ag_copy(p, buf, chip(1), 0).wait_recv()
            ag_copy(p, buf, chip(1), 4).start()
            ag_copy(p, buf, chip(2), 2).wait_recv()
            ag_copy(p, buf, chip(2), 5).start()

    def ag_wait(p, buf, j):
        for slot in ((), (1,), (3,), (4, 5))[j] if SPLIT else (j - 1,) * min(j, 1):
            ag_copy(p, buf, chip(j), slot).wait_recv()

    def ag_drain(p, buf):
        for slot in range(4) if SPLIT else range(C - 1):
            ag_copy(p, buf, c, slot).wait_send()
        if SPLIT:
            ag_copy(p, buf, chip(1), 4).wait_send()
            ag_copy(p, buf, chip(2), 5).wait_send()

    def rs_copy(p, j):
        return remote(rs_send.at[j - 1], rs_recv.at[j - 1], rs_s.at[p, j - 1], rs_r.at[p, j - 1], xy(j))

    def rs_put(p, j, value):
        @pl.when(j > 0)
        def _():
            rs_send[j - 1] = value.astype(BF)
            rs_copy(p, j).start()

        @pl.when(j == 0)
        def _():
            acc[...] = value

    def rs_block(p, b, value):
        rs_put(p, chip(block(b)), value)

    def rs_pair(p, i, value):
        rs_put(p, 2 * i, value[0:TB])
        rs_send[2 * i] = value[TB:].astype(BF)
        rs_copy(p, 2 * i + 1).start()

    def arrivals(p, buf, use):
        def step(i, carry):
            for at in range(C // 2):
                @pl.when(i == at)
                def _(at=at):
                    ag_wait(p, buf, 2 * at)
                    ag_wait(p, buf, 2 * at + 1)

            use(i, (block(chip(2 * i)), block(chip(2 * i + 1))))
            return carry

        lax.fori_loop(0, C // 2, step, 0)

    def both(ref, pair):
        return jnp.concatenate([ref[b] for b in pair], axis=0)

    def rs_finish(p):
        total = acc[...]
        for j in range(1, C):
            rs_copy(p, j).wait()
            total = total + rs_recv[j - 1].astype(F32)
        return total

    lane = lax.broadcasted_iota(jnp.int32, (TB, FQ), 1)
    low_half = lax.rem(lane, HEAD_DIM) < HEAD_DIM // 2
    head_of = lane // HEAD_DIM
    causal = lax.broadcasted_iota(jnp.int32, (HPC * TB, TB), 1) <= lax.rem(
        lax.broadcasted_iota(jnp.int32, (HPC * TB, TB), 0), TB
    )

    def tables(b):
        rows = pl.ds(b * TB, TB)
        reps = FQ // LANES
        return (
            jnp.concatenate([cos_ref[rows, :]] * reps, axis=1),
            jnp.concatenate([sin_ref[rows, :]] * reps, axis=1),
        )

    def swapped(u):
        half_dim = HEAD_DIM // 2
        return jnp.where(
            low_half, pltpu.roll(u, FQ - half_dim, 1), pltpu.roll(u, half_dim, 1)
        )

    def w_qkv(l):
        return wa[l, :, :, :, :, 0 : 3 * FQ].reshape(D, 3 * FQ)

    def w_proj(l):
        return wa[l, :, :, :, :, 3 * FQ : 4 * FQ].reshape(D, FQ)

    def w_up(l):
        return wm[l, :, :, :, 0:D].reshape(UQ, D)

    def w_down(l):
        return wm[l, :, :, :, D : 2 * D].reshape(UQ, D)

    def by_head(rows):
        return jnp.concatenate(
            [jnp.where(head_of == h, rows, jnp.zeros((), rows.dtype)) for h in range(HPC)], axis=0
        )

    def of_heads(stacked):
        out = stacked[0:TB]
        for h in range(1, HPC):
            out = jnp.where(head_of == h, stacked[h * TB : (h + 1) * TB], out)
        return out

    def exp_scores(l, b):
        scores = dot_nt(by_head(qs_[l, b]), ks_[l, 0 : b + 1].reshape((b + 1) * TB, FQ))
        last = jnp.where(causal, scores[:, b * TB :], MASKED)
        scores = jnp.concatenate([scores[:, : b * TB], last], axis=1) if b else last
        weights = jnp.exp(scores - jnp.max(scores, axis=-1, keepdims=True))
        return weights, 1.0 / jnp.sum(weights, axis=-1, keepdims=True)

    w_relay(0)
    own_wm(0).wait()
    w_send(1)
    perm_wait(0)
    st[0] = hid_p[...].astype(F32)
    for l in range(LAYERS):
        nhat, unused = normalize(st[l])
        ag_start(2 * l, a1.at[l], (nhat * gain(l, 0) + gain(l, 1)).astype(BF))
        if l == 0:
            a2a_start(1)
        ag_pass(2 * l, a1.at[l])
        w_arrive(2 * l)
        w_ready(2 * l)

        def qkv_step(i, pair, l=l):
            u = dot_nn(both(a1.at[l], pair), w_qkv(l))
            for e, b in enumerate(pair):
                cosine, sine = tables(b)
                uq = u[e * TB : (e + 1) * TB, 0:FQ]
                uk = u[e * TB : (e + 1) * TB, FQ : 2 * FQ]
                uq = (uq * cosine + swapped(uq) * sine).astype(BF)
                qs_[l, b] = (uq * HEAD_DIM ** (-0.5)).astype(BF)
                ks_[l, b] = (uk * cosine + swapped(uk) * sine).astype(BF)
                vs_[l, b] = u[e * TB : (e + 1) * TB, 2 * FQ :].astype(BF)

        arrivals(2 * l, a1.at[l], qkv_step)
        for b in range(C):
            weights, inverse = exp_scores(l, b)
            mixed = dot_nn(weights.astype(BF), vs_[l, 0 : b + 1].reshape((b + 1) * TB, FQ))
            low = of_heads(mixed * inverse).astype(BF)
            att[l, b] = low
            rs_block(2 * l, b, dot_nt(low, w_proj(l)))
        w_relay(2 * l + 1)
        if l + 1 < LAYERS:
            own_wa(l + 1).wait()
            for j in range(1, C):
                a2a_all(l + 1, j).wait_recv()
            w_send(2 * l + 2)
        branch = rs_finish(2 * l)
        ag_drain(2 * l, a1.at[l])
        br[l] = branch
        nhat, unused = normalize(branch)
        middle = st[l] + nhat * gain(l, 2) + gain(l, 3)
        mid[l] = middle
        nhat, unused = normalize(middle)
        ag_start(2 * l + 1, a3.at[l], (nhat * gain(l, 4) + gain(l, 5)).astype(BF))
        ag_pass(2 * l + 1, a3.at[l])
        w_arrive(2 * l + 1)
        w_ready(2 * l + 1)

        def feed(i, pair, l=l):
            hidden = gelu(dot_nt(both(a3.at[l], pair), w_up(l))).astype(BF)
            rs_pair(2 * l + 1, i, dot_nn(hidden, w_down(l)))

        arrivals(2 * l + 1, a3.at[l], feed)
        if l + 1 < LAYERS:
            w_relay(2 * l + 2)
            own_wm(l + 1).wait()
            w_send(2 * l + 3)
        else:
            perm_start(1)
            ids = jnp.broadcast_to(ids_ref[...], (TB, TB))
            scale = jnp.zeros((TB, TB), F32)
            for i in range(cw_ref.shape[1]):
                scale = jnp.where(ids == i, cw_ref[:, i : i + 1], scale)
            here = lax.broadcasted_iota(jnp.int32, (TB, TB), 0) == lax.broadcasted_iota(
                jnp.int32, (TB, TB), 1
            )
            column = jnp.sum(jnp.where(here, scale, 0.0), axis=1, keepdims=True)
            sc_own[...] = jnp.broadcast_to(column, (TB, LANES))
            perm_start(2)
        mlp_out = rs_finish(2 * l + 1)
        ag_drain(2 * l + 1, a3.at[l])
        mo[l] = mlp_out
        nhat, unused = normalize(mlp_out)
        new_state = mid[l] + nhat * gain(l, 6) + gain(l, 7)
        if l + 1 < LAYERS:
            st[l + 1] = new_state
        else:
            outh_s[...] = new_state.astype(BF)
            perm_wait(1)
            perm_wait(2)
            g[...] = g_p[...].astype(F32) * sc_p[:, 0:1]

    def add_norm(l, col, grad, nhat):
        ngrad[pl.ds(l * 8 + col, 1), :] = jnp.sum(grad * nhat, axis=0, keepdims=True)
        ngrad[pl.ds(l * 8 + col + 1, 1), :] = jnp.sum(grad, axis=0, keepdims=True)

    def gm_of(l):
        return gmb if l == LAYERS - 1 else wm.at[LAYERS - 1]

    def ga_of(l):
        return gab if l == LAYERS - 1 else wa.at[LAYERS - 1]

    def gm_all(l):
        dst = gm_of(l)
        per = UNITS // US
        count = HALF // UNITS

        def chunk(i, carry):
            core = jnp.where(i < count, 1 - k, k)
            at = lax.rem(i, count)
            off = pl.multiple_of(core * HALF + at * UNITS, LANES)
            up = dot_tn(dpre_s[:, pl.ds(off, UNITS)], a3[l].reshape(T, D))
            down = dot_tn(hid_s[:, pl.ds(off, UNITS)], dm[...].reshape(T, D))
            rows = pl.ds(at * per, per)
            dst[core, rows, :, 0:D] = up.astype(BF).reshape(per, US, D)
            dst[core, rows, :, D : 2 * D] = down.astype(BF).reshape(per, US, D)

            @pl.when(i < count)
            def _():
                for e in range(per):
                    gm_mate(l, at * per + e).start()

            return carry

        lax.fori_loop(0, 2 * count, chunk, 0)

    def gm_mate(l, at):
        return remote(gm_of(l).at[1 - k, at], gmr.at[at], mgm_s.at[l, at], mgm_r.at[l, at], mate)

    def ga_all(l):
        dst = ga_of(l)
        rows = 2 * N * RW

        def chunk(i, carry):
            off = pl.multiple_of(i * rows, LANES)
            grad_a = dot_tn(a1[l, :, :, pl.ds(off, rows)].reshape(T, rows), dqkv[...])
            grad_p = dot_tn(db[:, :, pl.ds(off, rows)].reshape(T, rows), att[l].reshape(T, FQ))
            dst[i, :, :, :, 0 : 3 * FQ] = grad_a.astype(BF).reshape(2, N, RW, 3 * FQ)
            dst[i, :, :, :, 3 * FQ : 4 * FQ] = grad_p.astype(BF).reshape(2, N, RW, FQ)
            return carry

        lax.fori_loop(0, C, chunk, 0)

    def ga_mate(l):
        return remote(ga_of(l).at[:, 1 - k], gar, mga_s.at[l], mga_r.at[l], mate)

    def zpart(s, at):
        return ga_of(s // 2).at[:, k, at] if s % 2 == 0 else gm_of(s // 2).at[k, at]

    def zbuf(s, slot):
        return gaz.at[s // 2, slot] if s % 2 == 0 else gmz.at[s // 2, slot]

    def zg_copy(s, owner, device, send, recv):
        return remote(zpart(s, owner), zbuf(s, recv), zg_s.at[s, send], zg_r.at[s, recv], zdev(device))

    def z_direct(s, d):
        return zg_copy(s, n + d, n + d, d + N - 1, (-d) % N - 1)

    def z_beyond(s, d):
        sign = 1 if d > 0 else -1
        return zg_copy(s, n + d, n + d - sign * REACH, d + N - 1, N - 1 + abs(d) - REACH - 1)

    def z_spread(s):
        for d in signed(REACH + 1, N - 1) + signed(1, REACH - 1):
            @pl.when(inside(n + d))
            def _(d=d):
                (z_beyond(s, d) if abs(d) > REACH else z_direct(s, d)).start()

    def z_relay(s):
        for sign in (1, -1):
            owner = n + sign * REACH

            @pl.when(inside(owner))
            def _(sign=sign, owner=owner):
                part = zpart(s, owner)
                for q in range(1, REACH):
                    @pl.when(inside(n - sign * q))
                    def _(q=q):
                        slot = N - 1 + q - 1
                        zg_copy(s, n, n, 0, slot).wait_recv()
                        part[...] = (part[...].astype(F32) + zbuf(s, slot)[...].astype(F32)).astype(BF)
                z_direct(s, sign * REACH).start()

    def z_arrive(s, add):
        for d in reversed(signed(1, REACH)):
            @pl.when(inside(n + d))
            def _(d=d):
                slot = d % N - 1
                zg_copy(s, n, n, 0, slot).wait_recv()
                add(zbuf(s, slot))

    def z_drain(s):
        for d in signed(1, N - 1):
            @pl.when(inside(n + d))
            def _(d=d):
                (z_beyond(s, d) if abs(d) > REACH else z_direct(s, d)).wait_send()

    def gm_spread(l):
        src = gm_of(l)
        s = 2 * l + 1

        def add(e, carry):
            at = flipped(n, N - 1 - e, N)
            gm_mate(l, at).wait_recv()
            src[k, at] = (src[k, at].astype(F32) + gmr[at].astype(F32)).astype(BF)
            dist = jnp.where(at > n, at - n, n - at)
            sign = jnp.where(at > n, 1, -1)
            far = dist > REACH
            device = jnp.where(far, at - sign * REACH, at)
            slot = jnp.where(far, N - 2 + dist - REACH, lax.rem(n - at + N, N) - 1)

            @pl.when((dist != 0) & (dist != REACH))
            def _():
                zg_copy(s, at, device, at - n + N - 1, slot).start()

            return carry

        lax.fori_loop(0, N, add, 0)

    def ga_spread(l):
        ga_mate(l).wait_recv()
        src = ga_of(l)
        src[:, k] = (src[:, k].astype(F32) + gar[...].astype(F32)).astype(BF)
        z_spread(2 * l)

    def gm_out(l):
        return local(stage, out_mlp.at[l], loc.at[2 * LAYERS + l])

    def gm_finish(l):
        stage[...] = gm_of(l)[k, n].astype(F32)

        def add(ref):
            stage[...] += ref[...].astype(F32)

        z_arrive(2 * l + 1, add)
        gm_out(l).start()

    def xg(l, j):
        return remote(gax_s.at[l, j - 1], gax_r.at[l, j - 1], xg_s.at[l, j - 1], xg_r.at[l, j - 1], xy(j))

    def place(l, at, value):
        for part in range(3):
            cols = pl.ds(pl.multiple_of(part * D + at * FQ, LANES), FQ)
            out_qkv[l, :, cols] = value[:, part * FQ : (part + 1) * FQ]
        out_proj[l, :, pl.ds(pl.multiple_of(at * FQ, LANES), FQ)] = value[:, 3 * FQ : 4 * FQ]

    def ga_finish(l):
        stage_a[...] = ga_of(l)[:, k, n].astype(F32)

        def add(ref):
            stage_a[...] += ref[...].astype(F32)

        z_arrive(2 * l, add)
        for j in range(1, C):
            gax_s[l, j - 1] = stage_a[chip(j)].astype(BF)
            xg(l, j).start()
        place(l, c, stage_a[c])

    def ga_place(l):
        for j in range(1, C):
            xg(l, j).wait()
            place(l, chip(j), gax_r[l, j - 1].astype(F32))

    for l in reversed(range(LAYERS)):
        p = 2 * LAYERS + 2 * (LAYERS - 1 - l)
        grad = g[...]
        nhat, rstd = normalize(mo[l])
        ag_start(p, dm, norm_back(nhat, rstd, grad, gain(l, 6)).astype(BF))
        add_norm(l, 6, grad, nhat)
        if l + 1 < LAYERS:
            z_relay(2 * l + 2)
        else:
            perm_start(3)
            for s in range(2 * LAYERS):
                w_drain(s)
            for i in range(3):
                perm_drain(i)

        ag_pass(p, dm)

        def redo(i, carry, l=l):
            pre = dot_nt(a3[l, pl.ds(2 * i, 2)].reshape(2 * TB, D), w_up(l))
            rows = pl.ds(i * 2 * TB, 2 * TB)
            pre_s[rows, :] = pre
            hid_s[rows, :] = gelu(pre).astype(BF)
            return carry

        lax.fori_loop(0, C // 2, redo, 0)

        def feed_back(i, pair, l=l, p=p):
            where = [pl.ds(b * TB, TB) for b in pair]
            pre = jnp.concatenate([pre_s[rows, :] for rows in where], axis=0)
            slope = (dot_nt(both(dm, pair), w_down(l)) * gelu_slope(pre)).astype(BF)
            for e, rows in enumerate(where):
                dpre_s[rows, :] = slope[e * TB : (e + 1) * TB]
            rs_pair(p, i, dot_nn(slope, w_up(l)))

        arrivals(p, dm, feed_back)
        if l + 1 < LAYERS:
            for at in range(N):
                gm_mate(l + 1, at).wait_send()
            pl.semaphore_wait(credit.at[1], 1)
        gm_all(l)
        gm_spread(l)
        if l > 0:
            pl.semaphore_signal(credit.at[1], inc=1, device_id=mate, device_id_type=MESH)
        d_a3 = rs_finish(p)
        ag_drain(p, dm)
        nhat, rstd = normalize(mid[l])
        add_norm(l, 4, d_a3, nhat)
        d_mid = g[...] + norm_back(nhat, rstd, d_a3, gain(l, 4))
        g[...] = d_mid
        nhat, rstd = normalize(br[l])
        ag_start(p + 1, db, norm_back(nhat, rstd, d_mid, gain(l, 2)).astype(BF))
        add_norm(l, 2, d_mid, nhat)
        for b in range(C):
            weights, inverse = exp_scores(l, b)
            cols = pl.ds(TB * (b * (b + 1) // 2), (b + 1) * TB)
            p_s[:, cols] = (weights * inverse).astype(BF)
        dk_s[...] = jnp.zeros_like(dk_s)
        dv_s[...] = jnp.zeros_like(dv_s)
        ag_pass(p + 1, db)
        if l + 1 < LAYERS:
            gm_finish(l + 1)
        for j in range(1, C):
            ag_wait(p + 1, db, j)
        for b in reversed(range(C)):
            size = (b + 1) * TB
            rows = pl.ds(b * TB, TB)
            seen = pl.ds(0, size)
            d_att = by_head(dot_nn(db[b], w_proj(l)).astype(BF))
            d_probs = dot_nt(d_att, vs_[l, 0 : b + 1].reshape(size, FQ))
            low = p_s[:, pl.ds(TB * (b * (b + 1) // 2), size)]
            probs = low.astype(F32)
            delta = jnp.sum(probs * d_probs, axis=-1, keepdims=True)
            d_scores = (probs * (d_probs - delta)).astype(BF)
            d_query = of_heads(dot_nn(d_scores, ks_[l, 0 : b + 1].reshape(size, FQ)))
            d_query = d_query * HEAD_DIM ** (-0.5)
            dk_s[seen, :] += dot_tn(d_scores, by_head(qs_[l, b]))
            dv_s[seen, :] += dot_tn(low, d_att)
            d_key = dk_s[rows, :]
            cosine, sine = tables(b)
            dqkv[rows, 0:FQ] = (d_query * cosine - swapped(d_query) * sine).astype(BF)
            dqkv[rows, FQ : 2 * FQ] = (d_key * cosine - swapped(d_key) * sine).astype(BF)
            dqkv[rows, 2 * FQ : 3 * FQ] = dv_s[rows, :].astype(BF)
            rs_block(p + 1, b, dot_nt(dqkv[rows, :], w_qkv(l)))
        z_relay(2 * l + 1)
        ga_all(l)
        if l + 1 < LAYERS:
            pl.semaphore_wait(credit.at[0], 1)
        ga_mate(l).start()
        if l + 1 < LAYERS:
            ga_finish(l + 1)
        ga_spread(l)
        if l > 0:
            pl.semaphore_signal(credit.at[0], inc=1, device_id=mate, device_id_type=MESH)
        d_a1 = rs_finish(p + 1)
        ag_drain(p + 1, db)
        nhat, rstd = normalize(st[l])
        add_norm(l, 0, d_a1, nhat)
        g[...] = g[...] + norm_back(nhat, rstd, d_a1, gain(l, 0))

    g_p[...] = g[...].astype(BF)
    perm_wait(3)
    perm_start(4)
    n_start(1, "m", ngrad[...])
    n_start(1, "x", n_finish(1, "m"))
    z_relay(0)
    n_start(1, "z", n_finish(1, "x"))
    ga_place(1)
    gm_out(1).wait()
    gm_finish(0)
    gm_out(0).wait()
    ga_finish(0)
    total = n_finish(1, "z")
    for l in range(LAYERS):
        out_n[l] = lax.dot_general(
            spot, total[l * 8 : (l + 1) * 8], (((1,), (1,)), ((), ())),
            preferred_element_type=F32, precision=lax.Precision.HIGHEST,
        )
    ga_place(0)

    for s in range(2 * LAYERS):
        z_drain(s)
    for l in range(LAYERS):
        ga_mate(l).wait_send()
        for j in range(1, C):
            a2a_all(l, j).wait_send()
    for at in range(N):
        gm_mate(0, at).wait_send()
    perm_wait(4)
    out_g[...] = hid_p[...].astype(F32)
    perm_drain(3)
    perm_drain(4)


def copy_out(*refs):
    count = (len(refs) - 1) // 3
    sems = refs[-1]
    into = [pltpu.make_async_copy(refs[i], refs[2 * count + i], sems.at[i]) for i in range(count)]
    out = [
        pltpu.make_async_copy(refs[2 * count + i], refs[count + i], sems.at[count + i])
        for i in range(count)
    ]
    for copy in into:
        copy.start()
    for i in range(count):
        into[i].wait()
        out[i].start()
    for copy in out:
        copy.wait()


def body(mesh, hidden_in, w_qkv, w_proj, w_mlp, norm_params, grad_output, corpus_id, corpus_weight):
    W, N = mesh.shape["wide"], mesh.shape["narrow"]
    C = W // 2
    TB, D = hidden_in.shape
    FQ, UQ, RW, US = D // C, FF // C, D // (W * N), FF // (W * N)
    AW = 4 * FQ
    T = C * TB
    REACH = N // 2
    assert C == N and w_mlp.shape[1] == US and w_qkv.shape[1] == RW

    half = HEAD_DIM // 2
    freqs = np.float32(ROPE_BASE) ** (-np.arange(half, dtype=np.float32) / np.float32(half))
    angles = (np.arange(T, dtype=np.float32)[:, None] * freqs[None, :]).astype(np.float32)
    cosine = np.tile(np.cos(angles), (1, LANES // half)).astype(np.float32)
    sine = np.sin(angles)
    sine = np.tile(np.concatenate([-sine, sine], axis=1), (1, LANES // HEAD_DIM)).astype(np.float32)

    NR = LAYERS * 8
    dma = pltpu.SemaphoreType.DMA
    vm = pltpu.VMEM
    L = LAYERS
    scratch = [
        vm((L, C, 2, N, RW, AW), BF),
        vm((L, 2, N, US, 2 * D), BF),
        vm((L, C, TB, D), BF),
        vm((L, C, TB, D), BF),
        vm((C, TB, D), BF),
        vm((C, TB, D), BF),
        vm((L, C, TB, FQ), BF),
        vm((L, C, TB, FQ), BF),
        vm((L, C, TB, FQ), BF),
        vm((L, C, TB, FQ), BF),
        vm((L, TB, D), F32),
        vm((L, TB, D), F32),
        vm((L, TB, D), F32),
        vm((L, TB, D), F32),
        vm((T, UQ), F32),
        vm((T, UQ), BF),
        vm((T, UQ), BF),
        vm((FQ // HEAD_DIM * TB, TB * C * (C + 1) // 2), BF),
        vm((T, FQ), F32),
        vm((T, FQ), F32),
        vm((T, 3 * FQ), BF),
        vm((C - 1, TB, D), BF),
        vm((C - 1, TB, D), BF),
        vm((TB, D), F32),
        vm((TB, D), BF),
        vm((TB, D), BF),
        vm((TB, LANES), F32),
        vm((TB, LANES), F32),
        vm((TB, D), BF),
        vm((TB, D), F32),
        vm((2, N, US, 2 * D), BF),
        vm((N, US, 2 * D), BF),
        vm((L, N + REACH - 2, US, 2 * D), BF),
        vm((US, 2 * D), F32),
        vm((C, RW, AW), F32),
        vm((C, 2, N, RW, AW), BF),
        vm((C, N, RW, AW), BF),
        vm((L, N + REACH - 2, C, RW, AW), BF),
        vm((L, C - 1, RW, AW), BF),
        vm((L, C - 1, RW, AW), BF),
        vm((NR, D), F32),
        vm((NR, D), F32),
        vm((3, NR, D), BF),
        vm((3, C - 1, NR, D), BF),
        vm((3, NR, D), F32),
        vm((3, C - 1, NR, D), F32),
        dma((5,)), dma((5,)),
        dma((3 * L,)),
        dma((L, C - 1)), dma((L, C - 1)),
        dma((4 * L, max(C - 1, 6))), dma((4 * L, max(C - 1, 6))),
        dma((4 * L, C - 1)), dma((4 * L, C - 1)),
        dma((2 * L, 4 * REACH)), dma((2 * L, N)),
        dma((2 * L, N)), dma((2 * L, N)),
        dma((2 * L, 2 * N - 1)), dma((2 * L, N + REACH - 2)),
        dma((L,)), dma((L,)),
        dma((L, N)), dma((L, N)),
        dma((L, C - 1)), dma((L, C - 1)),
        dma((2, C - 1)), dma((2, C - 1)),
        dma((2, N - 1)), dma((2, N - 1)),
        dma((2,)), dma((2,)),
        pltpu.SemaphoreType.REGULAR((2,)),
    ]
    vspec = pl.BlockSpec(memory_space=pltpu.VMEM)
    anyspec = pl.BlockSpec(memory_space=pl.ANY)
    shapes = (
        jax.ShapeDtypeStruct((TB, D), BF),
        jax.ShapeDtypeStruct((TB, D), F32),
        jax.ShapeDtypeStruct((L, RW, 3 * D), F32),
        jax.ShapeDtypeStruct((L, RW, D), F32),
        jax.ShapeDtypeStruct((L, US, 2 * D), F32),
        jax.ShapeDtypeStruct((L, RW, 8), F32),
    )
    outs = pl.pallas_call(
        partial(kernel_body, (C, N, TB, D, FQ, UQ, RW, US, AW)),
        out_shape=shapes,
        in_specs=[anyspec] * 2 + [vspec] * 5 + [anyspec] * 3,
        out_specs=(anyspec, vspec, vspec, vspec, anyspec, vspec),
        scratch_shapes=scratch,
        compiler_params=pltpu.CompilerParams(
            collective_id=0, has_side_effects=True, vmem_limit_bytes=63 << 20
        ),
    )(
        hidden_in, grad_output, corpus_id.reshape(1, TB), corpus_weight.reshape(1, -1), norm_params,
        jnp.asarray(cosine), jnp.asarray(sine), w_qkv, w_proj, w_mlp,
    )
    return tuple(
        pl.pallas_call(
            copy_out,
            out_shape=shapes,
            in_specs=[anyspec] * len(shapes),
            out_specs=(anyspec,) * len(shapes),
            scratch_shapes=[vm(one.shape, one.dtype) for one in shapes] + [dma((2 * len(shapes),))],
            compiler_params=pltpu.CompilerParams(vmem_limit_bytes=60 << 20),
        )(*outs)
    )


def solution(mesh):
    rows = P(("wide", "narrow"), None)
    layered = P(None, ("wide", "narrow"), None)
    return jax.shard_map(
        partial(body, mesh),
        mesh=mesh,
        in_specs=(rows, layered, layered, layered, layered, rows, P(("wide", "narrow")), P()),
        out_specs=(rows, rows, layered, layered, layered, layered),
        check_vma=False,
    )
```

```python
from functools import partial

import jax
import jax.numpy as jnp
import numpy as np
from jax import lax
from jax.experimental import pallas as pl
from jax.experimental.pallas import tpu as pltpu
from jax.sharding import PartitionSpec as P

HEADS = 16
HEAD_DIM = 64
FF = 4096
LAYERS = 2
EPS = 1e-05
MASKED = -1e30
ROPE_BASE = 10000.0
MESH = pl.DeviceIdType.MESH
BF = jnp.bfloat16
F32 = jnp.float32
LANES = 128
UNITS = 256


def dot_nn(left, right):
    return lax.dot_general(left, right, (((1,), (0,)), ((), ())), preferred_element_type=F32)


def dot_nt(left, right):
    return lax.dot_general(left, right, (((1,), (1,)), ((), ())), preferred_element_type=F32)


def dot_tn(left, right):
    return lax.dot_general(left, right, (((0,), (0,)), ((), ())), preferred_element_type=F32)


def normalize(inputs):
    centre = jnp.mean(inputs, axis=-1, keepdims=True)
    centered = inputs - centre
    rstd = lax.rsqrt(jnp.mean(centered * centered, axis=-1, keepdims=True) + EPS)
    return centered * rstd, rstd


def norm_back(nhat, rstd, grad, gain):
    scaled = grad * gain
    mean_f = jnp.mean(scaled, axis=-1, keepdims=True)
    mean_fn = jnp.mean(scaled * nhat, axis=-1, keepdims=True)
    return rstd * (scaled - mean_f - nhat * mean_fn)


GELU_S = 0.7978845608028654
GELU_A = 0.044715


def gelu(pre):
    return 0.5 * pre * (1.0 + jnp.tanh(GELU_S * (pre + GELU_A * pre * pre * pre)))


def gelu_slope(pre):
    square = pre * pre
    turned = jnp.tanh(GELU_S * (pre + GELU_A * pre * square))
    inner = GELU_S * (1.0 + 3.0 * GELU_A * square)
    return 0.5 * (1.0 + turned) + 0.5 * pre * (1.0 - turned * turned) * inner


def kernel_body(
    dims,
    hid_ref, gout_ref, ids_ref, cw_ref, nrm_ref, cos_in, sin_in, wq_ref, wp_ref, wm_ref,
    out_h, out_g, out_qkv, out_proj, out_mlp, out_n,
    cos_ref, sin_ref, held_qkv, held_proj,
    wa, wm, a1, a3, dm, db, qs_, ks_, vs_, att, st, br, mid, mo,
    pre_s, hid_s, dpre_s, p_s, dk_s, dv_s, dqkv,
    rs_send, rs_recv, rs_mid, acc, hid_p, g_p, sc_own, sc_p, outh_s, g,
    gmr, gmz, stage, stage_a, gar, gaz, gax_s, gax_r,
    npar, ngrad, nf_send, nf_recv, nb_send, nb_recv,
    perm_s, perm_r, loc, a2a_s, a2a_r, ag_s, ag_r, rs_s, rs_r,
    zw_s, zw_r, mw_s, mw_r, zg_s, zg_r, mga_s, mga_r, mgm_s, mgm_r, xg_s, xg_r,
    nx_s, nx_r, nz_s, nz_r, nm_s, nm_r, fin, credit,
):
    C, N, TB, D, FQ, UQ, RW, US, AW = dims
    T = C * TB
    HPC = FQ // HEAD_DIM
    HALF = N * US
    REACH = N // 2
    w = lax.axis_index("wide")
    n = lax.axis_index("narrow")
    c = w // 2
    k = lax.rem(w, 2)
    mate = (2 * c + (1 - k), n)
    to_chip = n + k * (N - 1 - 2 * n)
    to_plane = c + k * (N - 1 - 2 * c)
    swap = (2 * to_chip + k, to_plane)
    moves = to_chip != c

    def block(at):
        return at + k * (C - 1 - 2 * at)

    mine = block(c)

    def flipped(base, j, count):
        out, bit = 0, 1
        while bit < count:
            ours = lax.rem(base // bit, 2)
            flip = (j // bit) % 2 if isinstance(j, int) else lax.rem(j // bit, 2)
            out = out + bit * (ours + flip - 2 * ours * flip)
            bit *= 2
        return out

    def chip(j):
        return flipped(c, j, C)

    def xy(j):
        return (2 * chip(j) + k, n)

    def zdev(at):
        return (w, at)

    def remote(src, dst, ssem, rsem, device):
        return pltpu.make_async_remote_copy(
            src_ref=src, dst_ref=dst, send_sem=ssem, recv_sem=rsem,
            device_id=device, device_id_type=MESH,
        )

    def local(src, dst, sem):
        return pltpu.make_async_copy(src, dst, sem)

    barrier = pltpu.get_barrier_semaphore()
    partners = [xy(j) for j in range(1, C)] + [mate]
    partners += [zdev(lax.rem(n + j, N)) for j in range(1, N)]
    for device in partners:
        pl.semaphore_signal(barrier, inc=1, device_id=device, device_id_type=MESH)

    @pl.when(moves)
    def _():
        pl.semaphore_signal(barrier, inc=1, device_id=swap, device_id_type=MESH)

    pl.semaphore_wait(barrier, len(partners) + jnp.where(moves, 1, 0))

    rope = (
        local(cos_in, cos_ref, fin.at[2 * LAYERS + 1]), local(sin_in, sin_ref, fin.at[2 * LAYERS + 2])
    )
    for copy in rope:
        copy.start()

    def perm(i):
        src, dst = (
            (hid_ref, hid_p), (gout_ref, g_p), (sc_own, sc_p), (outh_s, out_h), (g_p, hid_p)
        )[i]
        return src, dst, perm_s.at[i], perm_r.at[i]

    def perm_start(i):
        src, dst, ssem, rsem = perm(i)

        @pl.when(moves)
        def _():
            remote(src, dst, ssem, rsem, swap).start()

        @pl.when(jnp.logical_not(moves))
        def _():
            local(src, dst, rsem).start()

    def perm_wait(i):
        src, dst, ssem, rsem = perm(i)

        @pl.when(moves)
        def _():
            remote(src, dst, ssem, rsem, swap).wait_recv()

        @pl.when(jnp.logical_not(moves))
        def _():
            local(src, dst, rsem).wait()

    def perm_drain(i):
        src, dst, ssem, rsem = perm(i)

        @pl.when(moves)
        def _():
            remote(src, dst, ssem, rsem, swap).wait_send()

    perm_start(0)

    def n_copy(way, axis, j):
        send, heard = (nf_send, nf_recv) if way == 0 else (nb_send, nb_recv)
        slot = n_slot[axis]
        if axis == "x":
            return remote(send.at[slot], heard.at[slot, j - 1], nx_s.at[way, j - 1], nx_r.at[way, j - 1], xy(j))
        if axis == "z":
            there = zdev(lax.rem(n + j, N))
            return remote(send.at[slot], heard.at[slot, j - 1], nz_s.at[way, j - 1], nz_r.at[way, j - 1], there)
        return remote(send.at[slot], heard.at[slot, j - 1], nm_s.at[way], nm_r.at[way], mate)

    n_count = {"x": C, "z": N, "m": 2}
    n_slot = {"x": 0, "z": 1, "m": 2}

    def n_start(way, axis, value):
        send = nf_send if way == 0 else nb_send
        send[n_slot[axis]] = value.astype(send.dtype)
        for j in range(1, n_count[axis]):
            n_copy(way, axis, j).start()

    def n_finish(way, axis):
        send, heard = (nf_send, nf_recv) if way == 0 else (nb_send, nb_recv)
        total = send[n_slot[axis]].astype(F32)
        for j in range(1, n_count[axis]):
            n_copy(way, axis, j).wait()
            total = total + heard[n_slot[axis], j - 1].astype(F32)
        return total

    first = (w * N + n) * RW
    spot = lax.broadcasted_iota(jnp.int32, (RW, D), 1) == (
        lax.broadcasted_iota(jnp.int32, (RW, D), 0) + first
    )
    spot = spot.astype(F32)
    n_start(0, "x", jnp.concatenate(
        [dot_nn(nrm_ref[l], spot.astype(BF)) for l in range(LAYERS)], axis=0
    ))

    def pieces(l, at):
        for part in range(3):
            cols = pl.ds(pl.multiple_of(part * D + at * FQ, LANES), FQ)
            yield wq_ref.at[l, :, cols], wa.at[l, c, k, n, :, pl.ds(part * FQ, FQ)]
        cols = pl.ds(pl.multiple_of(at * FQ, LANES), FQ)
        yield wp_ref.at[l, :, cols], wa.at[l, c, k, n, :, pl.ds(3 * FQ, FQ)]

    def a2a_start(l):
        for j in range(1, C):
            for src, dst in pieces(l, chip(j)):
                remote(src, dst, a2a_s.at[l, j - 1], a2a_r.at[l, j - 1], xy(j)).start()

    def a2a_all(l, j):
        there = wa.at[l, chip(j), k, n]
        return remote(there, there, a2a_s.at[l, j - 1], a2a_r.at[l, j - 1], xy(j))

    def own_wa(l):
        mine = wa.at[l, c, k, n]
        return local(mine, mine, loc.at[l])

    def own_wm(l):
        return local(wm_ref.at[l], wm.at[l, k, n], loc.at[LAYERS + l])

    a2a_start(0)
    for l in range(LAYERS):
        for src, dst in pieces(l, c):
            local(src, dst, loc.at[l]).start()
        own_wm(l).start()

    def shard(kind, l, core, at):
        return wm.at[l, core, at] if kind else wa.at[l, :, core, at]

    def inside(at):
        return (at >= 0) & (at < N)

    def signed(least, most):
        return [sign * d for d in range(most, least - 1, -1) for sign in (1, -1)]

    def zw_copy(kind, l, origin, at, slot):
        rows = shard(kind, l, k, origin)
        return remote(rows, rows, zw_s.at[2 * l + kind, slot], zw_r.at[2 * l + kind, origin], zdev(at))

    def direct_slot(d):
        return d + REACH

    def relay_slot(sign, q):
        return 2 * REACH + (q if sign > 0 else q + REACH - 1)

    def to_mate(kind, l, at, core=k):
        rows = shard(kind, l, core, at)
        return remote(rows, rows, mw_s.at[2 * l + kind, at], mw_r.at[2 * l + kind, at], mate)

    def w_send(kind, l):
        for d in signed(1, REACH):
            @pl.when(inside(n + d))
            def _(d=d):
                zw_copy(kind, l, n, n + d, direct_slot(d)).start()

        to_mate(kind, l, n).start()

    def w_relay(kind, l):
        for sign in (1, -1):
            origin = n - sign * REACH

            @pl.when(inside(origin) & inside(n + sign))
            def _(sign=sign, origin=origin):
                zw_copy(kind, l, origin, n, 0).wait_recv()
                for q in range(1, REACH):
                    @pl.when(inside(n + sign * q))
                    def _(q=q):
                        zw_copy(kind, l, origin, n + sign * q, relay_slot(sign, q)).start()

    def w_arrive(kind, l):
        for d in reversed(signed(1, N - 1)):
            origin = n + d

            @pl.when(inside(origin))
            def _(d=d, origin=origin):
                if abs(d) == REACH:
                    sign = -1 if d > 0 else 1

                    @pl.when(jnp.logical_not(inside(n + sign)))
                    def _():
                        zw_copy(kind, l, origin, n, 0).wait_recv()
                else:
                    zw_copy(kind, l, origin, n, 0).wait_recv()
                to_mate(kind, l, origin).start()

    def w_ready(kind, l):
        for at in range(N):
            to_mate(kind, l, at, 1 - k).wait_recv()

    def w_drain(kind, l):
        for d in signed(1, REACH):
            @pl.when(inside(n + d))
            def _(d=d):
                zw_copy(kind, l, n, n + d, direct_slot(d)).wait_send()

        for sign in (1, -1):
            origin = n - sign * REACH
            for q in range(1, REACH):
                @pl.when(inside(origin) & inside(n + sign) & inside(n + sign * q))
                def _(sign=sign, origin=origin, q=q):
                    zw_copy(kind, l, origin, n + sign * q, relay_slot(sign, q)).wait_send()

        for at in range(N):
            to_mate(kind, l, at).wait_send()

    n_start(0, "z", n_finish(0, "x"))
    own_wa(0).wait()
    for j in range(1, C):
        a2a_all(0, j).wait_recv()
    w_send(0, 0)
    n_start(0, "m", n_finish(0, "z"))
    npar[...] = n_finish(0, "m")
    ngrad[...] = jnp.zeros_like(ngrad)

    def gain(l, col):
        return npar[pl.ds(l * 8 + col, 1), :]

    SPLIT = C == 4
    hops = ((1, 0), (1, 1), (2, 1), (2, 0), (2, 0), (1, 1))

    def ag_copy(p, buf, source, slot):
        if not SPLIT:
            rows = buf.at[block(source)]
            return remote(rows, rows, ag_s.at[lax.rem(p, 2), slot], ag_r.at[lax.rem(p, 2), slot], xy(slot + 1))
        j, part = hops[slot]
        rows = buf.at[block(source), pl.ds(part * (TB // 2), TB // 2)]
        return remote(rows, rows, ag_s.at[lax.rem(p, 2), slot], ag_r.at[lax.rem(p, 2), slot], xy(j))

    def ag_start(p, buf, value):
        buf[mine] = value
        for slot in (0, 2, 1, 3) if SPLIT else range(C - 1):
            ag_copy(p, buf, c, slot).start()

    def ag_pass(p, buf):
        if SPLIT:
            ag_copy(p, buf, chip(1), 0).wait_recv()
            ag_copy(p, buf, chip(1), 4).start()
            ag_copy(p, buf, chip(2), 2).wait_recv()
            ag_copy(p, buf, chip(2), 5).start()

    def ag_wait(p, buf, j):
        for slot in ((), (1,), (3,), (4, 5))[j] if SPLIT else (j - 1,) * min(j, 1):
            ag_copy(p, buf, chip(j), slot).wait_recv()

    def ag_drain(p, buf):
        for slot in range(4) if SPLIT else range(C - 1):
            ag_copy(p, buf, c, slot).wait_send()
        if SPLIT:
            ag_copy(p, buf, chip(1), 4).wait_send()
            ag_copy(p, buf, chip(2), 5).wait_send()

    def rs_copy(p, j):
        return remote(rs_send.at[j - 1], rs_recv.at[j - 1], rs_s.at[lax.rem(p, 2), j - 1], rs_r.at[lax.rem(p, 2), j - 1], xy(j))

    def rs_put(p, j, value):
        @pl.when(j > 0)
        def _():
            rs_send[j - 1] = value.astype(BF)
            rs_copy(p, j).start()

        @pl.when(j == 0)
        def _():
            acc[...] = value

    def rs_block(p, b, value):
        rs_put(p, chip(block(b)), value)

    def rs_pair(p, i, value):
        rs_put(p, 2 * i, value[0:TB])
        rs_send[2 * i] = value[TB:].astype(BF)
        rs_copy(p, 2 * i + 1).start()

    def half_copy(p, slot):
        part = pl.ds((0, 1, 1, 0, 0, 1)[slot] * (TB // 2), TB // 2)
        src = rs_send.at[(0, 0, 1, 1, 2, 2)[slot], part]
        dst = rs_mid.at[slot - 4] if slot >= 4 else rs_recv.at[(0, 0, 1, 1)[slot], part]
        return remote(src, dst, rs_s.at[lax.rem(p, 2), slot], rs_r.at[lax.rem(p, 2), slot], xy((1, 1, 2, 2, 1, 2)[slot]))

    def rs_halves(p, buf, part):
        for j in range(1, C):
            ag_wait(p, buf, j)

        def step(i, carry):
            value = part((block(chip(3 - i)), block(chip(1 - i))))

            @pl.when(i == 0)
            def _():
                rs_send[2] = value[0:TB].astype(BF)
                half_copy(p, 4).start()
                half_copy(p, 5).start()
                rs_send[0] = value[TB:].astype(BF)
                half_copy(p, 0).start()

            @pl.when(i == 1)
            def _():
                rs_send[1] = value[0:TB].astype(BF)
                half_copy(p, 2).start()
                acc[...] = value[TB:]

            return carry

        lax.fori_loop(0, 2, step, 0)

        @pl.when(p == 2 * LAYERS - 1)
        def _():
            perm_start(1)
            perm_start(2)

        for slot, at, rows, onward in ((4, 1, pl.ds(0, TB // 2), 3), (5, 0, pl.ds(TB // 2, TB // 2), 1)):
            half_copy(p, slot).wait_recv()
            rs_send[at, rows] = (rs_send[at, rows].astype(F32) + rs_mid[slot - 4].astype(F32)).astype(BF)
            half_copy(p, onward).start()

    def rs_halves_finish(p):
        for slot in range(4):
            half_copy(p, slot).wait()
        half_copy(p, 4).wait_send()
        half_copy(p, 5).wait_send()
        return acc[...] + rs_recv[0].astype(F32) + rs_recv[1].astype(F32)

    def arrivals(p, buf, use):
        def step(i, carry):
            for at in range(C // 2):
                @pl.when(i == at)
                def _(at=at):
                    ag_wait(p, buf, 2 * at)
                    ag_wait(p, buf, 2 * at + 1)

            use(i, (block(chip(2 * i)), block(chip(2 * i + 1))))
            return carry

        lax.fori_loop(0, C // 2, step, 0)

    def both(ref, pair):
        return jnp.concatenate([ref[b] for b in pair], axis=0)

    def rs_finish(p):
        total = acc[...]
        for j in range(1, C):
            rs_copy(p, j).wait()
            total = total + rs_recv[j - 1].astype(F32)
        return total

    lane = lax.broadcasted_iota(jnp.int32, (TB, FQ), 1)
    low_half = lax.rem(lane, HEAD_DIM) < HEAD_DIM // 2
    head_of = lane // HEAD_DIM
    causal = lax.broadcasted_iota(jnp.int32, (HPC * TB, TB), 1) <= lax.rem(
        lax.broadcasted_iota(jnp.int32, (HPC * TB, TB), 0), TB
    )

    def tables(b):
        rows = pl.ds(b * TB, TB)
        reps = FQ // LANES
        return (
            jnp.concatenate([cos_ref[rows, :]] * reps, axis=1),
            jnp.concatenate([sin_ref[rows, :]] * reps, axis=1),
        )

    def swapped(u):
        half_dim = HEAD_DIM // 2
        return jnp.where(
            low_half, pltpu.roll(u, FQ - half_dim, 1), pltpu.roll(u, half_dim, 1)
        )

    def w_qkv(l):
        return wa[l, :, :, :, :, 0 : 3 * FQ].reshape(D, 3 * FQ)

    def w_proj(l):
        return wa[l, :, :, :, :, 3 * FQ : 4 * FQ].reshape(D, FQ)

    def w_up(l):
        return wm[l, :, :, :, 0:D].reshape(UQ, D)

    def w_down(l):
        return wm[l, :, :, :, D : 2 * D].reshape(UQ, D)

    def by_head(rows):
        return jnp.concatenate(
            [jnp.where(head_of == h, rows, jnp.zeros((), rows.dtype)) for h in range(HPC)], axis=0
        )

    def of_heads(stacked):
        out = stacked[0:TB]
        for h in range(1, HPC):
            out = jnp.where(head_of == h, stacked[h * TB : (h + 1) * TB], out)
        return out

    def exp_scores(l, b):
        scores = dot_nt(by_head(qs_[l, b]), ks_[l, 0 : b + 1].reshape((b + 1) * TB, FQ))
        last = jnp.where(causal, scores[:, b * TB :], MASKED)
        scores = jnp.concatenate([scores[:, : b * TB], last], axis=1) if b else last
        weights = jnp.exp(scores - jnp.max(scores, axis=-1, keepdims=True))
        return weights, 1.0 / jnp.sum(weights, axis=-1, keepdims=True)

    w_relay(0, 0)
    own_wm(0).wait()
    w_send(1, 0)
    perm_wait(0)
    st[0] = hid_p[...].astype(F32)
    ids = jnp.broadcast_to(ids_ref[...], (8, TB))
    scale = jnp.zeros((8, TB), F32)
    for i in range(cw_ref.shape[1]):
        scale = jnp.where(ids == i, cw_ref[:, i : i + 1], scale)
    sc_own[...] = scale
    for copy in rope:
        copy.wait()

    def forward(l, carry):
        p = 2 * l
        more = l + 1 < LAYERS
        nhat, unused = normalize(st[l])
        ag_start(p, a1.at[l], (nhat * gain(l, 0) + gain(l, 1)).astype(BF))

        @pl.when(l == 0)
        def _():
            a2a_start(1)

        ag_pass(p, a1.at[l])
        w_arrive(0, l)
        w_ready(0, l)

        def qkv_step(i, pair):
            u = dot_nn(both(a1.at[l], pair), w_qkv(l))
            for e, b in enumerate(pair):
                cosine, sine = tables(b)
                uq = u[e * TB : (e + 1) * TB, 0:FQ]
                uk = u[e * TB : (e + 1) * TB, FQ : 2 * FQ]
                uq = (uq * cosine + swapped(uq) * sine).astype(BF)
                qs_[l, b] = (uq * HEAD_DIM ** (-0.5)).astype(BF)
                ks_[l, b] = (uk * cosine + swapped(uk) * sine).astype(BF)
                vs_[l, b] = u[e * TB : (e + 1) * TB, 2 * FQ :].astype(BF)

        arrivals(p, a1.at[l], qkv_step)
        for b in range(C):
            weights, inverse = exp_scores(l, b)
            mixed = dot_nn(weights.astype(BF), vs_[l, 0 : b + 1].reshape((b + 1) * TB, FQ))
            low = of_heads(mixed * inverse).astype(BF)
            att[l, b] = low
            rs_block(p, b, dot_nt(low, w_proj(l)))
        w_relay(1, l)

        @pl.when(more)
        def _():
            own_wa(l + 1).wait()
            for j in range(1, C):
                a2a_all(l + 1, j).wait_recv()
            w_send(0, l + 1)

        branch = rs_finish(p)
        br[l] = branch
        nhat, unused = normalize(branch)
        middle = st[l] + nhat * gain(l, 2) + gain(l, 3)
        mid[l] = middle
        nhat, unused = normalize(middle)
        ag_start(p + 1, a3.at[l], (nhat * gain(l, 4) + gain(l, 5)).astype(BF))
        ag_drain(p, a1.at[l])
        ag_pass(p + 1, a3.at[l])
        w_arrive(1, l)
        w_ready(1, l)


        def feed(pair):
            hidden = gelu(dot_nt(both(a3.at[l], pair), w_up(l))).astype(BF)
            return dot_nn(hidden, w_down(l))

        if SPLIT:
            rs_halves(p + 1, a3.at[l], feed)
        else:
            arrivals(p + 1, a3.at[l], lambda i, pair: rs_pair(p + 1, i, feed(pair)))

        @pl.when(more)
        def _():
            w_relay(0, l + 1)
            own_wm(l + 1).wait()
            w_send(1, l + 1)

        mlp_out = (rs_halves_finish if SPLIT else rs_finish)(p + 1)
        mo[l] = mlp_out

        @pl.when(more)
        def _():
            nhat, unused = normalize(mlp_out)
            st[l + 1] = mid[l] + nhat * gain(l, 6) + gain(l, 7)

        ag_drain(p + 1, a3.at[l])
        return carry

    lax.fori_loop(0, LAYERS, forward, 0)
    perm_wait(1)
    perm_wait(2)
    here = lax.broadcasted_iota(jnp.int32, (TB, TB), 0) == lax.broadcasted_iota(jnp.int32, (TB, TB), 1)
    column = jnp.sum(
        jnp.where(here, jnp.broadcast_to(sc_p[0:1, :], (TB, TB)), 0.0), axis=1, keepdims=True
    )
    g[...] = g_p[...].astype(F32) * column

    def add_norm(l, col, grad, nhat):
        ngrad[pl.ds(l * 8 + col, 1), :] = jnp.sum(grad * nhat, axis=0, keepdims=True)
        ngrad[pl.ds(l * 8 + col + 1, 1), :] = jnp.sum(grad, axis=0, keepdims=True)

    def gm_all(l):
        dst = wm.at[l + 1]
        per = UNITS // US
        count = HALF // UNITS
        far = flipped(n, N - 1, N)

        def chunk(i, carry):
            core = jnp.where(i < count, 1 - k, k)
            at = flipped(far // per, lax.rem(i, count), count)
            off = pl.multiple_of(core * HALF + at * UNITS, LANES)
            up = dot_tn(dpre_s[:, pl.ds(off, UNITS)], a3[l].reshape(T, D))
            down = dot_tn(hid_s[:, pl.ds(off, UNITS)], dm[...].reshape(T, D))
            rows = pl.ds(at * per, per)
            dst[core, rows, :, 0:D] = up.astype(BF).reshape(per, US, D)
            dst[core, rows, :, D : 2 * D] = down.astype(BF).reshape(per, US, D)

            @pl.when(i < count)
            def _():
                for e in range(per):
                    gm_mate(l, at * per + flipped(lax.rem(far, per), e, per)).start()

            return carry

        lax.fori_loop(0, 2 * count, chunk, 0)

    def gm_mate(l, at):
        return remote(wm.at[l + 1, 1 - k, at], gmr.at[at], mgm_s.at[l, at], mgm_r.at[l, at], mate)

    def ga_all(l):
        dst = wa.at[l + 1]
        rows = 2 * N * RW

        def chunk(i, carry):
            off = pl.multiple_of(i * rows, LANES)
            grad_a = dot_tn(a1[l, :, :, pl.ds(off, rows)].reshape(T, rows), dqkv[...])
            grad_p = dot_tn(db[:, :, pl.ds(off, rows)].reshape(T, rows), att[l].reshape(T, FQ))
            dst[i, :, :, :, 0 : 3 * FQ] = grad_a.astype(BF).reshape(2, N, RW, 3 * FQ)
            dst[i, :, :, :, 3 * FQ : 4 * FQ] = grad_p.astype(BF).reshape(2, N, RW, FQ)
            return carry

        lax.fori_loop(0, C, chunk, 0)

    def ga_mate(l):
        return remote(wa.at[l + 1, :, 1 - k], gar, mga_s.at[l], mga_r.at[l], mate)

    def zpart(kind, l, at):
        return wm.at[l + 1, k, at] if kind else wa.at[l + 1, :, k, at]

    def zbuf(kind, l, slot):
        return gmz.at[l, slot] if kind else gaz.at[l, slot]

    def zg_copy(kind, l, owner, device, send, recv):
        ssem, rsem = zg_s.at[2 * l + kind, send], zg_r.at[2 * l + kind, recv]
        return remote(zpart(kind, l, owner), zbuf(kind, l, recv), ssem, rsem, zdev(device))

    def z_direct(kind, l, d):
        return zg_copy(kind, l, n + d, n + d, d + N - 1, (-d) % N - 1)

    def z_beyond(kind, l, d):
        sign = 1 if d > 0 else -1
        return zg_copy(kind, l, n + d, n + d - sign * REACH, d + N - 1, N - 1 + abs(d) - REACH - 1)

    def z_spread(kind, l):
        for d in signed(1, N - 1):
            ready = inside(n + d)
            if abs(d) == REACH:
                ready = ready & jnp.logical_not(inside(n - d // REACH))

            @pl.when(ready)
            def _(d=d):
                (z_beyond if abs(d) > REACH else z_direct)(kind, l, d).start()

    def z_relay(kind, l):
        for sign in (1, -1):
            owner = n + sign * REACH

            @pl.when(inside(owner) & inside(n - sign))
            def _(sign=sign, owner=owner):
                part = zpart(kind, l, owner)
                for q in range(1, REACH):
                    @pl.when(inside(n - sign * q))
                    def _(q=q):
                        slot = N - 1 + q - 1
                        zg_copy(kind, l, n, n, 0, slot).wait_recv()
                        part[...] = (part[...].astype(F32) + zbuf(kind, l, slot)[...].astype(F32)).astype(BF)
                z_direct(kind, l, sign * REACH).start()

    def z_arrive(kind, l, add):
        for d in reversed(signed(1, REACH)):
            @pl.when(inside(n + d))
            def _(d=d):
                slot = d % N - 1
                zg_copy(kind, l, n, n, 0, slot).wait_recv()
                add(zbuf(kind, l, slot))

    def z_drain(kind, l):
        for d in signed(1, N - 1):
            @pl.when(inside(n + d))
            def _(d=d):
                (z_beyond if abs(d) > REACH else z_direct)(kind, l, d).wait_send()

    def gm_spread(l):
        src = wm.at[l + 1]

        def add(e, carry):
            at = flipped(n, N - 1 - e, N)
            gm_mate(l, at).wait_recv()
            src[k, at] = (src[k, at].astype(F32) + gmr[at].astype(F32)).astype(BF)
            dist = jnp.where(at > n, at - n, n - at)
            sign = jnp.where(at > n, 1, -1)
            far = dist > REACH
            device = jnp.where(far, at - sign * REACH, at)
            slot = jnp.where(far, N - 2 + dist - REACH, lax.rem(n - at + N, N) - 1)

            @pl.when((dist != 0) & ((dist != REACH) | jnp.logical_not(inside(n - sign))))
            def _():
                zg_copy(1, l, at, device, at - n + N - 1, slot).start()

            return carry

        lax.fori_loop(0, N, add, 0)

    def ga_spread(l):
        ga_mate(l).wait_recv()
        src = wa.at[l + 1]
        src[:, k] = (src[:, k].astype(F32) + gar[...].astype(F32)).astype(BF)
        z_spread(0, l)

    def gm_out(l):
        return local(stage, out_mlp.at[l], loc.at[2 * LAYERS + l])

    def gm_finish(l):
        stage[...] = wm[l + 1, k, n].astype(F32)

        def add(ref):
            stage[...] += ref[...].astype(F32)

        z_arrive(1, l, add)
        gm_out(l).start()
        z_drain(1, l)
        for at in range(N):
            gm_mate(l, at).wait_send()

    def xg(l, j):
        return remote(gax_s.at[l, j - 1], gax_r.at[l, j - 1], xg_s.at[l, j - 1], xg_r.at[l, j - 1], xy(j))

    def place(l, at, value):
        for part in range(3):
            cols = pl.ds(pl.multiple_of(part * D + at * FQ, LANES), FQ)
            held_qkv[l, :, cols] = value[:, part * FQ : (part + 1) * FQ]
        held_proj[l, :, pl.ds(pl.multiple_of(at * FQ, LANES), FQ)] = value[:, 3 * FQ : 4 * FQ]

    def ga_finish(l):
        stage_a[...] = wa[l + 1, :, k, n].astype(F32)

        def add(ref):
            stage_a[...] += ref[...].astype(F32)

        z_arrive(0, l, add)
        z_drain(0, l)
        ga_mate(l).wait_send()
        for j in range(1, C):
            gax_s[l, j - 1] = stage_a[chip(j)].astype(BF)
            xg(l, j).start()
        place(l, c, stage_a[c])

    def ga_out(l):
        return (
            local(held_qkv.at[l], out_qkv.at[l], fin.at[2 * l]),
            local(held_proj.at[l], out_proj.at[l], fin.at[2 * l + 1]),
        )

    def ga_place(l):
        for j in range(1, C):
            xg(l, j).wait()
            place(l, chip(j), gax_r[l, j - 1].astype(F32))
        for copy in ga_out(l):
            copy.start()

    def backward(i, carry):
        l = LAYERS - 1 - i
        p = 2 * LAYERS + 2 * i
        grad = g[...]
        nhat, rstd = normalize(mo[l])
        ag_start(p, dm, norm_back(nhat, rstd, grad, gain(l, 6)).astype(BF))
        add_norm(l, 6, grad, nhat)

        @pl.when(i == 0)
        def _():
            outh_s[...] = (mid[l] + nhat * gain(l, 6) + gain(l, 7)).astype(BF)
            perm_start(3)

        ag_pass(p, dm)

        def redo(i, carry):
            pre = dot_nt(a3[l, pl.ds(2 * i, 2)].reshape(2 * TB, D), w_up(l))
            rows = pl.ds(i * 2 * TB, 2 * TB)
            pre_s[rows, :] = pre
            hid_s[rows, :] = gelu(pre).astype(BF)
            return carry

        lax.fori_loop(0, C // 2, redo, 0)

        @pl.when(i > 0)
        def _():
            z_relay(0, l + 1)


        def feed_back(i, pair):
            where = [pl.ds(b * TB, TB) for b in pair]
            pre = jnp.concatenate([pre_s[rows, :] for rows in where], axis=0)
            slope = (dot_nt(both(dm, pair), w_down(l)) * gelu_slope(pre)).astype(BF)
            for e, rows in enumerate(where):
                dpre_s[rows, :] = slope[e * TB : (e + 1) * TB]
            rs_pair(p, i, dot_nn(slope, w_up(l)))

        arrivals(p, dm, feed_back)

        @pl.when(i > 0)
        def _():
            pl.semaphore_wait(credit.at[1], 1)

        gm_all(l)
        gm_spread(l)

        @pl.when(l > 0)
        def _():
            pl.semaphore_signal(credit.at[1], inc=1, device_id=mate, device_id_type=MESH)

        d_a3 = rs_finish(p)
        nhat, rstd = normalize(mid[l])
        d_mid = g[...] + norm_back(nhat, rstd, d_a3, gain(l, 4))
        g[...] = d_mid
        nhat_b, rstd_b = normalize(br[l])
        ag_start(p + 1, db, norm_back(nhat_b, rstd_b, d_mid, gain(l, 2)).astype(BF))
        add_norm(l, 4, d_a3, nhat)
        add_norm(l, 2, d_mid, nhat_b)
        ag_drain(p, dm)
        for b in range(C):
            weights, inverse = exp_scores(l, b)
            cols = pl.ds(TB * (b * (b + 1) // 2), (b + 1) * TB)
            p_s[:, cols] = (weights * inverse).astype(BF)
        dk_s[...] = jnp.zeros_like(dk_s)
        dv_s[...] = jnp.zeros_like(dv_s)
        ag_pass(p + 1, db)
        for j in range(1, C):
            ag_wait(p + 1, db, j)
        for b in reversed(range(C)):
            size = (b + 1) * TB
            rows = pl.ds(b * TB, TB)
            seen = pl.ds(0, size)
            d_att = by_head(dot_nn(db[b], w_proj(l)).astype(BF))
            d_probs = dot_nt(d_att, vs_[l, 0 : b + 1].reshape(size, FQ))
            low = p_s[:, pl.ds(TB * (b * (b + 1) // 2), size)]
            probs = low.astype(F32)
            delta = jnp.sum(probs * d_probs, axis=-1, keepdims=True)
            d_scores = (probs * (d_probs - delta)).astype(BF)
            d_query = of_heads(dot_nn(d_scores, ks_[l, 0 : b + 1].reshape(size, FQ)))
            d_query = d_query * HEAD_DIM ** (-0.5)
            dk_s[seen, :] += dot_tn(d_scores, by_head(qs_[l, b]))
            dv_s[seen, :] += dot_tn(low, d_att)
            d_key = dk_s[rows, :]
            cosine, sine = tables(b)
            dqkv[rows, 0:FQ] = (d_query * cosine - swapped(d_query) * sine).astype(BF)
            dqkv[rows, FQ : 2 * FQ] = (d_key * cosine - swapped(d_key) * sine).astype(BF)
            dqkv[rows, 2 * FQ : 3 * FQ] = dv_s[rows, :].astype(BF)
            rs_block(p + 1, b, dot_nt(dqkv[rows, :], w_qkv(l)))
        z_relay(1, l)

        @pl.when(i > 0)
        def _():
            pl.semaphore_wait(credit.at[0], 1)

        ga_all(l)
        ga_mate(l).start()

        @pl.when(i > 0)
        def _():
            gm_finish(l + 1)
            ga_finish(l + 1)

        ga_spread(l)

        @pl.when(l > 0)
        def _():
            pl.semaphore_signal(credit.at[0], inc=1, device_id=mate, device_id_type=MESH)

        d_a1 = rs_finish(p + 1)
        nhat, rstd = normalize(st[l])
        g[...] = g[...] + norm_back(nhat, rstd, d_a1, gain(l, 0))
        add_norm(l, 0, d_a1, nhat)
        ag_drain(p + 1, db)

        @pl.when(i == 0)
        def _():
            for kind in range(2):
                for at in range(LAYERS):
                    w_drain(kind, at)
            for at in range(3):
                perm_drain(at)

        return carry

    lax.fori_loop(0, LAYERS, backward, 0)

    g_p[...] = g[...].astype(BF)
    perm_wait(3)
    n_start(1, "m", ngrad[...])
    n_start(1, "x", n_finish(1, "m"))
    z_relay(0, 0)
    n_start(1, "z", n_finish(1, "x"))
    ga_place(1)
    gm_out(1).wait()
    perm_start(4)
    gm_finish(0)
    ga_finish(0)
    total = n_finish(1, "z")
    for l in range(LAYERS):
        out_n[l] = lax.dot_general(
            total[l * 8 : (l + 1) * 8], spot, (((1,), (1,)), ((), ())),
            preferred_element_type=F32, precision=lax.Precision.HIGHEST,
        )
    ga_place(0)
    gm_out(0).wait()

    for l in range(LAYERS):
        for j in range(1, C):
            a2a_all(l, j).wait_send()
    perm_wait(4)
    g[...] = hid_p[...].astype(F32)
    grad_out = local(g, out_g, fin.at[2 * LAYERS])
    grad_out.start()
    perm_drain(3)
    perm_drain(4)
    for l in range(LAYERS):
        for copy in ga_out(l):
            copy.wait()
    grad_out.wait()


def copy_out(*refs):
    count = (len(refs) - 1) // 3
    sems = refs[-1]
    into, out = [], []
    for i in range(count):
        src, dst, held = refs[i], refs[count + i], refs[2 * count + i]
        cuts = [(l,) for l in range(held.shape[0])] if len(held.shape) == 3 else [()]
        for at in cuts:
            one, two, three = (ref.at[at] if at else ref for ref in (src, held, dst))
            into.append(pltpu.make_async_copy(one, two, sems.at[2 * len(into)]))
            out.append(pltpu.make_async_copy(two, three, sems.at[2 * len(out) + 1]))
    for copy in into:
        copy.start()
    for first, second in zip(into, out):
        first.wait()
        second.start()
    for copy in out:
        copy.wait()


def body(mesh, hidden_in, w_qkv, w_proj, w_mlp, norm_params, grad_output, corpus_id, corpus_weight):
    W, N = mesh.shape["wide"], mesh.shape["narrow"]
    C = W // 2
    TB, D = hidden_in.shape
    FQ, UQ, RW, US = D // C, FF // C, D // (W * N), FF // (W * N)
    AW = 4 * FQ
    T = C * TB
    REACH = N // 2
    assert C == N and w_mlp.shape[1] == US and w_qkv.shape[1] == RW

    half = HEAD_DIM // 2
    freqs = np.float32(ROPE_BASE) ** (-np.arange(half, dtype=np.float32) / np.float32(half))
    angles = (np.arange(T, dtype=np.float32)[:, None] * freqs[None, :]).astype(np.float32)
    cosine = np.tile(np.cos(angles), (1, LANES // half)).astype(np.float32)
    sine = np.sin(angles)
    sine = np.tile(np.concatenate([-sine, sine], axis=1), (1, LANES // HEAD_DIM)).astype(np.float32)

    NR = LAYERS * 8
    dma = pltpu.SemaphoreType.DMA
    vm = pltpu.VMEM
    L = LAYERS
    scratch = [
        vm((T, LANES), F32),
        vm((T, LANES), F32),
        vm((L, RW, 3 * D), F32),
        vm((L, RW, D), F32),
        vm((L + 1, C, 2, N, RW, AW), BF),
        vm((L + 1, 2, N, US, 2 * D), BF),
        vm((L, C, TB, D), BF),
        vm((L, C, TB, D), BF),
        vm((C, TB, D), BF),
        vm((C, TB, D), BF),
        vm((L, C, TB, FQ), BF),
        vm((L, C, TB, FQ), BF),
        vm((L, C, TB, FQ), BF),
        vm((L, C, TB, FQ), BF),
        vm((L, TB, D), F32),
        vm((L, TB, D), F32),
        vm((L, TB, D), F32),
        vm((L, TB, D), F32),
        vm((T, UQ), F32),
        vm((T, UQ), BF),
        vm((T, UQ), BF),
        vm((FQ // HEAD_DIM * TB, TB * C * (C + 1) // 2), BF),
        vm((T, FQ), F32),
        vm((T, FQ), F32),
        vm((T, 3 * FQ), BF),
        vm((C - 1, TB, D), BF),
        vm((C - 1, TB, D), BF),
        vm((2, TB // 2, D), BF),
        vm((TB, D), F32),
        vm((TB, D), BF),
        vm((TB, D), BF),
        vm((8, TB), F32),
        vm((8, TB), F32),
        vm((TB, D), BF),
        vm((TB, D), F32),
        vm((N, US, 2 * D), BF),
        vm((L, N + REACH - 2, US, 2 * D), BF),
        vm((US, 2 * D), F32),
        vm((C, RW, AW), F32),
        vm((C, N, RW, AW), BF),
        vm((L, N + REACH - 2, C, RW, AW), BF),
        vm((L, C - 1, RW, AW), BF),
        vm((L, C - 1, RW, AW), BF),
        vm((NR, D), F32),
        vm((NR, D), F32),
        vm((3, NR, D), BF),
        vm((3, C - 1, NR, D), BF),
        vm((3, NR, D), F32),
        vm((3, C - 1, NR, D), F32),
        dma((5,)), dma((5,)),
        dma((3 * L,)),
        dma((L, C - 1)), dma((L, C - 1)),
        dma((2, max(C - 1, 6))), dma((2, max(C - 1, 6))),
        dma((2, max(C - 1, 6))), dma((2, max(C - 1, 6))),
        dma((2 * L, 4 * REACH)), dma((2 * L, N)),
        dma((2 * L, N)), dma((2 * L, N)),
        dma((2 * L, 2 * N - 1)), dma((2 * L, N + REACH - 2)),
        dma((L,)), dma((L,)),
        dma((L, N)), dma((L, N)),
        dma((L, C - 1)), dma((L, C - 1)),
        dma((2, C - 1)), dma((2, C - 1)),
        dma((2, N - 1)), dma((2, N - 1)),
        dma((2,)), dma((2,)),
        dma((2 * L + 3,)),
        pltpu.SemaphoreType.REGULAR((2,)),
    ]
    vspec = pl.BlockSpec(memory_space=pltpu.VMEM)
    anyspec = pl.BlockSpec(memory_space=pl.ANY)
    shapes = (
        jax.ShapeDtypeStruct((TB, D), BF),
        jax.ShapeDtypeStruct((TB, D), F32),
        jax.ShapeDtypeStruct((L, RW, 3 * D), F32),
        jax.ShapeDtypeStruct((L, RW, D), F32),
        jax.ShapeDtypeStruct((L, US, 2 * D), F32),
        jax.ShapeDtypeStruct((L, 8, RW), F32),
    )
    outs = pl.pallas_call(
        partial(kernel_body, (C, N, TB, D, FQ, UQ, RW, US, AW)),
        out_shape=shapes,
        in_specs=[anyspec] * 2 + [vspec] * 3 + [anyspec] * 5,
        out_specs=(anyspec,) * 5 + (vspec,),
        scratch_shapes=scratch,
        compiler_params=pltpu.CompilerParams(
            collective_id=0, has_side_effects=True, vmem_limit_bytes=63 << 20
        ),
    )(
        hidden_in, grad_output, corpus_id.reshape(1, TB), corpus_weight.reshape(1, -1), norm_params.transpose(0, 2, 1),
        jnp.asarray(cosine), jnp.asarray(sine), w_qkv, w_proj, w_mlp,
    )
    outs = pl.pallas_call(
        copy_out,
        out_shape=shapes,
        in_specs=[anyspec] * len(shapes),
        out_specs=(anyspec,) * len(shapes),
        scratch_shapes=[vm(one.shape, one.dtype) for one in shapes] + [dma((4 * len(shapes),))],
        compiler_params=pltpu.CompilerParams(vmem_limit_bytes=60 << 20),
    )(*outs)
    return (*outs[:5], outs[5].transpose(0, 2, 1))


def solution(mesh):
    rows = P(("wide", "narrow"), None)
    layered = P(None, ("wide", "narrow"), None)
    return jax.shard_map(
        partial(body, mesh),
        mesh=mesh,
        in_specs=(rows, layered, layered, layered, layered, rows, P(("wide", "narrow")), P()),
        out_specs=(rows, rows, layered, layered, layered, layered),
        check_vma=False,
    )
```

```python
from functools import partial

import jax
import jax.numpy as jnp
import numpy as np
from jax import lax
from jax.experimental import pallas as pl
from jax.experimental.pallas import tpu as pltpu
from jax.sharding import PartitionSpec as P

HEADS = 16
HEAD_DIM = 64
FF = 4096
LAYERS = 2
EPS = 1e-05
MASKED = -1e30
ROPE_BASE = 10000.0
MESH = pl.DeviceIdType.MESH
BF = jnp.bfloat16
F32 = jnp.float32
LANES = 128
UNITS = 256


def dot_nn(left, right):
    return lax.dot_general(left, right, (((1,), (0,)), ((), ())), preferred_element_type=F32)


def dot_nt(left, right):
    return lax.dot_general(left, right, (((1,), (1,)), ((), ())), preferred_element_type=F32)


def dot_tn(left, right):
    return lax.dot_general(left, right, (((0,), (0,)), ((), ())), preferred_element_type=F32)


def normalize(inputs):
    centre = jnp.mean(inputs, axis=-1, keepdims=True)
    centered = inputs - centre
    rstd = lax.rsqrt(jnp.mean(centered * centered, axis=-1, keepdims=True) + EPS)
    return centered * rstd, rstd


def norm_back(nhat, rstd, grad, gain):
    scaled = grad * gain
    mean_f = jnp.mean(scaled, axis=-1, keepdims=True)
    mean_fn = jnp.mean(scaled * nhat, axis=-1, keepdims=True)
    return rstd * (scaled - mean_f - nhat * mean_fn)


GELU_S = 0.7978845608028654
GELU_A = 0.044715


def gelu(pre):
    return 0.5 * pre * (1.0 + jnp.tanh(GELU_S * (pre + GELU_A * pre * pre * pre)))


def gelu_slope(pre):
    square = pre * pre
    turned = jnp.tanh(GELU_S * (pre + GELU_A * pre * square))
    inner = GELU_S * (1.0 + 3.0 * GELU_A * square)
    return 0.5 * (1.0 + turned) + 0.5 * pre * (1.0 - turned * turned) * inner


def kernel_body(
    dims,
    hid_ref, gout_ref, ids_ref, cw_ref, nrm_ref, cos_in, sin_in, wq_ref, wp_ref, wm_ref,
    out_h, out_g, out_qkv, out_proj, out_mlp, out_n,
    cos_ref, sin_ref, held_qkv, held_proj,
    wa, wm, a1, a3, dm, db, qs_, ks_, vs_, att, st, br, mid, mo,
    pre_s, hid_s, dpre_s, p_s, dk_s, dv_s, dqkv,
    rs_send, rs_recv, rs_mid, acc, hid_p, g_p, sc_own, sc_x, sc_p, outh_s, hx, g,
    gmr, gmz, stage, stage_a, gar, gaz, gax_s, gax_r,
    npar, ngrad, nf_send, nf_recv, nb_send, nb_recv,
    perm_s, perm_r, gp_s, gp_r, gz_s, gz_r, oz_s, oz_r, op_s, op_r, loc, a2a_s, a2a_r, ag_s, ag_r, rs_s, rs_r,
    zw_s, zw_r, mw_s, mw_r, zg_s, zg_r, mga_s, mga_r, mgm_s, mgm_r, xg_s, xg_r,
    nx_s, nx_r, nz_s, nz_r, nm_s, nm_r, fin, credit,
):
    C, N, TB, D, FQ, UQ, RW, US, AW = dims
    T = C * TB
    HPC = FQ // HEAD_DIM
    HALF = N * US
    REACH = N // 2
    w = lax.axis_index("wide")
    n = lax.axis_index("narrow")
    c = w // 2
    k = lax.rem(w, 2)
    mate = (2 * c + (1 - k), n)
    to_chip = n + k * (N - 1 - 2 * n)
    to_plane = c + k * (N - 1 - 2 * c)
    swap = (2 * to_chip + k, to_plane)
    moves = to_chip != c

    def block(at):
        return at + k * (C - 1 - 2 * at)

    mine = block(c)

    def flipped(base, j, count):
        out, bit = 0, 1
        while bit < count:
            ours = lax.rem(base // bit, 2)
            flip = (j // bit) % 2 if isinstance(j, int) else lax.rem(j // bit, 2)
            out = out + bit * (ours + flip - 2 * ours * flip)
            bit *= 2
        return out

    def chip(j):
        return flipped(c, j, C)

    def xy(j):
        return (2 * chip(j) + k, n)

    def zdev(at):
        return (w, at)

    def remote(src, dst, ssem, rsem, device):
        return pltpu.make_async_remote_copy(
            src_ref=src, dst_ref=dst, send_sem=ssem, recv_sem=rsem,
            device_id=device, device_id_type=MESH,
        )

    def local(src, dst, sem):
        return pltpu.make_async_copy(src, dst, sem)

    barrier = pltpu.get_barrier_semaphore()
    partners = [xy(j) for j in range(1, C)] + [mate]
    partners += [zdev(lax.rem(n + j, N)) for j in range(1, N)]
    for device in partners:
        pl.semaphore_signal(barrier, inc=1, device_id=device, device_id_type=MESH)

    @pl.when(moves)
    def _():
        pl.semaphore_signal(barrier, inc=1, device_id=swap, device_id_type=MESH)

    pl.semaphore_wait(barrier, len(partners) + jnp.where(moves, 1, 0))

    rope = (
        local(cos_in, cos_ref, fin.at[2 * LAYERS + 1]), local(sin_in, sin_ref, fin.at[2 * LAYERS + 2])
    )
    for copy in rope:
        copy.start()

    def either(far, src, dst, ssem, rsem, device, act):
        @pl.when(far)
        def _():
            getattr(remote(src, dst, ssem, rsem, device), {"here": "wait_recv", "sent": "wait_send"}.get(act, act))()

        if act != "sent":
            @pl.when(jnp.logical_not(far))
            def _():
                getattr(local(src, dst, rsem), {"here": "wait"}.get(act, act))()

    def perm(i, act):
        src, dst = ((hid_ref, hid_p), (g_p, hid_p))[i]
        either(moves, src, dst, perm_s.at[i], perm_r.at[i], swap, act)

    holder = c == to_chip

    def grad_plane(act):
        for e, (src, dst) in enumerate(((gout_ref, db.at[c]), (sc_own, sc_x.at[c]))):
            either(jnp.logical_not(holder), src, dst, gp_s.at[e], gp_r.at[e, c], (2 * to_chip + k, n), act)

    def grad_held():
        for at in range(C):
            for e, dst in enumerate((db.at[at], sc_x.at[at])):
                either(c != at, dst, dst, gp_s.at[e], gp_r.at[e, at], (2 * at + k, n), "here")

    def grad_z(act):
        for at in range(C):
            plane = at + k * (N - 1 - 2 * at)
            for e, (src, dst) in enumerate(((db.at[at], g_p), (sc_x.at[at], sc_p))):
                either(plane != n, src, dst, gz_s.at[e, at], gz_r.at[e], (w, plane), act)

    def grad_here():
        for e, dst in enumerate((g_p, sc_p)):
            either(to_plane != n, dst, dst, gz_s.at[e, 0], gz_r.at[e], (w, to_plane), "here")

    def out_z(act):
        either(to_plane != n, outh_s, hx.at[n], oz_s.at[0], oz_r.at[n], (w, to_plane), act)

    def out_held():
        for at in range(N):
            either(n != at, hx.at[at], hx.at[at], oz_s.at[0], oz_r.at[at], (w, at), "here")

    def out_plane(act):
        for at in range(N):
            dest = at + k * (N - 1 - 2 * at)
            either(dest != c, hx.at[at], out_h, op_s.at[at], op_r.at[0], (2 * dest + k, n), act)

    def out_here():
        either(jnp.logical_not(holder), hx.at[0], out_h, op_s.at[0], op_r.at[0], (2 * to_chip + k, n), "here")

    perm(0, "start")

    def n_copy(way, axis, j):
        send, heard = (nf_send, nf_recv) if way == 0 else (nb_send, nb_recv)
        slot = n_slot[axis]
        if axis == "x":
            return remote(send.at[slot], heard.at[slot, j - 1], nx_s.at[way, j - 1], nx_r.at[way, j - 1], xy(j))
        if axis == "z":
            there = zdev(lax.rem(n + j, N))
            return remote(send.at[slot], heard.at[slot, j - 1], nz_s.at[way, j - 1], nz_r.at[way, j - 1], there)
        return remote(send.at[slot], heard.at[slot, j - 1], nm_s.at[way], nm_r.at[way], mate)

    n_count = {"x": C, "z": N, "m": 2}
    n_slot = {"x": 0, "z": 1, "m": 2}

    def n_start(way, axis, value):
        send = nf_send if way == 0 else nb_send
        send[n_slot[axis]] = value.astype(send.dtype)
        for j in range(1, n_count[axis]):
            n_copy(way, axis, j).start()

    def n_finish(way, axis):
        send, heard = (nf_send, nf_recv) if way == 0 else (nb_send, nb_recv)
        total = send[n_slot[axis]].astype(F32)
        for j in range(1, n_count[axis]):
            n_copy(way, axis, j).wait()
            total = total + heard[n_slot[axis], j - 1].astype(F32)
        return total

    first = (w * N + n) * RW
    spot = lax.broadcasted_iota(jnp.int32, (RW, D), 1) == (
        lax.broadcasted_iota(jnp.int32, (RW, D), 0) + first
    )
    spot = spot.astype(F32)
    n_start(0, "x", jnp.concatenate(
        [dot_nn(nrm_ref[l], spot.astype(BF)) for l in range(LAYERS)], axis=0
    ))

    def pieces(l, at):
        for part in range(3):
            cols = pl.ds(pl.multiple_of(part * D + at * FQ, LANES), FQ)
            yield wq_ref.at[l, :, cols], wa.at[l, c, k, n, :, pl.ds(part * FQ, FQ)]
        cols = pl.ds(pl.multiple_of(at * FQ, LANES), FQ)
        yield wp_ref.at[l, :, cols], wa.at[l, c, k, n, :, pl.ds(3 * FQ, FQ)]

    def a2a_start(l):
        for j in range(1, C):
            for src, dst in pieces(l, chip(j)):
                remote(src, dst, a2a_s.at[l, j - 1], a2a_r.at[l, j - 1], xy(j)).start()

    def a2a_all(l, j):
        there = wa.at[l, chip(j), k, n]
        return remote(there, there, a2a_s.at[l, j - 1], a2a_r.at[l, j - 1], xy(j))

    def own_wa(l):
        mine = wa.at[l, c, k, n]
        return local(mine, mine, loc.at[l])

    def own_wm(l):
        return local(wm_ref.at[l], wm.at[l, k, n], loc.at[LAYERS + l])

    a2a_start(0)
    for l in range(LAYERS):
        for src, dst in pieces(l, c):
            local(src, dst, loc.at[l]).start()
        own_wm(l).start()

    def shard(kind, l, core, at):
        return wm.at[l, core, at] if kind else wa.at[l, :, core, at]

    def inside(at):
        return (at >= 0) & (at < N)

    def signed(least, most):
        return [sign * d for d in range(most, least - 1, -1) for sign in (1, -1)]

    def zw_copy(kind, l, origin, at, slot):
        rows = shard(kind, l, k, origin)
        return remote(rows, rows, zw_s.at[2 * l + kind, slot], zw_r.at[2 * l + kind, origin], zdev(at))

    def direct_slot(d):
        return d + REACH

    def relay_slot(sign, q):
        return 2 * REACH + (q if sign > 0 else q + REACH - 1)

    def to_mate(kind, l, at, core=k):
        rows = shard(kind, l, core, at)
        return remote(rows, rows, mw_s.at[2 * l + kind, at], mw_r.at[2 * l + kind, at], mate)

    def w_send(kind, l):
        for d in signed(1, REACH):
            @pl.when(inside(n + d))
            def _(d=d):
                zw_copy(kind, l, n, n + d, direct_slot(d)).start()

        to_mate(kind, l, n).start()

    def w_relay(kind, l):
        for sign in (1, -1):
            origin = n - sign * REACH

            @pl.when(inside(origin) & inside(n + sign))
            def _(sign=sign, origin=origin):
                zw_copy(kind, l, origin, n, 0).wait_recv()
                for q in range(1, REACH):
                    @pl.when(inside(n + sign * q))
                    def _(q=q):
                        zw_copy(kind, l, origin, n + sign * q, relay_slot(sign, q)).start()

    def w_arrive(kind, l):
        for d in reversed(signed(1, N - 1)):
            origin = n + d

            @pl.when(inside(origin))
            def _(d=d, origin=origin):
                if abs(d) == REACH:
                    sign = -1 if d > 0 else 1

                    @pl.when(jnp.logical_not(inside(n + sign)))
                    def _():
                        zw_copy(kind, l, origin, n, 0).wait_recv()
                else:
                    zw_copy(kind, l, origin, n, 0).wait_recv()
                to_mate(kind, l, origin).start()

    def w_ready(kind, l):
        for at in range(N):
            to_mate(kind, l, at, 1 - k).wait_recv()

    def w_drain(kind, l):
        for d in signed(1, REACH):
            @pl.when(inside(n + d))
            def _(d=d):
                zw_copy(kind, l, n, n + d, direct_slot(d)).wait_send()

        for sign in (1, -1):
            origin = n - sign * REACH
            for q in range(1, REACH):
                @pl.when(inside(origin) & inside(n + sign) & inside(n + sign * q))
                def _(sign=sign, origin=origin, q=q):
                    zw_copy(kind, l, origin, n + sign * q, relay_slot(sign, q)).wait_send()

        for at in range(N):
            to_mate(kind, l, at).wait_send()

    n_start(0, "z", n_finish(0, "x"))
    own_wa(0).wait()
    for j in range(1, C):
        a2a_all(0, j).wait_recv()
    w_send(0, 0)
    n_start(0, "m", n_finish(0, "z"))
    npar[...] = n_finish(0, "m")
    ngrad[...] = jnp.zeros_like(ngrad)

    def gain(l, col):
        return npar[pl.ds(l * 8 + col, 1), :]

    SPLIT = C == 4
    hops = ((1, 0), (1, 1), (2, 1), (2, 0), (2, 0), (1, 1))

    def ag_copy(p, buf, source, slot):
        if not SPLIT:
            rows = buf.at[block(source)]
            return remote(rows, rows, ag_s.at[lax.rem(p, 2), slot], ag_r.at[lax.rem(p, 2), slot], xy(slot + 1))
        j, part = hops[slot]
        rows = buf.at[block(source), pl.ds(part * (TB // 2), TB // 2)]
        return remote(rows, rows, ag_s.at[lax.rem(p, 2), slot], ag_r.at[lax.rem(p, 2), slot], xy(j))

    def ag_start(p, buf, value):
        buf[mine] = value
        for slot in (0, 2, 1, 3) if SPLIT else range(C - 1):
            ag_copy(p, buf, c, slot).start()

    def ag_pass(p, buf):
        if SPLIT:
            ag_copy(p, buf, chip(1), 0).wait_recv()
            ag_copy(p, buf, chip(1), 4).start()
            ag_copy(p, buf, chip(2), 2).wait_recv()
            ag_copy(p, buf, chip(2), 5).start()

    def ag_wait(p, buf, j):
        for slot in ((), (1,), (3,), (4, 5))[j] if SPLIT else (j - 1,) * min(j, 1):
            ag_copy(p, buf, chip(j), slot).wait_recv()

    def ag_drain(p, buf):
        for slot in range(4) if SPLIT else range(C - 1):
            ag_copy(p, buf, c, slot).wait_send()
        if SPLIT:
            ag_copy(p, buf, chip(1), 4).wait_send()
            ag_copy(p, buf, chip(2), 5).wait_send()

    def rs_copy(p, j):
        return remote(rs_send.at[j - 1], rs_recv.at[j - 1], rs_s.at[lax.rem(p, 2), j - 1], rs_r.at[lax.rem(p, 2), j - 1], xy(j))

    def rs_put(p, j, value):
        @pl.when(j > 0)
        def _():
            rs_send[j - 1] = value.astype(BF)
            rs_copy(p, j).start()

        @pl.when(j == 0)
        def _():
            acc[...] = value

    def rs_block(p, b, value):
        rs_put(p, chip(block(b)), value)

    def rs_pair(p, i, value):
        rs_put(p, 2 * i, value[0:TB])
        rs_send[2 * i] = value[TB:].astype(BF)
        rs_copy(p, 2 * i + 1).start()

    def half_copy(p, slot):
        part = pl.ds((0, 1, 1, 0, 0, 1)[slot] * (TB // 2), TB // 2)
        src = rs_send.at[(0, 0, 1, 1, 2, 2)[slot], part]
        dst = rs_mid.at[slot - 4] if slot >= 4 else rs_recv.at[(0, 0, 1, 1)[slot], part]
        return remote(src, dst, rs_s.at[lax.rem(p, 2), slot], rs_r.at[lax.rem(p, 2), slot], xy((1, 1, 2, 2, 1, 2)[slot]))

    def half_put(p, i, value):
        @pl.when(i == 0)
        def _():
            rs_send[2] = value.astype(BF)
            half_copy(p, 4).start()
            half_copy(p, 5).start()

        @pl.when(i == 1)
        def _():
            rs_send[0] = value.astype(BF)
            half_copy(p, 0).start()

        @pl.when(i == 2)
        def _():
            rs_send[1] = value.astype(BF)
            half_copy(p, 2).start()

        @pl.when(i == 3)
        def _():
            acc[...] = value

    def half_chip(i):
        return chip(jnp.where(i == 0, 3, jnp.where(i == 3, 0, i)))

    def half_pass(p):
        for slot, at, rows, onward in ((4, 1, pl.ds(0, TB // 2), 3), (5, 0, pl.ds(TB // 2, TB // 2), 1)):
            half_copy(p, slot).wait_recv()
            rs_send[at, rows] = (rs_send[at, rows].astype(F32) + rs_mid[slot - 4].astype(F32)).astype(BF)
            half_copy(p, onward).start()

    def rs_halves_finish(p):
        for slot in range(4):
            half_copy(p, slot).wait()
        half_copy(p, 4).wait_send()
        half_copy(p, 5).wait_send()
        return acc[...] + rs_recv[0].astype(F32) + rs_recv[1].astype(F32)

    def arrivals(p, buf, use):
        def step(i, carry):
            for at in range(C // 2):
                @pl.when(i == at)
                def _(at=at):
                    ag_wait(p, buf, 2 * at)
                    ag_wait(p, buf, 2 * at + 1)

            use(i, (block(chip(2 * i)), block(chip(2 * i + 1))))
            return carry

        lax.fori_loop(0, C // 2, step, 0)

    def both(ref, pair):
        return jnp.concatenate([ref[b] for b in pair], axis=0)

    def rs_finish(p):
        total = acc[...]
        for j in range(1, C):
            rs_copy(p, j).wait()
            total = total + rs_recv[j - 1].astype(F32)
        return total

    lane = lax.broadcasted_iota(jnp.int32, (TB, FQ), 1)
    low_half = lax.rem(lane, HEAD_DIM) < HEAD_DIM // 2
    head_of = lane // HEAD_DIM
    causal = lax.broadcasted_iota(jnp.int32, (HPC * TB, TB), 1) <= lax.rem(
        lax.broadcasted_iota(jnp.int32, (HPC * TB, TB), 0), TB
    )

    def tables(b):
        rows = pl.ds(b * TB, TB)
        reps = FQ // LANES
        return (
            jnp.concatenate([cos_ref[rows, :]] * reps, axis=1),
            jnp.concatenate([sin_ref[rows, :]] * reps, axis=1),
        )

    def swapped(u):
        half_dim = HEAD_DIM // 2
        return jnp.where(
            low_half, pltpu.roll(u, FQ - half_dim, 1), pltpu.roll(u, half_dim, 1)
        )

    def w_qkv(l):
        return wa[l, :, :, :, :, 0 : 3 * FQ].reshape(D, 3 * FQ)

    def w_proj(l):
        return wa[l, :, :, :, :, 3 * FQ : 4 * FQ].reshape(D, FQ)

    def w_up(l):
        return wm[l, :, :, :, 0:D].reshape(UQ, D)

    def w_down(l):
        return wm[l, :, :, :, D : 2 * D].reshape(UQ, D)

    def by_head(rows):
        return jnp.concatenate(
            [jnp.where(head_of == h, rows, jnp.zeros((), rows.dtype)) for h in range(HPC)], axis=0
        )

    def of_heads(stacked):
        out = stacked[0:TB]
        for h in range(1, HPC):
            out = jnp.where(head_of == h, stacked[h * TB : (h + 1) * TB], out)
        return out

    def exp_scores(l, b):
        scores = dot_nt(by_head(qs_[l, b]), ks_[l, 0 : b + 1].reshape((b + 1) * TB, FQ))
        last = jnp.where(causal, scores[:, b * TB :], MASKED)
        scores = jnp.concatenate([scores[:, : b * TB], last], axis=1) if b else last
        weights = jnp.exp(scores - jnp.max(scores, axis=-1, keepdims=True))
        return weights, 1.0 / jnp.sum(weights, axis=-1, keepdims=True)

    w_relay(0, 0)
    own_wm(0).wait()
    w_send(1, 0)
    perm(0, "here")
    st[0] = hid_p[...].astype(F32)
    ids = jnp.broadcast_to(ids_ref[...], (8, TB))
    scale = jnp.zeros((8, TB), F32)
    for i in range(cw_ref.shape[1]):
        scale = jnp.where(ids == i, cw_ref[:, i : i + 1], scale)
    sc_own[...] = scale
    for copy in rope:
        copy.wait()

    def grad_move():
        @pl.when(holder)
        def _():
            grad_held()
            grad_z("start")

    def forward(l, carry):
        p = 2 * l
        more = l + 1 < LAYERS
        nhat, unused = normalize(st[l])
        ag_start(p, a1.at[l], (nhat * gain(l, 0) + gain(l, 1)).astype(BF))

        @pl.when(l == 0)
        def _():
            a2a_start(1)

        ag_pass(p, a1.at[l])

        @pl.when(l == 0)
        def _():
            grad_plane("start")

        w_arrive(0, l)
        w_ready(0, l)

        def qkv_step(i, pair):
            u = dot_nn(both(a1.at[l], pair), w_qkv(l))
            for e, b in enumerate(pair):
                cosine, sine = tables(b)
                uq = u[e * TB : (e + 1) * TB, 0:FQ]
                uk = u[e * TB : (e + 1) * TB, FQ : 2 * FQ]
                uq = (uq * cosine + swapped(uq) * sine).astype(BF)
                qs_[l, b] = (uq * HEAD_DIM ** (-0.5)).astype(BF)
                ks_[l, b] = (uk * cosine + swapped(uk) * sine).astype(BF)
                vs_[l, b] = u[e * TB : (e + 1) * TB, 2 * FQ :].astype(BF)

        arrivals(p, a1.at[l], qkv_step)
        def attend(b):
            weights, inverse = exp_scores(l, b)
            mixed = dot_nn(weights.astype(BF), vs_[l, 0 : b + 1].reshape((b + 1) * TB, FQ))
            low = of_heads(mixed * inverse).astype(BF)
            att[l, b] = low
            return dot_nt(low, w_proj(l))

        if SPLIT:

            def attend_step(i, carry):
                for b in range(C):
                    @pl.when(block(half_chip(i)) == b)
                    def _(b=b):
                        acc[...] = attend(b)

                half_put(p, i, acc[...])
                return carry

            lax.fori_loop(0, C, attend_step, 0)
            half_pass(p)
        else:
            for b in range(C):
                rs_block(p, b, attend(b))
        w_relay(1, l)

        @pl.when(more)
        def _():
            own_wa(l + 1).wait()
            for j in range(1, C):
                a2a_all(l + 1, j).wait_recv()
            w_send(0, l + 1)

        branch = (rs_halves_finish if SPLIT else rs_finish)(p)
        br[l] = branch
        nhat, unused = normalize(branch)
        middle = st[l] + nhat * gain(l, 2) + gain(l, 3)
        mid[l] = middle
        nhat, unused = normalize(middle)
        ag_start(p + 1, a3.at[l], (nhat * gain(l, 4) + gain(l, 5)).astype(BF))
        ag_drain(p, a1.at[l])
        ag_pass(p + 1, a3.at[l])
        w_arrive(1, l)
        w_ready(1, l)


        def feed(pair):
            hidden = gelu(dot_nt(both(a3.at[l], pair), w_up(l))).astype(BF)
            return dot_nn(hidden, w_down(l))

        if SPLIT:
            for j in range(1, C):
                ag_wait(p + 1, a3.at[l], j)

            def feed_step(i, carry):
                value = feed((block(half_chip(2 * i)), block(half_chip(2 * i + 1))))
                half_put(p + 1, 2 * i, value[0:TB])
                half_put(p + 1, 2 * i + 1, value[TB:])
                return carry

            lax.fori_loop(0, 2, feed_step, 0)

            @pl.when(jnp.logical_not(more))
            def _():
                grad_move()

            half_pass(p + 1)
        else:
            @pl.when(jnp.logical_not(more))
            def _():
                grad_move()

            arrivals(p + 1, a3.at[l], lambda i, pair: rs_pair(p + 1, i, feed(pair)))

        @pl.when(more)
        def _():
            w_relay(0, l + 1)
            own_wm(l + 1).wait()
            w_send(1, l + 1)

        mlp_out = (rs_halves_finish if SPLIT else rs_finish)(p + 1)
        mo[l] = mlp_out

        @pl.when(more)
        def _():
            nhat, unused = normalize(mlp_out)
            st[l + 1] = mid[l] + nhat * gain(l, 6) + gain(l, 7)

        ag_drain(p + 1, a3.at[l])
        return carry

    lax.fori_loop(0, LAYERS, forward, 0)
    grad_here()
    here = lax.broadcasted_iota(jnp.int32, (TB, TB), 0) == lax.broadcasted_iota(jnp.int32, (TB, TB), 1)
    column = jnp.sum(
        jnp.where(here, jnp.broadcast_to(sc_p[0:1, :], (TB, TB)), 0.0), axis=1, keepdims=True
    )
    g[...] = g_p[...].astype(F32) * column

    def add_norm(l, col, grad, nhat):
        ngrad[pl.ds(l * 8 + col, 1), :] = jnp.sum(grad * nhat, axis=0, keepdims=True)
        ngrad[pl.ds(l * 8 + col + 1, 1), :] = jnp.sum(grad, axis=0, keepdims=True)

    def gm_mate(l, at):
        return remote(wm.at[l + 1, 1 - k, at], gmr.at[at], mgm_s.at[l, at], mgm_r.at[l, at], mate)

    def ga_all(l):
        dst = wa.at[l + 1]
        rows = 2 * N * RW

        def chunk(i, carry):
            off = pl.multiple_of(i * rows, LANES)
            grad_a = dot_tn(a1[l, :, :, pl.ds(off, rows)].reshape(T, rows), dqkv[...])
            grad_p = dot_tn(db[:, :, pl.ds(off, rows)].reshape(T, rows), att[l].reshape(T, FQ))
            dst[i, :, :, :, 0 : 3 * FQ] = grad_a.astype(BF).reshape(2, N, RW, 3 * FQ)
            dst[i, :, :, :, 3 * FQ : 4 * FQ] = grad_p.astype(BF).reshape(2, N, RW, FQ)
            return carry

        lax.fori_loop(0, C, chunk, 0)

    def ga_mate(l):
        return remote(wa.at[l + 1, :, 1 - k], gar, mga_s.at[l], mga_r.at[l], mate)

    def zpart(kind, l, at):
        return wm.at[l + 1, k, at] if kind else wa.at[l + 1, :, k, at]

    def zbuf(kind, l, slot):
        return gmz.at[l, slot] if kind else gaz.at[l, slot]

    def zg_copy(kind, l, owner, device, send, recv):
        ssem, rsem = zg_s.at[2 * l + kind, send], zg_r.at[2 * l + kind, recv]
        return remote(zpart(kind, l, owner), zbuf(kind, l, recv), ssem, rsem, zdev(device))

    def z_direct(kind, l, d):
        return zg_copy(kind, l, n + d, n + d, d + N - 1, (-d) % N - 1)

    def z_beyond(kind, l, d):
        sign = 1 if d > 0 else -1
        return zg_copy(kind, l, n + d, n + d - sign * REACH, d + N - 1, N - 1 + abs(d) - REACH - 1)

    def z_spread(kind, l):
        for d in signed(1, N - 1):
            ready = inside(n + d)
            if abs(d) == REACH:
                ready = ready & jnp.logical_not(inside(n - d // REACH))

            @pl.when(ready)
            def _(d=d):
                (z_beyond if abs(d) > REACH else z_direct)(kind, l, d).start()

    def z_relay(kind, l):
        for sign in (1, -1):
            owner = n + sign * REACH

            @pl.when(inside(owner) & inside(n - sign))
            def _(sign=sign, owner=owner):
                part = zpart(kind, l, owner)
                for q in range(1, REACH):
                    @pl.when(inside(n - sign * q))
                    def _(q=q):
                        slot = N - 1 + q - 1
                        zg_copy(kind, l, n, n, 0, slot).wait_recv()
                        part[...] = (part[...].astype(F32) + zbuf(kind, l, slot)[...].astype(F32)).astype(BF)
                z_direct(kind, l, sign * REACH).start()

    def z_arrive(kind, l, add):
        for d in reversed(signed(1, REACH)):
            @pl.when(inside(n + d))
            def _(d=d):
                slot = d % N - 1
                zg_copy(kind, l, n, n, 0, slot).wait_recv()
                add(zbuf(kind, l, slot))

    def z_drain(kind, l):
        for d in signed(1, N - 1):
            @pl.when(inside(n + d))
            def _(d=d):
                (z_beyond if abs(d) > REACH else z_direct)(kind, l, d).wait_send()

    def gm_add(l, at):
        gm_mate(l, at).wait_recv()
        src = wm.at[l + 1]
        src[k, at] = (src[k, at].astype(F32) + gmr[at].astype(F32)).astype(BF)
        dist = jnp.where(at > n, at - n, n - at)
        sign = jnp.where(at > n, 1, -1)
        beyond = dist > REACH
        device = jnp.where(beyond, at - sign * REACH, at)
        slot = jnp.where(beyond, N - 2 + dist - REACH, lax.rem(n - at + N, N) - 1)

        @pl.when((dist != 0) & ((dist != REACH) | jnp.logical_not(inside(n - sign))))
        def _():
            zg_copy(1, l, at, device, at - n + N - 1, slot).start()

    def gm_all(l):
        dst = wm.at[l + 1]
        per = UNITS // US
        count = HALF // UNITS
        far = flipped(n, N - 1, N)

        def chunk(i, carry):
            core = jnp.where(i < count, 1 - k, k)
            at = flipped(far // per, lax.rem(i, count), count)
            off = pl.multiple_of(core * HALF + at * UNITS, LANES)
            up = dot_tn(dpre_s[:, pl.ds(off, UNITS)], a3[l].reshape(T, D))
            down = dot_tn(hid_s[:, pl.ds(off, UNITS)], dm[...].reshape(T, D))
            rows = pl.ds(at * per, per)
            dst[core, rows, :, 0:D] = up.astype(BF).reshape(per, US, D)
            dst[core, rows, :, D : 2 * D] = down.astype(BF).reshape(per, US, D)

            def owners(e, carry):
                owner = at * per + flipped(lax.rem(far, per), e, per)

                @pl.when(i < count)
                def _():
                    gm_mate(l, owner).start()

                @pl.when(i >= count)
                def _():
                    gm_add(l, owner)

                return carry

            lax.fori_loop(0, per, owners, 0)
            return carry

        lax.fori_loop(0, 2 * count, chunk, 0)

    def ga_spread(l):
        ga_mate(l).wait_recv()
        src = wa.at[l + 1]
        src[:, k] = (src[:, k].astype(F32) + gar[...].astype(F32)).astype(BF)
        z_spread(0, l)

    def gm_out(l):
        return local(stage, out_mlp.at[l], loc.at[2 * LAYERS + l])

    def gm_finish(l):
        stage[...] = wm[l + 1, k, n].astype(F32)

        def add(ref):
            stage[...] += ref[...].astype(F32)

        z_arrive(1, l, add)
        gm_out(l).start()
        z_drain(1, l)
        for at in range(N):
            gm_mate(l, at).wait_send()

    def xg(l, j):
        return remote(gax_s.at[j - 1], gax_r.at[l, j - 1], xg_s.at[l, j - 1], xg_r.at[l, j - 1], xy(j))

    def place(l, at, value):
        for part in range(3):
            cols = pl.ds(pl.multiple_of(part * D + at * FQ, LANES), FQ)
            held_qkv[:, cols] = value[:, part * FQ : (part + 1) * FQ]
        held_proj[:, pl.ds(pl.multiple_of(at * FQ, LANES), FQ)] = value[:, 3 * FQ : 4 * FQ]

    def ga_finish(l):
        stage_a[...] = wa[l + 1, :, k, n].astype(F32)

        def add(ref):
            stage_a[...] += ref[...].astype(F32)

        z_arrive(0, l, add)
        z_drain(0, l)
        ga_mate(l).wait_send()
        for j in range(1, C):
            gax_s[j - 1] = stage_a[chip(j)].astype(BF)
            xg(l, j).start()
        place(l, c, stage_a[c])

    def ga_out(l):
        return (
            local(held_qkv, out_qkv.at[l], fin.at[2 * l]),
            local(held_proj, out_proj.at[l], fin.at[2 * l + 1]),
        )

    def ga_place(l):
        for j in range(1, C):
            xg(l, j).wait()
            place(l, chip(j), gax_r[l, j - 1].astype(F32))
        for copy in ga_out(l):
            copy.start()

    def backward(i, carry):
        l = LAYERS - 1 - i
        p = 2 * LAYERS + 2 * i
        grad = g[...]
        nhat, rstd = normalize(mo[l])
        ag_start(p, dm, norm_back(nhat, rstd, grad, gain(l, 6)).astype(BF))
        add_norm(l, 6, grad, nhat)

        @pl.when(i == 0)
        def _():
            outh_s[...] = (mid[l] + nhat * gain(l, 6) + gain(l, 7)).astype(BF)
            out_z("start")

        ag_pass(p, dm)

        @pl.when((i == 0) & holder)
        def _():
            grad_z("sent")


        def redo(i, carry):
            pre = dot_nt(a3[l, pl.ds(2 * i, 2)].reshape(2 * TB, D), w_up(l))
            rows = pl.ds(i * 2 * TB, 2 * TB)
            pre_s[rows, :] = pre
            hid_s[rows, :] = gelu(pre).astype(BF)
            return carry

        lax.fori_loop(0, C // 2, redo, 0)

        @pl.when(i > 0)
        def _():
            z_relay(0, l + 1)


        def feed_back(i, pair):
            where = [pl.ds(b * TB, TB) for b in pair]
            pre = jnp.concatenate([pre_s[rows, :] for rows in where], axis=0)
            slope = (dot_nt(both(dm, pair), w_down(l)) * gelu_slope(pre)).astype(BF)
            for e, rows in enumerate(where):
                dpre_s[rows, :] = slope[e * TB : (e + 1) * TB]
            rs_pair(p, i, dot_nn(slope, w_up(l)))

        arrivals(p, dm, feed_back)

        @pl.when(i > 0)
        def _():
            pl.semaphore_wait(credit.at[1], 1)

        gm_all(l)

        @pl.when(l > 0)
        def _():
            pl.semaphore_signal(credit.at[1], inc=1, device_id=mate, device_id_type=MESH)

        d_a3 = rs_finish(p)
        nhat, rstd = normalize(mid[l])
        d_mid = g[...] + norm_back(nhat, rstd, d_a3, gain(l, 4))
        g[...] = d_mid
        nhat_b, rstd_b = normalize(br[l])
        ag_start(p + 1, db, norm_back(nhat_b, rstd_b, d_mid, gain(l, 2)).astype(BF))
        add_norm(l, 4, d_a3, nhat)
        add_norm(l, 2, d_mid, nhat_b)
        ag_drain(p, dm)
        for b in range(C):
            weights, inverse = exp_scores(l, b)
            cols = pl.ds(TB * (b * (b + 1) // 2), (b + 1) * TB)
            p_s[:, cols] = (weights * inverse).astype(BF)
        dk_s[...] = jnp.zeros_like(dk_s)
        dv_s[...] = jnp.zeros_like(dv_s)
        ag_pass(p + 1, db)
        for j in range(1, C):
            ag_wait(p + 1, db, j)
        for b in reversed(range(C)):
            size = (b + 1) * TB
            rows = pl.ds(b * TB, TB)
            seen = pl.ds(0, size)
            d_att = by_head(dot_nn(db[b], w_proj(l)).astype(BF))
            d_probs = dot_nt(d_att, vs_[l, 0 : b + 1].reshape(size, FQ))
            low = p_s[:, pl.ds(TB * (b * (b + 1) // 2), size)]
            probs = low.astype(F32)
            delta = jnp.sum(probs * d_probs, axis=-1, keepdims=True)
            d_scores = (probs * (d_probs - delta)).astype(BF)
            d_query = of_heads(dot_nn(d_scores, ks_[l, 0 : b + 1].reshape(size, FQ)))
            d_query = d_query * HEAD_DIM ** (-0.5)
            dk_s[seen, :] += dot_tn(d_scores, by_head(qs_[l, b]))
            dv_s[seen, :] += dot_tn(low, d_att)
            d_key = dk_s[rows, :]
            cosine, sine = tables(b)
            dqkv[rows, 0:FQ] = (d_query * cosine - swapped(d_query) * sine).astype(BF)
            dqkv[rows, FQ : 2 * FQ] = (d_key * cosine - swapped(d_key) * sine).astype(BF)
            dqkv[rows, 2 * FQ : 3 * FQ] = dv_s[rows, :].astype(BF)
            rs_block(p + 1, b, dot_nt(dqkv[rows, :], w_qkv(l)))
        z_relay(1, l)

        @pl.when(i > 0)
        def _():
            pl.semaphore_wait(credit.at[0], 1)

        ga_all(l)
        ga_mate(l).start()

        @pl.when(i > 0)
        def _():
            gm_finish(l + 1)
            ga_finish(l + 1)

        ga_spread(l)

        @pl.when(l > 0)
        def _():
            pl.semaphore_signal(credit.at[0], inc=1, device_id=mate, device_id_type=MESH)

        d_a1 = rs_finish(p + 1)
        nhat, rstd = normalize(st[l])
        g[...] = g[...] + norm_back(nhat, rstd, d_a1, gain(l, 0))
        add_norm(l, 0, d_a1, nhat)
        ag_drain(p + 1, db)

        @pl.when(i == 0)
        def _():
            for kind in range(2):
                for at in range(LAYERS):
                    w_drain(kind, at)
            perm(0, "sent")
            grad_plane("sent")


        return carry

    lax.fori_loop(0, LAYERS, backward, 0)

    @pl.when(holder)
    def _():
        out_held()
        out_plane("start")

    g_p[...] = g[...].astype(BF)
    n_start(1, "m", ngrad[...])
    n_start(1, "x", n_finish(1, "m"))
    z_relay(0, 0)
    n_start(1, "z", n_finish(1, "x"))
    ga_place(1)
    gm_out(1).wait()
    perm(1, "start")
    gm_finish(0)
    for copy in ga_out(1):
        copy.wait()
    ga_finish(0)
    total = n_finish(1, "z")
    for l in range(LAYERS):
        out_n[l] = lax.dot_general(
            total[l * 8 : (l + 1) * 8], spot, (((1,), (1,)), ((), ())),
            preferred_element_type=F32, precision=lax.Precision.HIGHEST,
        )
    ga_place(0)
    gm_out(0).wait()

    for l in range(LAYERS):
        for j in range(1, C):
            a2a_all(l, j).wait_send()
    perm(1, "here")
    g[...] = hid_p[...].astype(F32)
    grad_out = local(g, out_g, fin.at[2 * LAYERS])
    grad_out.start()
    perm(1, "sent")
    out_z("sent")
    out_here()

    @pl.when(holder)
    def _():
        out_plane("sent")

    for copy in ga_out(0):
        copy.wait()
    grad_out.wait()


def copy_out(*refs):
    count = (len(refs) - 1) // 3
    sems = refs[-1]
    into, out = [], []
    for i in range(count):
        src, dst, held = refs[i], refs[count + i], refs[2 * count + i]
        cuts = [()]
        if len(held.shape) == 3:
            half = held.shape[1] // 2 if held.shape[1] >= 128 else held.shape[1]
            cuts = [(l, pl.ds(at, half)) for l in range(held.shape[0]) for at in range(0, held.shape[1], half)]
        for at in cuts:
            one, two, three = (ref.at[at] if at else ref for ref in (src, held, dst))
            into.append(pltpu.make_async_copy(one, two, sems.at[2 * len(into)]))
            out.append(pltpu.make_async_copy(two, three, sems.at[2 * len(out) + 1]))
    for copy in into:
        copy.start()
    for first, second in zip(into, out):
        first.wait()
        second.start()
    for copy in out:
        copy.wait()


def body(mesh, hidden_in, w_qkv, w_proj, w_mlp, norm_params, grad_output, corpus_id, corpus_weight):
    W, N = mesh.shape["wide"], mesh.shape["narrow"]
    C = W // 2
    TB, D = hidden_in.shape
    FQ, UQ, RW, US = D // C, FF // C, D // (W * N), FF // (W * N)
    AW = 4 * FQ
    T = C * TB
    REACH = N // 2
    assert C == N and w_mlp.shape[1] == US and w_qkv.shape[1] == RW

    half = HEAD_DIM // 2
    freqs = np.float32(ROPE_BASE) ** (-np.arange(half, dtype=np.float32) / np.float32(half))
    angles = (np.arange(T, dtype=np.float32)[:, None] * freqs[None, :]).astype(np.float32)
    cosine = np.tile(np.cos(angles), (1, LANES // half)).astype(np.float32)
    sine = np.sin(angles)
    sine = np.tile(np.concatenate([-sine, sine], axis=1), (1, LANES // HEAD_DIM)).astype(np.float32)

    NR = LAYERS * 8
    dma = pltpu.SemaphoreType.DMA
    vm = pltpu.VMEM
    L = LAYERS
    scratch = [
        vm((T, LANES), F32),
        vm((T, LANES), F32),
        vm((RW, 3 * D), F32),
        vm((RW, D), F32),
        vm((L + 1, C, 2, N, RW, AW), BF),
        vm((L + 1, 2, N, US, 2 * D), BF),
        vm((L, C, TB, D), BF),
        vm((L, C, TB, D), BF),
        vm((C, TB, D), BF),
        vm((C, TB, D), BF),
        vm((L, C, TB, FQ), BF),
        vm((L, C, TB, FQ), BF),
        vm((L, C, TB, FQ), BF),
        vm((L, C, TB, FQ), BF),
        vm((L, TB, D), F32),
        vm((L, TB, D), F32),
        vm((L, TB, D), F32),
        vm((L, TB, D), F32),
        vm((T, UQ), F32),
        vm((T, UQ), BF),
        vm((T, UQ), BF),
        vm((FQ // HEAD_DIM * TB, TB * C * (C + 1) // 2), BF),
        vm((T, FQ), F32),
        vm((T, FQ), F32),
        vm((T, 3 * FQ), BF),
        vm((C - 1, TB, D), BF),
        vm((C - 1, TB, D), BF),
        vm((2, TB // 2, D), BF),
        vm((TB, D), F32),
        vm((TB, D), BF),
        vm((TB, D), BF),
        vm((8, TB), F32),
        vm((C, 8, TB), F32),
        vm((8, TB), F32),
        vm((TB, D), BF),
        vm((N, TB, D), BF),
        vm((TB, D), F32),
        vm((N, US, 2 * D), BF),
        vm((L, N + REACH - 2, US, 2 * D), BF),
        vm((US, 2 * D), F32),
        vm((C, RW, AW), F32),
        vm((C, N, RW, AW), BF),
        vm((L, N + REACH - 2, C, RW, AW), BF),
        vm((C - 1, RW, AW), BF),
        vm((L, C - 1, RW, AW), BF),
        vm((NR, D), F32),
        vm((NR, D), F32),
        vm((3, NR, D), BF),
        vm((3, C - 1, NR, D), BF),
        vm((3, NR, D), F32),
        vm((3, C - 1, NR, D), F32),
        dma((2,)), dma((2,)),
        dma((2,)), dma((2, C)),
        dma((2, C)), dma((2,)),
        dma((1,)), dma((N,)),
        dma((N,)), dma((1,)),
        dma((3 * L,)),
        dma((L, C - 1)), dma((L, C - 1)),
        dma((2, max(C - 1, 6))), dma((2, max(C - 1, 6))),
        dma((2, max(C - 1, 6))), dma((2, max(C - 1, 6))),
        dma((2 * L, 4 * REACH)), dma((2 * L, N)),
        dma((2 * L, N)), dma((2 * L, N)),
        dma((2 * L, 2 * N - 1)), dma((2 * L, N + REACH - 2)),
        dma((L,)), dma((L,)),
        dma((L, N)), dma((L, N)),
        dma((L, C - 1)), dma((L, C - 1)),
        dma((2, C - 1)), dma((2, C - 1)),
        dma((2, N - 1)), dma((2, N - 1)),
        dma((2,)), dma((2,)),
        dma((2 * L + 3,)),
        pltpu.SemaphoreType.REGULAR((2,)),
    ]
    vspec = pl.BlockSpec(memory_space=pltpu.VMEM)
    anyspec = pl.BlockSpec(memory_space=pl.ANY)
    shapes = (
        jax.ShapeDtypeStruct((TB, D), BF),
        jax.ShapeDtypeStruct((TB, D), F32),
        jax.ShapeDtypeStruct((L, RW, 3 * D), F32),
        jax.ShapeDtypeStruct((L, RW, D), F32),
        jax.ShapeDtypeStruct((L, US, 2 * D), F32),
        jax.ShapeDtypeStruct((L, 8, RW), F32),
    )
    outs = pl.pallas_call(
        partial(kernel_body, (C, N, TB, D, FQ, UQ, RW, US, AW)),
        out_shape=shapes,
        in_specs=[anyspec] * 2 + [vspec] * 3 + [anyspec] * 5,
        out_specs=(anyspec,) * 5 + (vspec,),
        scratch_shapes=scratch,
        compiler_params=pltpu.CompilerParams(
            collective_id=0, has_side_effects=True, vmem_limit_bytes=127 << 19
        ),
    )(
        hidden_in, grad_output, corpus_id.reshape(1, TB), corpus_weight.reshape(1, -1), norm_params.transpose(0, 2, 1),
        jnp.asarray(cosine), jnp.asarray(sine), w_qkv, w_proj, w_mlp,
    )
    outs = pl.pallas_call(
        copy_out,
        out_shape=shapes,
        in_specs=[anyspec] * len(shapes),
        out_specs=(anyspec,) * len(shapes),
        scratch_shapes=[vm(one.shape, one.dtype) for one in shapes] + [dma((4 * len(shapes),))],
        compiler_params=pltpu.CompilerParams(vmem_limit_bytes=60 << 20),
    )(*outs)
    return (*outs[:5], outs[5].transpose(0, 2, 1))


def solution(mesh):
    rows = P(("wide", "narrow"), None)
    layered = P(None, ("wide", "narrow"), None)
    return jax.shard_map(
        partial(body, mesh),
        mesh=mesh,
        in_specs=(rows, layered, layered, layered, layered, rows, P(("wide", "narrow")), P()),
        out_specs=(rows, rows, layered, layered, layered, layered),
        check_vma=False,
    )
```

```python
from functools import partial

import jax
import jax.numpy as jnp
import numpy as np
from jax import lax
from jax.experimental import pallas as pl
from jax.experimental.pallas import tpu as pltpu
from jax.sharding import PartitionSpec as P

HEADS = 16
HEAD_DIM = 64
FF = 4096
LAYERS = 2
EPS = 1e-05
MASKED = -1e30
ROPE_BASE = 10000.0
MESH = pl.DeviceIdType.MESH
BF = jnp.bfloat16
F32 = jnp.float32
LANES = 128
UNITS = 256


def dot_nn(left, right):
    return lax.dot_general(left, right, (((1,), (0,)), ((), ())), preferred_element_type=F32)


def dot_nt(left, right):
    return lax.dot_general(left, right, (((1,), (1,)), ((), ())), preferred_element_type=F32)


def dot_tn(left, right):
    return lax.dot_general(left, right, (((0,), (0,)), ((), ())), preferred_element_type=F32)


def normalize(inputs):
    centre = jnp.mean(inputs, axis=-1, keepdims=True)
    centered = inputs - centre
    rstd = lax.rsqrt(jnp.mean(centered * centered, axis=-1, keepdims=True) + EPS)
    return centered * rstd, rstd


def norm_back(nhat, rstd, grad, gain):
    scaled = grad * gain
    mean_f = jnp.mean(scaled, axis=-1, keepdims=True)
    mean_fn = jnp.mean(scaled * nhat, axis=-1, keepdims=True)
    return rstd * (scaled - mean_f - nhat * mean_fn)


GELU_S = 0.7978845608028654
GELU_A = 0.044715


def gelu(pre):
    return 0.5 * pre * (1.0 + jnp.tanh(GELU_S * (pre + GELU_A * pre * pre * pre)))


def gelu_slope(pre):
    square = pre * pre
    turned = jnp.tanh(GELU_S * (pre + GELU_A * pre * square))
    inner = GELU_S * (1.0 + 3.0 * GELU_A * square)
    return 0.5 * (1.0 + turned) + 0.5 * pre * (1.0 - turned * turned) * inner


def kernel_body(
    dims,
    hid_ref, gout_ref, ids_ref, cw_ref, nrm_ref, cos_in, sin_in, wq_ref, wp_ref, wm_ref,
    out_h, out_g, out_qkv, out_proj, out_mlp, out_n,
    cos_ref, sin_ref, held_qkv, held_proj,
    wa, wm, a1, a3, dm, db, qs_, ks_, vs_, att, st, br, mid, mo,
    pre_s, hid_s, dpre_s, p_s, dk_s, dv_s, dqkv,
    rs_send, rs_recv, rs_mid, acc, hid_p, g_p, sc_own, sc_x, sc_p, outh_s, hx, g,
    gmr, gmz, stage, stage_a, gar, gaz, gax_s, gax_r,
    npar, ngrad, nf_send, nf_recv, nb_send, nb_recv,
    perm_s, perm_r, gp_s, gp_r, gz_s, gz_r, oz_s, oz_r, op_s, op_r, loc, a2a_s, a2a_r, ag_s, ag_r, rs_s, rs_r,
    zw_s, zw_r, mw_s, mw_r, zg_s, zg_r, mga_s, mga_r, mgm_s, mgm_r, xg_s, xg_r,
    nx_s, nx_r, nz_s, nz_r, nm_s, nm_r, fin, credit,
):
    C, N, TB, D, FQ, UQ, RW, US, AW = dims
    T = C * TB
    HPC = FQ // HEAD_DIM
    HALF = N * US
    REACH = N // 2
    w = lax.axis_index("wide")
    n = lax.axis_index("narrow")
    c = w // 2
    k = lax.rem(w, 2)
    mate = (2 * c + (1 - k), n)
    to_chip = n + k * (N - 1 - 2 * n)
    to_plane = c + k * (N - 1 - 2 * c)
    swap = (2 * to_chip + k, to_plane)
    moves = to_chip != c

    def block(at):
        return at + k * (C - 1 - 2 * at)

    mine = block(c)

    def flipped(base, j, count):
        out, bit = 0, 1
        while bit < count:
            ours = lax.rem(base // bit, 2)
            flip = (j // bit) % 2 if isinstance(j, int) else lax.rem(j // bit, 2)
            out = out + bit * (ours + flip - 2 * ours * flip)
            bit *= 2
        return out

    def chip(j):
        return flipped(c, j, C)

    def xy(j):
        return (2 * chip(j) + k, n)

    def zdev(at):
        return (w, at)

    def remote(src, dst, ssem, rsem, device):
        return pltpu.make_async_remote_copy(
            src_ref=src, dst_ref=dst, send_sem=ssem, recv_sem=rsem,
            device_id=device, device_id_type=MESH,
        )

    def local(src, dst, sem):
        return pltpu.make_async_copy(src, dst, sem)

    barrier = pltpu.get_barrier_semaphore()
    partners = [xy(j) for j in range(1, C)] + [mate]
    partners += [zdev(lax.rem(n + j, N)) for j in range(1, N)]
    for device in partners:
        pl.semaphore_signal(barrier, inc=1, device_id=device, device_id_type=MESH)

    @pl.when(moves)
    def _():
        pl.semaphore_signal(barrier, inc=1, device_id=swap, device_id_type=MESH)

    pl.semaphore_wait(barrier, len(partners) + jnp.where(moves, 1, 0))

    rope = (
        local(cos_in, cos_ref, fin.at[2 * LAYERS + 1]), local(sin_in, sin_ref, fin.at[2 * LAYERS + 2])
    )
    for copy in rope:
        copy.start()

    def either(far, src, dst, ssem, rsem, device, act):
        @pl.when(far)
        def _():
            getattr(remote(src, dst, ssem, rsem, device), {"here": "wait_recv", "sent": "wait_send"}.get(act, act))()

        if act != "sent":
            @pl.when(jnp.logical_not(far))
            def _():
                getattr(local(src, dst, rsem), {"here": "wait"}.get(act, act))()

    def perm(i, act):
        src, dst = ((hid_ref, hid_p), (g_p, hid_p))[i]
        either(moves, src, dst, perm_s.at[i], perm_r.at[i], swap, act)

    holder = c == to_chip

    def grad_plane(act):
        for e, (src, dst) in enumerate(((gout_ref, db.at[c]), (sc_own, sc_x.at[c]))):
            either(jnp.logical_not(holder), src, dst, gp_s.at[e], gp_r.at[e, c], (2 * to_chip + k, n), act)

    def grad_held():
        for at in range(C):
            for e, dst in enumerate((db.at[at], sc_x.at[at])):
                either(c != at, dst, dst, gp_s.at[e], gp_r.at[e, at], (2 * at + k, n), "here")

    def grad_z(act):
        for at in range(C):
            plane = at + k * (N - 1 - 2 * at)
            for e, (src, dst) in enumerate(((db.at[at], g_p), (sc_x.at[at], sc_p))):
                either(plane != n, src, dst, gz_s.at[e, at], gz_r.at[e], (w, plane), act)

    def grad_here():
        for e, dst in enumerate((g_p, sc_p)):
            either(to_plane != n, dst, dst, gz_s.at[e, 0], gz_r.at[e], (w, to_plane), "here")

    def out_z(act):
        either(to_plane != n, outh_s, hx.at[n], oz_s.at[0], oz_r.at[n], (w, to_plane), act)

    def out_held():
        for at in range(N):
            either(n != at, hx.at[at], hx.at[at], oz_s.at[0], oz_r.at[at], (w, at), "here")

    def out_plane(act):
        for at in range(N):
            dest = at + k * (N - 1 - 2 * at)
            either(dest != c, hx.at[at], out_h, op_s.at[at], op_r.at[0], (2 * dest + k, n), act)

    def out_here():
        either(jnp.logical_not(holder), hx.at[0], out_h, op_s.at[0], op_r.at[0], (2 * to_chip + k, n), "here")

    perm(0, "start")

    def n_copy(way, axis, j):
        send, heard = (nf_send, nf_recv) if way == 0 else (nb_send, nb_recv)
        slot = n_slot[axis]
        if axis == "x":
            return remote(send.at[slot], heard.at[slot, j - 1], nx_s.at[way, j - 1], nx_r.at[way, j - 1], xy(j))
        if axis == "z":
            there = zdev(lax.rem(n + j, N))
            return remote(send.at[slot], heard.at[slot, j - 1], nz_s.at[way, j - 1], nz_r.at[way, j - 1], there)
        return remote(send.at[slot], heard.at[slot, j - 1], nm_s.at[way], nm_r.at[way], mate)

    n_count = {"x": C, "z": N, "m": 2}
    n_slot = {"x": 0, "z": 1, "m": 2}

    def n_start(way, axis, value):
        send = nf_send if way == 0 else nb_send
        send[n_slot[axis]] = value.astype(send.dtype)
        for j in range(1, n_count[axis]):
            n_copy(way, axis, j).start()

    def n_finish(way, axis):
        send, heard = (nf_send, nf_recv) if way == 0 else (nb_send, nb_recv)
        total = send[n_slot[axis]].astype(F32)
        for j in range(1, n_count[axis]):
            n_copy(way, axis, j).wait()
            total = total + heard[n_slot[axis], j - 1].astype(F32)
        return total

    first = (w * N + n) * RW
    spot = lax.broadcasted_iota(jnp.int32, (RW, D), 1) == (
        lax.broadcasted_iota(jnp.int32, (RW, D), 0) + first
    )
    spot = spot.astype(F32)
    n_start(0, "x", jnp.concatenate(
        [dot_nn(nrm_ref[l], spot.astype(BF)) for l in range(LAYERS)], axis=0
    ))

    def pieces(l, at):
        for part in range(3):
            cols = pl.ds(pl.multiple_of(part * D + at * FQ, LANES), FQ)
            yield wq_ref.at[l, :, cols], wa.at[l, c, k, n, :, pl.ds(part * FQ, FQ)]
        cols = pl.ds(pl.multiple_of(at * FQ, LANES), FQ)
        yield wp_ref.at[l, :, cols], wa.at[l, c, k, n, :, pl.ds(3 * FQ, FQ)]

    def a2a_start(l):
        for j in range(1, C):
            for src, dst in pieces(l, chip(j)):
                remote(src, dst, a2a_s.at[l, j - 1], a2a_r.at[l, j - 1], xy(j)).start()

    def a2a_all(l, j):
        there = wa.at[l, chip(j), k, n]
        return remote(there, there, a2a_s.at[l, j - 1], a2a_r.at[l, j - 1], xy(j))

    def own_wa(l):
        mine = wa.at[l, c, k, n]
        return local(mine, mine, loc.at[l])

    def own_wm(l):
        return local(wm_ref.at[l], wm.at[l, k, n], loc.at[LAYERS + l])

    a2a_start(0)
    for l in range(LAYERS):
        for src, dst in pieces(l, c):
            local(src, dst, loc.at[l]).start()
        own_wm(l).start()

    def shard(kind, l, core, at):
        return wm.at[l, core, at] if kind else wa.at[l, :, core, at]

    def inside(at):
        return (at >= 0) & (at < N)

    def signed(least, most):
        return [sign * d for d in range(most, least - 1, -1) for sign in (1, -1)]

    def zw_copy(kind, l, origin, at, slot):
        rows = shard(kind, l, k, origin)
        return remote(rows, rows, zw_s.at[2 * l + kind, slot], zw_r.at[2 * l + kind, origin], zdev(at))

    def direct_slot(d):
        return d + REACH

    def relay_slot(sign, q):
        return 2 * REACH + (q if sign > 0 else q + REACH - 1)

    def to_mate(kind, l, at, core=k):
        rows = shard(kind, l, core, at)
        return remote(rows, rows, mw_s.at[2 * l + kind, at], mw_r.at[2 * l + kind, at], mate)

    def w_send(kind, l):
        for d in signed(1, REACH):
            @pl.when(inside(n + d))
            def _(d=d):
                zw_copy(kind, l, n, n + d, direct_slot(d)).start()

        to_mate(kind, l, n).start()

    def w_relay(kind, l):
        for sign in (1, -1):
            origin = n - sign * REACH

            @pl.when(inside(origin) & inside(n + sign))
            def _(sign=sign, origin=origin):
                zw_copy(kind, l, origin, n, 0).wait_recv()
                for q in range(1, REACH):
                    @pl.when(inside(n + sign * q))
                    def _(q=q):
                        zw_copy(kind, l, origin, n + sign * q, relay_slot(sign, q)).start()

    def w_arrive(kind, l):
        for d in reversed(signed(1, N - 1)):
            origin = n + d

            @pl.when(inside(origin))
            def _(d=d, origin=origin):
                if abs(d) == REACH:
                    sign = -1 if d > 0 else 1

                    @pl.when(jnp.logical_not(inside(n + sign)))
                    def _():
                        zw_copy(kind, l, origin, n, 0).wait_recv()
                else:
                    zw_copy(kind, l, origin, n, 0).wait_recv()
                to_mate(kind, l, origin).start()

    def w_ready(kind, l):
        for at in range(N):
            to_mate(kind, l, at, 1 - k).wait_recv()

    def w_drain(kind, l):
        for d in signed(1, REACH):
            @pl.when(inside(n + d))
            def _(d=d):
                zw_copy(kind, l, n, n + d, direct_slot(d)).wait_send()

        for sign in (1, -1):
            origin = n - sign * REACH
            for q in range(1, REACH):
                @pl.when(inside(origin) & inside(n + sign) & inside(n + sign * q))
                def _(sign=sign, origin=origin, q=q):
                    zw_copy(kind, l, origin, n + sign * q, relay_slot(sign, q)).wait_send()

        for at in range(N):
            to_mate(kind, l, at).wait_send()

    n_start(0, "z", n_finish(0, "x"))
    own_wa(0).wait()
    for j in range(1, C):
        a2a_all(0, j).wait_recv()
    w_send(0, 0)
    n_start(0, "m", n_finish(0, "z"))
    npar[...] = n_finish(0, "m")
    ngrad[...] = jnp.zeros_like(ngrad)

    def gain(l, col):
        return npar[pl.ds(l * 8 + col, 1), :]

    SPLIT = C == 4
    hops = ((1, 0), (1, 1), (2, 1), (2, 0), (2, 0), (1, 1))

    def ag_copy(p, buf, source, slot):
        if not SPLIT:
            rows = buf.at[block(source)]
            return remote(rows, rows, ag_s.at[lax.rem(p, 2), slot], ag_r.at[lax.rem(p, 2), slot], xy(slot + 1))
        j, part = hops[slot]
        rows = buf.at[block(source), pl.ds(part * (TB // 2), TB // 2)]
        return remote(rows, rows, ag_s.at[lax.rem(p, 2), slot], ag_r.at[lax.rem(p, 2), slot], xy(j))

    def ag_start(p, buf, value):
        buf[mine] = value
        for slot in (0, 2, 1, 3) if SPLIT else range(C - 1):
            ag_copy(p, buf, c, slot).start()

    def ag_pass(p, buf):
        if SPLIT:
            ag_copy(p, buf, chip(1), 0).wait_recv()
            ag_copy(p, buf, chip(1), 4).start()
            ag_copy(p, buf, chip(2), 2).wait_recv()
            ag_copy(p, buf, chip(2), 5).start()

    def ag_wait(p, buf, j):
        for slot in ((), (1,), (3,), (4, 5))[j] if SPLIT else (j - 1,) * min(j, 1):
            ag_copy(p, buf, chip(j), slot).wait_recv()

    def ag_drain(p, buf):
        for slot in range(4) if SPLIT else range(C - 1):
            ag_copy(p, buf, c, slot).wait_send()
        if SPLIT:
            ag_copy(p, buf, chip(1), 4).wait_send()
            ag_copy(p, buf, chip(2), 5).wait_send()

    def rs_copy(p, j):
        return remote(rs_send.at[j - 1], rs_recv.at[j - 1], rs_s.at[lax.rem(p, 2), j - 1], rs_r.at[lax.rem(p, 2), j - 1], xy(j))

    def rs_put(p, j, value):
        @pl.when(j > 0)
        def _():
            rs_send[j - 1] = value.astype(BF)
            rs_copy(p, j).start()

        @pl.when(j == 0)
        def _():
            acc[...] = value

    def rs_block(p, b, value):
        rs_put(p, chip(block(b)), value)

    def rs_pair(p, i, value):
        rs_put(p, 2 * i, value[0:TB])
        rs_send[2 * i] = value[TB:].astype(BF)
        rs_copy(p, 2 * i + 1).start()

    def half_copy(p, slot):
        part = pl.ds((0, 1, 1, 0, 0, 1)[slot] * (TB // 2), TB // 2)
        src = rs_send.at[(0, 0, 1, 1, 2, 2)[slot], part]
        dst = rs_mid.at[slot - 4] if slot >= 4 else rs_recv.at[(0, 0, 1, 1)[slot], part]
        return remote(src, dst, rs_s.at[lax.rem(p, 2), slot], rs_r.at[lax.rem(p, 2), slot], xy((1, 1, 2, 2, 1, 2)[slot]))

    def half_put(p, i, value):
        @pl.when(i == 0)
        def _():
            rs_send[2] = value.astype(BF)
            half_copy(p, 4).start()
            half_copy(p, 5).start()

        @pl.when(i == 1)
        def _():
            rs_send[0] = value.astype(BF)
            half_copy(p, 0).start()

        @pl.when(i == 2)
        def _():
            rs_send[1] = value.astype(BF)
            half_copy(p, 2).start()

        @pl.when(i == 3)
        def _():
            acc[...] = value

    def half_chip(i):
        return chip(jnp.where(i == 0, 3, jnp.where(i == 3, 0, i)))

    def half_pass(p):
        for slot, at, rows, onward in ((4, 1, pl.ds(0, TB // 2), 3), (5, 0, pl.ds(TB // 2, TB // 2), 1)):
            half_copy(p, slot).wait_recv()
            rs_send[at, rows] = (rs_send[at, rows].astype(F32) + rs_mid[slot - 4].astype(F32)).astype(BF)
            half_copy(p, onward).start()

    def rs_halves_finish(p):
        for slot in range(4):
            half_copy(p, slot).wait()
        half_copy(p, 4).wait_send()
        half_copy(p, 5).wait_send()
        return acc[...] + rs_recv[0].astype(F32) + rs_recv[1].astype(F32)

    def arrivals(p, buf, use):
        def step(i, carry):
            for at in range(C // 2):
                @pl.when(i == at)
                def _(at=at):
                    ag_wait(p, buf, 2 * at)
                    ag_wait(p, buf, 2 * at + 1)

            use(i, (block(chip(2 * i)), block(chip(2 * i + 1))))
            return carry

        lax.fori_loop(0, C // 2, step, 0)

    def both(ref, pair):
        return jnp.concatenate([ref[b] for b in pair], axis=0)

    def rs_finish(p):
        total = acc[...]
        for j in range(1, C):
            rs_copy(p, j).wait()
            total = total + rs_recv[j - 1].astype(F32)
        return total

    lane = lax.broadcasted_iota(jnp.int32, (TB, FQ), 1)
    low_half = lax.rem(lane, HEAD_DIM) < HEAD_DIM // 2
    head_of = lane // HEAD_DIM
    causal = lax.broadcasted_iota(jnp.int32, (HPC * TB, TB), 1) <= lax.rem(
        lax.broadcasted_iota(jnp.int32, (HPC * TB, TB), 0), TB
    )

    def tables(b):
        rows = pl.ds(b * TB, TB)
        reps = FQ // LANES
        return (
            jnp.concatenate([cos_ref[rows, :]] * reps, axis=1),
            jnp.concatenate([sin_ref[rows, :]] * reps, axis=1),
        )

    def swapped(u):
        half_dim = HEAD_DIM // 2
        return jnp.where(
            low_half, pltpu.roll(u, FQ - half_dim, 1), pltpu.roll(u, half_dim, 1)
        )

    def w_qkv(l):
        return wa[l, :, :, :, :, 0 : 3 * FQ].reshape(D, 3 * FQ)

    def w_proj(l):
        return wa[l, :, :, :, :, 3 * FQ : 4 * FQ].reshape(D, FQ)

    def w_up(l):
        return wm[l, :, :, :, 0:D].reshape(UQ, D)

    def w_down(l):
        return wm[l, :, :, :, D : 2 * D].reshape(UQ, D)

    def by_head(rows):
        return jnp.concatenate(
            [jnp.where(head_of == h, rows, jnp.zeros((), rows.dtype)) for h in range(HPC)], axis=0
        )

    def of_heads(stacked):
        out = stacked[0:TB]
        for h in range(1, HPC):
            out = jnp.where(head_of == h, stacked[h * TB : (h + 1) * TB], out)
        return out

    def exp_scores(l, b):
        scores = dot_nt(by_head(qs_[l, b]), ks_[l, 0 : b + 1].reshape((b + 1) * TB, FQ))
        last = jnp.where(causal, scores[:, b * TB :], MASKED)
        scores = jnp.concatenate([scores[:, : b * TB], last], axis=1) if b else last
        weights = jnp.exp(scores - jnp.max(scores, axis=-1, keepdims=True))
        return weights, 1.0 / jnp.sum(weights, axis=-1, keepdims=True)

    w_relay(0, 0)
    own_wm(0).wait()
    w_send(1, 0)
    perm(0, "here")
    st[0] = hid_p[...].astype(F32)
    ids = jnp.broadcast_to(ids_ref[...], (8, TB))
    scale = jnp.zeros((8, TB), F32)
    for i in range(cw_ref.shape[1]):
        scale = jnp.where(ids == i, cw_ref[:, i : i + 1], scale)
    sc_own[...] = scale
    for copy in rope:
        copy.wait()

    def grad_move():
        @pl.when(holder)
        def _():
            grad_held()
            grad_z("start")

    def forward(l, carry):
        p = 2 * l
        more = l + 1 < LAYERS
        nhat, unused = normalize(st[l])
        ag_start(p, a1.at[l], (nhat * gain(l, 0) + gain(l, 1)).astype(BF))

        @pl.when(l == 0)
        def _():
            a2a_start(1)

        ag_pass(p, a1.at[l])

        @pl.when(l == 0)
        def _():
            grad_plane("start")

        w_arrive(0, l)
        w_ready(0, l)

        def qkv_step(i, pair):
            u = dot_nn(both(a1.at[l], pair), w_qkv(l))
            for e, b in enumerate(pair):
                cosine, sine = tables(b)
                uq = u[e * TB : (e + 1) * TB, 0:FQ]
                uk = u[e * TB : (e + 1) * TB, FQ : 2 * FQ]
                uq = (uq * cosine + swapped(uq) * sine).astype(BF)
                qs_[l, b] = (uq * HEAD_DIM ** (-0.5)).astype(BF)
                ks_[l, b] = (uk * cosine + swapped(uk) * sine).astype(BF)
                vs_[l, b] = u[e * TB : (e + 1) * TB, 2 * FQ :].astype(BF)

        arrivals(p, a1.at[l], qkv_step)
        def attend(b):
            weights, inverse = exp_scores(l, b)
            mixed = dot_nn(weights.astype(BF), vs_[l, 0 : b + 1].reshape((b + 1) * TB, FQ))
            low = of_heads(mixed * inverse).astype(BF)
            att[l, b] = low
            return dot_nt(low, w_proj(l))

        if SPLIT:

            def attend_step(i, carry):
                for b in range(C):
                    @pl.when(block(half_chip(i)) == b)
                    def _(b=b):
                        acc[...] = attend(b)

                half_put(p, i, acc[...])
                return carry

            lax.fori_loop(0, C, attend_step, 0)
            half_pass(p)
        else:
            for b in range(C):
                rs_block(p, b, attend(b))
        w_relay(1, l)

        @pl.when(more)
        def _():
            own_wa(l + 1).wait()
            for j in range(1, C):
                a2a_all(l + 1, j).wait_recv()
            w_send(0, l + 1)

        branch = (rs_halves_finish if SPLIT else rs_finish)(p)
        br[l] = branch
        nhat, unused = normalize(branch)
        middle = st[l] + nhat * gain(l, 2) + gain(l, 3)
        mid[l] = middle
        nhat, unused = normalize(middle)
        ag_start(p + 1, a3.at[l], (nhat * gain(l, 4) + gain(l, 5)).astype(BF))
        ag_drain(p, a1.at[l])
        ag_pass(p + 1, a3.at[l])
        w_arrive(1, l)


        def feed(x, core):
            up = wm[l, core, :, :, 0:D].reshape(N * US, D)
            down = wm[l, core, :, :, D : 2 * D].reshape(N * US, D)
            return dot_nn(gelu(dot_nt(x, up)).astype(BF), down)

        if SPLIT:
            for j in range(1, C):
                ag_wait(p + 1, a3.at[l], j)
            pre_s[...] = feed(a3[l].reshape(T, D), k)
            w_ready(1, l)

            def feed_step(i, carry):
                pair = (block(half_chip(2 * i)), block(half_chip(2 * i + 1)))
                value = feed(both(a3.at[l], pair), 1 - k)
                value = value + jnp.concatenate([pre_s[pl.ds(b * TB, TB), :] for b in pair], axis=0)
                half_put(p + 1, 2 * i, value[0:TB])
                half_put(p + 1, 2 * i + 1, value[TB:])
                return carry

            lax.fori_loop(0, 2, feed_step, 0)

            @pl.when(jnp.logical_not(more))
            def _():
                grad_move()

            half_pass(p + 1)
        else:
            @pl.when(jnp.logical_not(more))
            def _():
                grad_move()

            w_ready(1, l)
            arrivals(p + 1, a3.at[l], lambda i, pair: rs_pair(
                p + 1, i, feed(both(a3.at[l], pair), k) + feed(both(a3.at[l], pair), 1 - k)
            ))

        @pl.when(more)
        def _():
            w_relay(0, l + 1)
            own_wm(l + 1).wait()
            w_send(1, l + 1)

        mlp_out = (rs_halves_finish if SPLIT else rs_finish)(p + 1)
        mo[l] = mlp_out

        @pl.when(more)
        def _():
            nhat, unused = normalize(mlp_out)
            st[l + 1] = mid[l] + nhat * gain(l, 6) + gain(l, 7)

        ag_drain(p + 1, a3.at[l])
        return carry

    lax.fori_loop(0, LAYERS, forward, 0)
    grad_here()
    here = lax.broadcasted_iota(jnp.int32, (TB, TB), 0) == lax.broadcasted_iota(jnp.int32, (TB, TB), 1)
    column = jnp.sum(
        jnp.where(here, jnp.broadcast_to(sc_p[0:1, :], (TB, TB)), 0.0), axis=1, keepdims=True
    )
    g[...] = g_p[...].astype(F32) * column

    def add_norm(l, col, grad, nhat):
        ngrad[pl.ds(l * 8 + col, 1), :] = jnp.sum(grad * nhat, axis=0, keepdims=True)
        ngrad[pl.ds(l * 8 + col + 1, 1), :] = jnp.sum(grad, axis=0, keepdims=True)

    def gm_mate(l, at):
        return remote(wm.at[l + 1, 1 - k, at], gmr.at[at], mgm_s.at[l, at], mgm_r.at[l, at], mate)

    def ga_all(l):
        dst = wa.at[l + 1]
        rows = 2 * N * RW

        def chunk(i, carry):
            off = pl.multiple_of(i * rows, LANES)
            grad_a = dot_tn(a1[l, :, :, pl.ds(off, rows)].reshape(T, rows), dqkv[...])
            grad_p = dot_tn(db[:, :, pl.ds(off, rows)].reshape(T, rows), att[l].reshape(T, FQ))
            dst[i, :, :, :, 0 : 3 * FQ] = grad_a.astype(BF).reshape(2, N, RW, 3 * FQ)
            dst[i, :, :, :, 3 * FQ : 4 * FQ] = grad_p.astype(BF).reshape(2, N, RW, FQ)
            return carry

        lax.fori_loop(0, C, chunk, 0)

    def ga_mate(l):
        return remote(wa.at[l + 1, :, 1 - k], gar, mga_s.at[l], mga_r.at[l], mate)

    def zpart(kind, l, at):
        return wm.at[l + 1, k, at] if kind else wa.at[l + 1, :, k, at]

    def zbuf(kind, l, slot):
        return gmz.at[l, slot] if kind else gaz.at[l, slot]

    def zg_copy(kind, l, owner, device, send, recv):
        ssem, rsem = zg_s.at[2 * l + kind, send], zg_r.at[2 * l + kind, recv]
        return remote(zpart(kind, l, owner), zbuf(kind, l, recv), ssem, rsem, zdev(device))

    def z_direct(kind, l, d):
        return zg_copy(kind, l, n + d, n + d, d + N - 1, (-d) % N - 1)

    def z_beyond(kind, l, d):
        sign = 1 if d > 0 else -1
        return zg_copy(kind, l, n + d, n + d - sign * REACH, d + N - 1, N - 1 + abs(d) - REACH - 1)

    def z_spread(kind, l):
        for d in signed(1, N - 1):
            ready = inside(n + d)
            if abs(d) == REACH:
                ready = ready & jnp.logical_not(inside(n - d // REACH))

            @pl.when(ready)
            def _(d=d):
                (z_beyond if abs(d) > REACH else z_direct)(kind, l, d).start()

    def z_relay(kind, l):
        for sign in (1, -1):
            owner = n + sign * REACH

            @pl.when(inside(owner) & inside(n - sign))
            def _(sign=sign, owner=owner):
                part = zpart(kind, l, owner)
                for q in range(1, REACH):
                    @pl.when(inside(n - sign * q))
                    def _(q=q):
                        slot = N - 1 + q - 1
                        zg_copy(kind, l, n, n, 0, slot).wait_recv()
                        part[...] = (part[...].astype(F32) + zbuf(kind, l, slot)[...].astype(F32)).astype(BF)
                z_direct(kind, l, sign * REACH).start()

    def z_arrive(kind, l, add):
        for d in reversed(signed(1, REACH)):
            @pl.when(inside(n + d))
            def _(d=d):
                slot = d % N - 1
                zg_copy(kind, l, n, n, 0, slot).wait_recv()
                add(zbuf(kind, l, slot))

    def z_drain(kind, l):
        for d in signed(1, N - 1):
            @pl.when(inside(n + d))
            def _(d=d):
                (z_beyond if abs(d) > REACH else z_direct)(kind, l, d).wait_send()

    def gm_add(l, at):
        gm_mate(l, at).wait_recv()
        src = wm.at[l + 1]
        src[k, at] = (src[k, at].astype(F32) + gmr[at].astype(F32)).astype(BF)
        dist = jnp.where(at > n, at - n, n - at)
        sign = jnp.where(at > n, 1, -1)
        beyond = dist > REACH
        device = jnp.where(beyond, at - sign * REACH, at)
        slot = jnp.where(beyond, N - 2 + dist - REACH, lax.rem(n - at + N, N) - 1)

        @pl.when((dist != 0) & ((dist != REACH) | jnp.logical_not(inside(n - sign))))
        def _():
            zg_copy(1, l, at, device, at - n + N - 1, slot).start()

    def gm_all(l):
        dst = wm.at[l + 1]
        per = UNITS // US
        count = HALF // UNITS
        far = flipped(n, N - 1, N)

        def chunk(i, carry):
            core = jnp.where(i < count, 1 - k, k)
            at = flipped(far // per, lax.rem(i, count), count)
            off = pl.multiple_of(core * HALF + at * UNITS, LANES)
            up = dot_tn(dpre_s[:, pl.ds(off, UNITS)], a3[l].reshape(T, D))
            down = dot_tn(hid_s[:, pl.ds(off, UNITS)], dm[...].reshape(T, D))
            rows = pl.ds(at * per, per)
            dst[core, rows, :, 0:D] = up.astype(BF).reshape(per, US, D)
            dst[core, rows, :, D : 2 * D] = down.astype(BF).reshape(per, US, D)

            def owners(e, carry):
                owner = at * per + flipped(lax.rem(far, per), e, per)

                @pl.when(i < count)
                def _():
                    gm_mate(l, owner).start()

                @pl.when(i >= count)
                def _():
                    gm_add(l, owner)

                return carry

            lax.fori_loop(0, per, owners, 0)
            return carry

        lax.fori_loop(0, 2 * count, chunk, 0)

    def ga_spread(l):
        ga_mate(l).wait_recv()
        src = wa.at[l + 1]
        src[:, k] = (src[:, k].astype(F32) + gar[...].astype(F32)).astype(BF)
        z_spread(0, l)

    def gm_out(l):
        return local(stage, out_mlp.at[l], loc.at[2 * LAYERS + l])

    def gm_finish(l):
        stage[...] = wm[l + 1, k, n].astype(F32)

        def add(ref):
            stage[...] += ref[...].astype(F32)

        z_arrive(1, l, add)
        gm_out(l).start()
        z_drain(1, l)
        for at in range(N):
            gm_mate(l, at).wait_send()

    def xg(l, j):
        return remote(gax_s.at[j - 1], gax_r.at[l, j - 1], xg_s.at[l, j - 1], xg_r.at[l, j - 1], xy(j))

    def place(l, at, value):
        for part in range(3):
            cols = pl.ds(pl.multiple_of(part * D + at * FQ, LANES), FQ)
            held_qkv[:, cols] = value[:, part * FQ : (part + 1) * FQ]
        held_proj[:, pl.ds(pl.multiple_of(at * FQ, LANES), FQ)] = value[:, 3 * FQ : 4 * FQ]

    def ga_finish(l):
        stage_a[...] = wa[l + 1, :, k, n].astype(F32)

        def add(ref):
            stage_a[...] += ref[...].astype(F32)

        z_arrive(0, l, add)
        z_drain(0, l)
        ga_mate(l).wait_send()
        for j in range(1, C):
            gax_s[j - 1] = stage_a[chip(j)].astype(BF)
            xg(l, j).start()
        place(l, c, stage_a[c])

    def ga_out(l):
        return (
            local(held_qkv, out_qkv.at[l], fin.at[2 * l]),
            local(held_proj, out_proj.at[l], fin.at[2 * l + 1]),
        )

    def ga_place(l):
        for j in range(1, C):
            xg(l, j).wait()
            place(l, chip(j), gax_r[l, j - 1].astype(F32))
        for copy in ga_out(l):
            copy.start()

    def backward(i, carry):
        l = LAYERS - 1 - i
        p = 2 * LAYERS + 2 * i
        grad = g[...]
        nhat, rstd = normalize(mo[l])
        ag_start(p, dm, norm_back(nhat, rstd, grad, gain(l, 6)).astype(BF))
        add_norm(l, 6, grad, nhat)

        @pl.when(i == 0)
        def _():
            outh_s[...] = (mid[l] + nhat * gain(l, 6) + gain(l, 7)).astype(BF)
            out_z("start")

        ag_pass(p, dm)

        @pl.when((i == 0) & holder)
        def _():
            grad_z("sent")


        def redo(i, carry):
            pre = dot_nt(a3[l, pl.ds(2 * i, 2)].reshape(2 * TB, D), w_up(l))
            rows = pl.ds(i * 2 * TB, 2 * TB)
            pre_s[rows, :] = pre
            hid_s[rows, :] = gelu(pre).astype(BF)
            return carry

        lax.fori_loop(0, C // 2, redo, 0)

        @pl.when(i > 0)
        def _():
            z_relay(0, l + 1)


        def feed_back(i, pair):
            where = [pl.ds(b * TB, TB) for b in pair]
            pre = jnp.concatenate([pre_s[rows, :] for rows in where], axis=0)
            slope = (dot_nt(both(dm, pair), w_down(l)) * gelu_slope(pre)).astype(BF)
            for e, rows in enumerate(where):
                dpre_s[rows, :] = slope[e * TB : (e + 1) * TB]
            rs_pair(p, i, dot_nn(slope, w_up(l)))

        arrivals(p, dm, feed_back)

        @pl.when(i > 0)
        def _():
            pl.semaphore_wait(credit.at[1], 1)

        gm_all(l)

        @pl.when(l > 0)
        def _():
            pl.semaphore_signal(credit.at[1], inc=1, device_id=mate, device_id_type=MESH)

        d_a3 = rs_finish(p)
        nhat, rstd = normalize(mid[l])
        d_mid = g[...] + norm_back(nhat, rstd, d_a3, gain(l, 4))
        g[...] = d_mid
        nhat_b, rstd_b = normalize(br[l])
        ag_start(p + 1, db, norm_back(nhat_b, rstd_b, d_mid, gain(l, 2)).astype(BF))
        add_norm(l, 4, d_a3, nhat)
        add_norm(l, 2, d_mid, nhat_b)
        ag_drain(p, dm)
        for b in range(C):
            weights, inverse = exp_scores(l, b)
            cols = pl.ds(TB * (b * (b + 1) // 2), (b + 1) * TB)
            p_s[:, cols] = (weights * inverse).astype(BF)
        dk_s[...] = jnp.zeros_like(dk_s)
        dv_s[...] = jnp.zeros_like(dv_s)
        ag_pass(p + 1, db)
        for j in range(1, C):
            ag_wait(p + 1, db, j)
        for b in reversed(range(C)):
            size = (b + 1) * TB
            rows = pl.ds(b * TB, TB)
            seen = pl.ds(0, size)
            d_att = by_head(dot_nn(db[b], w_proj(l)).astype(BF))
            d_probs = dot_nt(d_att, vs_[l, 0 : b + 1].reshape(size, FQ))
            low = p_s[:, pl.ds(TB * (b * (b + 1) // 2), size)]
            probs = low.astype(F32)
            delta = jnp.sum(probs * d_probs, axis=-1, keepdims=True)
            d_scores = (probs * (d_probs - delta)).astype(BF)
            d_query = of_heads(dot_nn(d_scores, ks_[l, 0 : b + 1].reshape(size, FQ)))
            d_query = d_query * HEAD_DIM ** (-0.5)
            dk_s[seen, :] += dot_tn(d_scores, by_head(qs_[l, b]))
            dv_s[seen, :] += dot_tn(low, d_att)
            d_key = dk_s[rows, :]
            cosine, sine = tables(b)
            dqkv[rows, 0:FQ] = (d_query * cosine - swapped(d_query) * sine).astype(BF)
            dqkv[rows, FQ : 2 * FQ] = (d_key * cosine - swapped(d_key) * sine).astype(BF)
            dqkv[rows, 2 * FQ : 3 * FQ] = dv_s[rows, :].astype(BF)
            rs_block(p + 1, b, dot_nt(dqkv[rows, :], w_qkv(l)))
        z_relay(1, l)

        @pl.when(i > 0)
        def _():
            pl.semaphore_wait(credit.at[0], 1)

        ga_all(l)
        ga_mate(l).start()

        @pl.when(i > 0)
        def _():
            gm_finish(l + 1)
            ga_finish(l + 1)

        ga_spread(l)

        @pl.when(l > 0)
        def _():
            pl.semaphore_signal(credit.at[0], inc=1, device_id=mate, device_id_type=MESH)


        @pl.when((i == LAYERS - 1) & holder)
        def _():
            out_held()
            out_plane("start")

        d_a1 = rs_finish(p + 1)
        nhat, rstd = normalize(st[l])
        g[...] = g[...] + norm_back(nhat, rstd, d_a1, gain(l, 0))
        add_norm(l, 0, d_a1, nhat)
        ag_drain(p + 1, db)

        @pl.when(i == 0)
        def _():
            for kind in range(2):
                for at in range(LAYERS):
                    w_drain(kind, at)
            perm(0, "sent")
            grad_plane("sent")


        return carry

    lax.fori_loop(0, LAYERS, backward, 0)

    g_p[...] = g[...].astype(BF)
    n_start(1, "m", ngrad[...])

    z_relay(0, 0)
    n_start(1, "x", n_finish(1, "m"))
    gm_out(1).wait()
    gm_finish(0)
    perm(1, "start")
    n_start(1, "z", n_finish(1, "x"))
    ga_place(1)

    for copy in ga_out(1):
        copy.wait()
    ga_finish(0)
    total = n_finish(1, "z")
    for l in range(LAYERS):
        out_n[l] = lax.dot_general(
            total[l * 8 : (l + 1) * 8], spot, (((1,), (1,)), ((), ())),
            preferred_element_type=F32, precision=lax.Precision.HIGHEST,
        )
    ga_place(0)
    gm_out(0).wait()

    for l in range(LAYERS):
        for j in range(1, C):
            a2a_all(l, j).wait_send()
    perm(1, "here")
    g[...] = hid_p[...].astype(F32)
    grad_out = local(g, out_g, fin.at[2 * LAYERS])
    grad_out.start()
    perm(1, "sent")
    out_z("sent")
    out_here()

    @pl.when(holder)
    def _():
        out_plane("sent")

    for copy in ga_out(0):
        copy.wait()
    grad_out.wait()


def copy_out(*refs):
    count = (len(refs) - 1) // 3
    sems = refs[-1]
    into, out = [], []
    for i in range(count):
        src, dst, held = refs[i], refs[count + i], refs[2 * count + i]
        cuts = [()]
        if len(held.shape) == 3:
            half = held.shape[1] // 2 if held.shape[1] >= 128 else held.shape[1]
            cuts = [(l, pl.ds(at, half)) for l in range(held.shape[0]) for at in range(0, held.shape[1], half)]
        for at in cuts:
            one, two, three = (ref.at[at] if at else ref for ref in (src, held, dst))
            into.append(pltpu.make_async_copy(one, two, sems.at[2 * len(into)]))
            out.append(pltpu.make_async_copy(two, three, sems.at[2 * len(out) + 1]))
    for copy in into:
        copy.start()
    for first, second in zip(into, out):
        first.wait()
        second.start()
    for copy in out:
        copy.wait()


def body(mesh, hidden_in, w_qkv, w_proj, w_mlp, norm_params, grad_output, corpus_id, corpus_weight):
    W, N = mesh.shape["wide"], mesh.shape["narrow"]
    C = W // 2
    TB, D = hidden_in.shape
    FQ, UQ, RW, US = D // C, FF // C, D // (W * N), FF // (W * N)
    AW = 4 * FQ
    T = C * TB
    REACH = N // 2
    assert C == N and w_mlp.shape[1] == US and w_qkv.shape[1] == RW

    half = HEAD_DIM // 2
    freqs = np.float32(ROPE_BASE) ** (-np.arange(half, dtype=np.float32) / np.float32(half))
    angles = (np.arange(T, dtype=np.float32)[:, None] * freqs[None, :]).astype(np.float32)
    cosine = np.tile(np.cos(angles), (1, LANES // half)).astype(np.float32)
    sine = np.sin(angles)
    sine = np.tile(np.concatenate([-sine, sine], axis=1), (1, LANES // HEAD_DIM)).astype(np.float32)

    NR = LAYERS * 8
    dma = pltpu.SemaphoreType.DMA
    vm = pltpu.VMEM
    L = LAYERS
    scratch = [
        vm((T, LANES), F32),
        vm((T, LANES), F32),
        vm((RW, 3 * D), F32),
        vm((RW, D), F32),
        vm((L + 1, C, 2, N, RW, AW), BF),
        vm((L + 1, 2, N, US, 2 * D), BF),
        vm((L, C, TB, D), BF),
        vm((L, C, TB, D), BF),
        vm((C, TB, D), BF),
        vm((C, TB, D), BF),
        vm((L, C, TB, FQ), BF),
        vm((L, C, TB, FQ), BF),
        vm((L, C, TB, FQ), BF),
        vm((L, C, TB, FQ), BF),
        vm((L, TB, D), F32),
        vm((L, TB, D), F32),
        vm((L, TB, D), F32),
        vm((L, TB, D), F32),
        vm((T, UQ), F32),
        vm((T, UQ), BF),
        vm((T, UQ), BF),
        vm((FQ // HEAD_DIM * TB, TB * C * (C + 1) // 2), BF),
        vm((T, FQ), F32),
        vm((T, FQ), F32),
        vm((T, 3 * FQ), BF),
        vm((C - 1, TB, D), BF),
        vm((C - 1, TB, D), BF),
        vm((2, TB // 2, D), BF),
        vm((TB, D), F32),
        vm((TB, D), BF),
        vm((TB, D), BF),
        vm((8, TB), F32),
        vm((C, 8, TB), F32),
        vm((8, TB), F32),
        vm((TB, D), BF),
        vm((N, TB, D), BF),
        vm((TB, D), F32),
        vm((N, US, 2 * D), BF),
        vm((L, N + REACH - 2, US, 2 * D), BF),
        vm((US, 2 * D), F32),
        vm((C, RW, AW), F32),
        vm((C, N, RW, AW), BF),
        vm((L, N + REACH - 2, C, RW, AW), BF),
        vm((C - 1, RW, AW), BF),
        vm((L, C - 1, RW, AW), BF),
        vm((NR, D), F32),
        vm((NR, D), F32),
        vm((3, NR, D), BF),
        vm((3, C - 1, NR, D), BF),
        vm((3, NR, D), F32),
        vm((3, C - 1, NR, D), F32),
        dma((2,)), dma((2,)),
        dma((2,)), dma((2, C)),
        dma((2, C)), dma((2,)),
        dma((1,)), dma((N,)),
        dma((N,)), dma((1,)),
        dma((3 * L,)),
        dma((L, C - 1)), dma((L, C - 1)),
        dma((2, max(C - 1, 6))), dma((2, max(C - 1, 6))),
        dma((2, max(C - 1, 6))), dma((2, max(C - 1, 6))),
        dma((2 * L, 4 * REACH)), dma((2 * L, N)),
        dma((2 * L, N)), dma((2 * L, N)),
        dma((2 * L, 2 * N - 1)), dma((2 * L, N + REACH - 2)),
        dma((L,)), dma((L,)),
        dma((L, N)), dma((L, N)),
        dma((L, C - 1)), dma((L, C - 1)),
        dma((2, C - 1)), dma((2, C - 1)),
        dma((2, N - 1)), dma((2, N - 1)),
        dma((2,)), dma((2,)),
        dma((2 * L + 3,)),
        pltpu.SemaphoreType.REGULAR((2,)),
    ]
    vspec = pl.BlockSpec(memory_space=pltpu.VMEM)
    anyspec = pl.BlockSpec(memory_space=pl.ANY)
    shapes = (
        jax.ShapeDtypeStruct((TB, D), BF),
        jax.ShapeDtypeStruct((TB, D), F32),
        jax.ShapeDtypeStruct((L, RW, 3 * D), F32),
        jax.ShapeDtypeStruct((L, RW, D), F32),
        jax.ShapeDtypeStruct((L, US, 2 * D), F32),
        jax.ShapeDtypeStruct((L, 8, RW), F32),
    )
    outs = pl.pallas_call(
        partial(kernel_body, (C, N, TB, D, FQ, UQ, RW, US, AW)),
        out_shape=shapes,
        in_specs=[anyspec] * 2 + [vspec] * 3 + [anyspec] * 5,
        out_specs=(anyspec,) * 5 + (vspec,),
        scratch_shapes=scratch,
        compiler_params=pltpu.CompilerParams(
            collective_id=0, has_side_effects=True, vmem_limit_bytes=127 << 19
        ),
    )(
        hidden_in, grad_output, corpus_id.reshape(1, TB), corpus_weight.reshape(1, -1), norm_params.transpose(0, 2, 1),
        jnp.asarray(cosine), jnp.asarray(sine), w_qkv, w_proj, w_mlp,
    )
    outs = pl.pallas_call(
        copy_out,
        out_shape=shapes,
        in_specs=[anyspec] * len(shapes),
        out_specs=(anyspec,) * len(shapes),
        scratch_shapes=[vm(one.shape, one.dtype) for one in shapes] + [dma((4 * len(shapes),))],
        compiler_params=pltpu.CompilerParams(vmem_limit_bytes=60 << 20),
    )(*outs)
    return (*outs[:5], outs[5].transpose(0, 2, 1))


def solution(mesh):
    rows = P(("wide", "narrow"), None)
    layered = P(None, ("wide", "narrow"), None)
    return jax.shard_map(
        partial(body, mesh),
        mesh=mesh,
        in_specs=(rows, layered, layered, layered, layered, rows, P(("wide", "narrow")), P()),
        out_specs=(rows, rows, layered, layered, layered, layered),
        check_vma=False,
    )
```

```python
from functools import partial

import jax
import jax.numpy as jnp
import numpy as np
from jax import lax
from jax.experimental import pallas as pl
from jax.experimental.pallas import tpu as pltpu
from jax.sharding import PartitionSpec as P

HEADS = 16
HEAD_DIM = 64
FF = 4096
LAYERS = 2
EPS = 1e-05
MASKED = -1e30
ROPE_BASE = 10000.0
MESH = pl.DeviceIdType.MESH
BF = jnp.bfloat16
F32 = jnp.float32
LANES = 128
UNITS = 256


def dot_nn(left, right):
    return lax.dot_general(left, right, (((1,), (0,)), ((), ())), preferred_element_type=F32)


def dot_nt(left, right):
    return lax.dot_general(left, right, (((1,), (1,)), ((), ())), preferred_element_type=F32)


def dot_tn(left, right):
    return lax.dot_general(left, right, (((0,), (0,)), ((), ())), preferred_element_type=F32)


def normalize(inputs):
    centre = jnp.mean(inputs, axis=-1, keepdims=True)
    centered = inputs - centre
    rstd = lax.rsqrt(jnp.mean(centered * centered, axis=-1, keepdims=True) + EPS)
    return centered * rstd, rstd


def norm_back(nhat, rstd, grad, gain):
    scaled = grad * gain
    mean_f = jnp.mean(scaled, axis=-1, keepdims=True)
    mean_fn = jnp.mean(scaled * nhat, axis=-1, keepdims=True)
    return rstd * (scaled - mean_f - nhat * mean_fn)


GELU_S = 0.7978845608028654
GELU_A = 0.044715


def gelu(pre):
    return 0.5 * pre * (1.0 + jnp.tanh(GELU_S * (pre + GELU_A * pre * pre * pre)))


def gelu_slope(pre):
    square = pre * pre
    turned = jnp.tanh(GELU_S * (pre + GELU_A * pre * square))
    inner = GELU_S * (1.0 + 3.0 * GELU_A * square)
    return 0.5 * (1.0 + turned) + 0.5 * pre * (1.0 - turned * turned) * inner


def kernel_body(
    dims,
    hid_ref, gout_ref, ids_ref, cw_ref, nrm_ref, cos_in, sin_in, wq_ref, wp_ref, wm_ref,
    out_h, out_g, out_qkv, out_proj, out_mlp, out_n,
    cos_ref, sin_ref, held_qkv, held_proj,
    wa, wm, a1, a3, dm, db, qs_, ks_, vs_, att, st, br, mid, mo,
    pre_s, hid_s, dpre_s, p_s, dk_s, dv_s, dqkv,
    rs_send, rs_recv, rs_mid, acc, hid_p, g_p, sc_own, sc_x, sc_p, outh_s, hx, g,
    gmr, gmz, stage, stage_a, gar, gaz, gax_s, gax_r,
    npar, ngrad, nf_send, nf_recv, nb_send, nb_recv,
    perm_s, perm_r, gp_s, gp_r, gz_s, gz_r, oz_s, oz_r, op_s, op_r, loc, a2a_s, a2a_r, ag_s, ag_r, rs_s, rs_r,
    zw_s, zw_r, mw_s, mw_r, zg_s, zg_r, mga_s, mga_r, mgm_s, mgm_r, xg_s, xg_r,
    nx_s, nx_r, nz_s, nz_r, nm_s, nm_r, fin, credit,
):
    C, N, TB, D, FQ, UQ, RW, US, AW = dims
    T = C * TB
    HPC = FQ // HEAD_DIM
    HALF = N * US
    REACH = N // 2
    w = lax.axis_index("wide")
    n = lax.axis_index("narrow")
    c = w // 2
    k = lax.rem(w, 2)
    mate = (2 * c + (1 - k), n)
    to_chip = n + k * (N - 1 - 2 * n)
    to_plane = c + k * (N - 1 - 2 * c)
    swap = (2 * to_chip + k, to_plane)
    moves = to_chip != c

    def block(at):
        return at + k * (C - 1 - 2 * at)

    mine = block(c)

    def flipped(base, j, count):
        out, bit = 0, 1
        while bit < count:
            ours = lax.rem(base // bit, 2)
            flip = (j // bit) % 2 if isinstance(j, int) else lax.rem(j // bit, 2)
            out = out + bit * (ours + flip - 2 * ours * flip)
            bit *= 2
        return out

    def chip(j):
        return flipped(c, j, C)

    def xy(j):
        return (2 * chip(j) + k, n)

    def zdev(at):
        return (w, at)

    def remote(src, dst, ssem, rsem, device):
        return pltpu.make_async_remote_copy(
            src_ref=src, dst_ref=dst, send_sem=ssem, recv_sem=rsem,
            device_id=device, device_id_type=MESH,
        )

    def local(src, dst, sem):
        return pltpu.make_async_copy(src, dst, sem)

    barrier = pltpu.get_barrier_semaphore()
    partners = [xy(j) for j in range(1, C)] + [mate]
    partners += [zdev(lax.rem(n + j, N)) for j in range(1, N)]
    for device in partners:
        pl.semaphore_signal(barrier, inc=1, device_id=device, device_id_type=MESH)

    @pl.when(moves)
    def _():
        pl.semaphore_signal(barrier, inc=1, device_id=swap, device_id_type=MESH)

    pl.semaphore_wait(barrier, len(partners) + jnp.where(moves, 1, 0))

    rope = (
        local(cos_in, cos_ref, fin.at[2 * LAYERS + 1]), local(sin_in, sin_ref, fin.at[2 * LAYERS + 2])
    )
    for copy in rope:
        copy.start()

    def either(far, src, dst, ssem, rsem, device, act):
        @pl.when(far)
        def _():
            getattr(remote(src, dst, ssem, rsem, device), {"here": "wait_recv", "sent": "wait_send"}.get(act, act))()

        if act != "sent":
            @pl.when(jnp.logical_not(far))
            def _():
                getattr(local(src, dst, rsem), {"here": "wait"}.get(act, act))()

    def perm(i, act):
        src, dst = ((hid_ref, hid_p), (g_p, hid_p))[i]
        either(moves, src, dst, perm_s.at[i], perm_r.at[i], swap, act)

    holder = c == to_chip

    def grad_plane(act):
        for e, (src, dst) in enumerate(((gout_ref, db.at[c]), (sc_own, sc_x.at[c]))):
            either(jnp.logical_not(holder), src, dst, gp_s.at[e], gp_r.at[e, c], (2 * to_chip + k, n), act)

    def grad_held():
        for at in range(C):
            for e, dst in enumerate((db.at[at], sc_x.at[at])):
                either(c != at, dst, dst, gp_s.at[e], gp_r.at[e, at], (2 * at + k, n), "here")

    def grad_z(act):
        for at in range(C):
            plane = at + k * (N - 1 - 2 * at)
            for e, (src, dst) in enumerate(((db.at[at], g_p), (sc_x.at[at], sc_p))):
                either(plane != n, src, dst, gz_s.at[e, at], gz_r.at[e], (w, plane), act)

    def grad_here():
        for e, dst in enumerate((g_p, sc_p)):
            either(to_plane != n, dst, dst, gz_s.at[e, 0], gz_r.at[e], (w, to_plane), "here")

    def out_z(act):
        either(to_plane != n, outh_s, hx.at[n], oz_s.at[0], oz_r.at[n], (w, to_plane), act)

    def out_held():
        for at in range(N):
            either(n != at, hx.at[at], hx.at[at], oz_s.at[0], oz_r.at[at], (w, at), "here")

    def out_plane(act):
        for at in range(N):
            dest = at + k * (N - 1 - 2 * at)
            either(dest != c, hx.at[at], out_h, op_s.at[at], op_r.at[0], (2 * dest + k, n), act)

    def out_here():
        either(jnp.logical_not(holder), hx.at[0], out_h, op_s.at[0], op_r.at[0], (2 * to_chip + k, n), "here")

    perm(0, "start")

    def n_copy(way, axis, j):
        send, heard = (nf_send, nf_recv) if way == 0 else (nb_send, nb_recv)
        slot = n_slot[axis]
        if axis == "x":
            return remote(send.at[slot], heard.at[slot, j - 1], nx_s.at[way], nx_r.at[way], xy(j))
        if axis == "z":
            there = zdev(lax.rem(n + j, N))
            return remote(send.at[slot], heard.at[slot, j - 1], nz_s.at[way], nz_r.at[way], there)
        return remote(send.at[slot], heard.at[slot, j - 1], nm_s.at[way], nm_r.at[way], mate)

    n_count = {"x": C, "z": N, "m": 2}
    n_slot = {"x": 0, "z": 1, "m": 2}

    def n_start(way, axis, value):
        send = nf_send if way == 0 else nb_send
        send[n_slot[axis]] = value.astype(send.dtype)
        for j in range(1, n_count[axis]):
            n_copy(way, axis, j).start()

    def n_finish(way, axis):
        send, heard = (nf_send, nf_recv) if way == 0 else (nb_send, nb_recv)
        total = send[n_slot[axis]].astype(F32)
        whole = heard.at[n_slot[axis], pl.ds(0, n_count[axis] - 1)]
        ssem, rsem = {"x": (nx_s, nx_r), "z": (nz_s, nz_r), "m": (nm_s, nm_r)}[axis]
        remote(whole, whole, ssem.at[way], rsem.at[way], mate).wait()
        for j in range(1, n_count[axis]):
            total = total + heard[n_slot[axis], j - 1].astype(F32)
        return total

    first = (w * N + n) * RW
    spot = lax.broadcasted_iota(jnp.int32, (RW, D), 1) == (
        lax.broadcasted_iota(jnp.int32, (RW, D), 0) + first
    )
    spot = spot.astype(F32)
    n_start(0, "x", jnp.concatenate(
        [dot_nn(nrm_ref[l], spot.astype(BF)) for l in range(LAYERS)], axis=0
    ))

    def pieces(l, at):
        for part in range(3):
            cols = pl.ds(pl.multiple_of(part * D + at * FQ, LANES), FQ)
            yield wq_ref.at[l, :, cols], wa.at[l, c, k, n, :, pl.ds(part * FQ, FQ)]
        cols = pl.ds(pl.multiple_of(at * FQ, LANES), FQ)
        yield wp_ref.at[l, :, cols], wa.at[l, c, k, n, :, pl.ds(3 * FQ, FQ)]

    def a2a_start(l):
        for j in range(1, C):
            for src, dst in pieces(l, chip(j)):
                remote(src, dst, a2a_s.at[l, j - 1], a2a_r.at[l, j - 1], xy(j)).start()

    def a2a_all(l, j):
        there = wa.at[l, chip(j), k, n]
        return remote(there, there, a2a_s.at[l, j - 1], a2a_r.at[l, j - 1], xy(j))

    def own_wa(l):
        mine = wa.at[l, c, k, n]
        return local(mine, mine, loc.at[l])

    def own_wm(l):
        return local(wm_ref.at[l], wm.at[l, k, n], loc.at[LAYERS + l])

    a2a_start(0)
    for l in range(LAYERS):
        for src, dst in pieces(l, c):
            local(src, dst, loc.at[l]).start()
        own_wm(l).start()

    def shard(kind, l, core, at):
        return wm.at[l, core, at] if kind else wa.at[l, :, core, at]

    def inside(at):
        return (at >= 0) & (at < N)

    def signed(least, most):
        return [sign * d for d in range(most, least - 1, -1) for sign in (1, -1)]

    def zw_copy(kind, l, origin, at, slot):
        rows = shard(kind, l, k, origin)
        return remote(rows, rows, zw_s.at[2 * l + kind, slot], zw_r.at[2 * l + kind, origin], zdev(at))

    def direct_slot(d):
        return d + REACH

    def relay_slot(sign, q):
        return 2 * REACH + (q if sign > 0 else q + REACH - 1)

    def to_mate(kind, l, at):
        rows = shard(kind, l, k, at)
        return remote(rows, rows, mw_s.at[2 * l + kind], mw_r.at[2 * l + kind], mate)

    def mate_half(kind, l, core):
        rows = wm.at[l, core] if kind else wa.at[l, :, core]
        return remote(rows, rows, mw_s.at[2 * l + kind], mw_r.at[2 * l + kind], mate)

    def w_send(kind, l):
        for d in signed(1, REACH):
            @pl.when(inside(n + d))
            def _(d=d):
                zw_copy(kind, l, n, n + d, direct_slot(d)).start()

        to_mate(kind, l, n).start()

    def w_relay(kind, l):
        for sign in (1, -1):
            origin = n - sign * REACH

            @pl.when(inside(origin) & inside(n + sign))
            def _(sign=sign, origin=origin):
                zw_copy(kind, l, origin, n, 0).wait_recv()
                for q in range(1, REACH):
                    @pl.when(inside(n + sign * q))
                    def _(q=q):
                        zw_copy(kind, l, origin, n + sign * q, relay_slot(sign, q)).start()

    def w_arrive(kind, l):
        for d in reversed(signed(1, N - 1)):
            origin = n + d

            @pl.when(inside(origin))
            def _(d=d, origin=origin):
                if abs(d) == REACH:
                    sign = -1 if d > 0 else 1

                    @pl.when(jnp.logical_not(inside(n + sign)))
                    def _():
                        zw_copy(kind, l, origin, n, 0).wait_recv()
                else:
                    zw_copy(kind, l, origin, n, 0).wait_recv()
                to_mate(kind, l, origin).start()

    def w_ready(kind, l):
        mate_half(kind, l, 1 - k).wait_recv()

    def w_drain(kind, l):
        for d in signed(1, REACH):
            @pl.when(inside(n + d))
            def _(d=d):
                zw_copy(kind, l, n, n + d, direct_slot(d)).wait_send()

        for sign in (1, -1):
            origin = n - sign * REACH
            for q in range(1, REACH):
                @pl.when(inside(origin) & inside(n + sign) & inside(n + sign * q))
                def _(sign=sign, origin=origin, q=q):
                    zw_copy(kind, l, origin, n + sign * q, relay_slot(sign, q)).wait_send()

        mate_half(kind, l, k).wait_send()

    n_start(0, "z", n_finish(0, "x"))
    own_wa(0).wait()
    for j in range(1, C):
        a2a_all(0, j).wait_recv()
    w_send(0, 0)
    n_start(0, "m", n_finish(0, "z"))
    npar[...] = n_finish(0, "m")
    ngrad[...] = jnp.zeros_like(ngrad)

    def gain(l, col):
        return npar[pl.ds(l * 8 + col, 1), :]

    SPLIT = C == 4
    hops = ((1, 0), (1, 1), (2, 1), (2, 0), (2, 0), (1, 1))

    def ag_copy(p, buf, source, slot):
        if not SPLIT:
            rows = buf.at[block(source)]
            return remote(rows, rows, ag_s.at[lax.rem(p, 2), slot], ag_r.at[lax.rem(p, 2), slot], xy(slot + 1))
        j, part = hops[slot]
        rows = buf.at[block(source), pl.ds(part * (TB // 2), TB // 2)]
        return remote(rows, rows, ag_s.at[lax.rem(p, 2), slot], ag_r.at[lax.rem(p, 2), slot], xy(j))

    def ag_start(p, buf, value):
        buf[mine] = value
        for slot in (0, 2, 1, 3) if SPLIT else range(C - 1):
            ag_copy(p, buf, c, slot).start()

    def ag_pass(p, buf):
        if SPLIT:
            ag_copy(p, buf, chip(1), 0).wait_recv()
            ag_copy(p, buf, chip(1), 4).start()
            ag_copy(p, buf, chip(2), 2).wait_recv()
            ag_copy(p, buf, chip(2), 5).start()

    def ag_wait(p, buf, j):
        for slot in ((), (1,), (3,), (4, 5))[j] if SPLIT else (j - 1,) * min(j, 1):
            ag_copy(p, buf, chip(j), slot).wait_recv()

    def ag_drain(p, buf):
        for slot in range(4) if SPLIT else range(C - 1):
            ag_copy(p, buf, c, slot).wait_send()
        if SPLIT:
            ag_copy(p, buf, chip(1), 4).wait_send()
            ag_copy(p, buf, chip(2), 5).wait_send()

    def rs_copy(p, j):
        return remote(rs_send.at[j - 1], rs_recv.at[j - 1], rs_s.at[lax.rem(p, 2), j - 1], rs_r.at[lax.rem(p, 2), j - 1], xy(j))

    def rs_put(p, j, value):
        @pl.when(j > 0)
        def _():
            rs_send[j - 1] = value.astype(BF)
            rs_copy(p, j).start()

        @pl.when(j == 0)
        def _():
            acc[...] = value

    def rs_block(p, b, value):
        rs_put(p, chip(block(b)), value)

    def rs_pair(p, i, value):
        rs_put(p, 2 * i, value[0:TB])
        rs_send[2 * i] = value[TB:].astype(BF)
        rs_copy(p, 2 * i + 1).start()

    def half_copy(p, slot):
        part = pl.ds((0, 1, 1, 0, 0, 1)[slot] * (TB // 2), TB // 2)
        src = rs_send.at[(0, 0, 1, 1, 2, 2)[slot], part]
        dst = rs_mid.at[slot - 4] if slot >= 4 else rs_recv.at[(0, 0, 1, 1)[slot], part]
        return remote(src, dst, rs_s.at[lax.rem(p, 2), slot], rs_r.at[lax.rem(p, 2), slot], xy((1, 1, 2, 2, 1, 2)[slot]))

    def half_put(p, i, value):
        @pl.when(i == 0)
        def _():
            rs_send[2] = value.astype(BF)
            half_copy(p, 4).start()
            half_copy(p, 5).start()

        @pl.when(i == 1)
        def _():
            rs_send[0] = value.astype(BF)
            half_copy(p, 0).start()

        @pl.when(i == 2)
        def _():
            rs_send[1] = value.astype(BF)
            half_copy(p, 2).start()

        @pl.when(i == 3)
        def _():
            acc[...] = value

    def half_chip(i):
        return chip(jnp.where(i == 0, 3, jnp.where(i == 3, 0, i)))

    def half_pass(p):
        for slot, at, rows, onward in ((4, 1, pl.ds(0, TB // 2), 3), (5, 0, pl.ds(TB // 2, TB // 2), 1)):
            half_copy(p, slot).wait_recv()
            rs_send[at, rows] = (rs_send[at, rows].astype(F32) + rs_mid[slot - 4].astype(F32)).astype(BF)
            half_copy(p, onward).start()

    def rs_halves_finish(p):
        for slot in range(4):
            half_copy(p, slot).wait()
        half_copy(p, 4).wait_send()
        half_copy(p, 5).wait_send()
        return acc[...] + rs_recv[0].astype(F32) + rs_recv[1].astype(F32)

    def arrivals(p, buf, use):
        def step(i, carry):
            for at in range(C // 2):
                @pl.when(i == at)
                def _(at=at):
                    ag_wait(p, buf, 2 * at)
                    ag_wait(p, buf, 2 * at + 1)

            use(i, (block(chip(2 * i)), block(chip(2 * i + 1))))
            return carry

        lax.fori_loop(0, C // 2, step, 0)

    def both(ref, pair):
        return jnp.concatenate([ref[b] for b in pair], axis=0)

    def rs_finish(p):
        total = acc[...]
        for j in range(1, C):
            rs_copy(p, j).wait()
            total = total + rs_recv[j - 1].astype(F32)
        return total

    lane = lax.broadcasted_iota(jnp.int32, (TB, FQ), 1)
    low_half = lax.rem(lane, HEAD_DIM) < HEAD_DIM // 2
    head_of = lane // HEAD_DIM
    causal = lax.broadcasted_iota(jnp.int32, (HPC * TB, TB), 1) <= lax.rem(
        lax.broadcasted_iota(jnp.int32, (HPC * TB, TB), 0), TB
    )

    def tables(b):
        rows = pl.ds(b * TB, TB)
        reps = FQ // LANES
        return (
            jnp.concatenate([cos_ref[rows, :]] * reps, axis=1),
            jnp.concatenate([sin_ref[rows, :]] * reps, axis=1),
        )

    def swapped(u):
        half_dim = HEAD_DIM // 2
        return jnp.where(
            low_half, pltpu.roll(u, FQ - half_dim, 1), pltpu.roll(u, half_dim, 1)
        )

    def w_qkv(l):
        return wa[l, :, :, :, :, 0 : 3 * FQ].reshape(D, 3 * FQ)

    def w_proj(l):
        return wa[l, :, :, :, :, 3 * FQ : 4 * FQ].reshape(D, FQ)

    def w_up(l):
        return wm[l, :, :, :, 0:D].reshape(UQ, D)

    def w_down(l):
        return wm[l, :, :, :, D : 2 * D].reshape(UQ, D)

    def by_head(rows):
        return jnp.concatenate(
            [jnp.where(head_of == h, rows, jnp.zeros((), rows.dtype)) for h in range(HPC)], axis=0
        )

    def of_heads(stacked):
        out = stacked[0:TB]
        for h in range(1, HPC):
            out = jnp.where(head_of == h, stacked[h * TB : (h + 1) * TB], out)
        return out

    def exp_scores(l, b):
        scores = dot_nt(by_head(qs_[l, b]), ks_[l, 0 : b + 1].reshape((b + 1) * TB, FQ))
        last = jnp.where(causal, scores[:, b * TB :], MASKED)
        scores = jnp.concatenate([scores[:, : b * TB], last], axis=1) if b else last
        weights = jnp.exp(scores - jnp.max(scores, axis=-1, keepdims=True))
        return weights, 1.0 / jnp.sum(weights, axis=-1, keepdims=True)

    w_relay(0, 0)
    own_wm(0).wait()
    w_send(1, 0)
    perm(0, "here")
    st[0] = hid_p[...].astype(F32)
    ids = jnp.broadcast_to(ids_ref[...], (8, TB))
    scale = jnp.zeros((8, TB), F32)
    for i in range(cw_ref.shape[1]):
        scale = jnp.where(ids == i, cw_ref[:, i : i + 1], scale)
    sc_own[...] = scale
    for copy in rope:
        copy.wait()

    def grad_move():
        @pl.when(holder)
        def _():
            grad_held()
            grad_z("start")

    def forward(l, carry):
        p = 2 * l
        more = l + 1 < LAYERS
        nhat, unused = normalize(st[l])
        ag_start(p, a1.at[l], (nhat * gain(l, 0) + gain(l, 1)).astype(BF))

        @pl.when(l == 0)
        def _():
            a2a_start(1)

        ag_pass(p, a1.at[l])

        @pl.when(l == 0)
        def _():
            grad_plane("start")

        w_arrive(0, l)
        w_ready(0, l)

        def qkv_step(i, pair):
            u = dot_nn(both(a1.at[l], pair), w_qkv(l))
            for e, b in enumerate(pair):
                cosine, sine = tables(b)
                uq = u[e * TB : (e + 1) * TB, 0:FQ]
                uk = u[e * TB : (e + 1) * TB, FQ : 2 * FQ]
                uq = (uq * cosine + swapped(uq) * sine).astype(BF)
                qs_[l, b] = (uq * HEAD_DIM ** (-0.5)).astype(BF)
                ks_[l, b] = (uk * cosine + swapped(uk) * sine).astype(BF)
                vs_[l, b] = u[e * TB : (e + 1) * TB, 2 * FQ :].astype(BF)

        arrivals(p, a1.at[l], qkv_step)
        def attend(b):
            weights, inverse = exp_scores(l, b)
            mixed = dot_nn(weights.astype(BF), vs_[l, 0 : b + 1].reshape((b + 1) * TB, FQ))
            low = of_heads(mixed * inverse).astype(BF)
            att[l, b] = low
            return dot_nt(low, w_proj(l))

        if SPLIT:

            def attend_step(i, carry):
                for b in range(C):
                    @pl.when(block(half_chip(i)) == b)
                    def _(b=b):
                        acc[...] = attend(b)

                half_put(p, i, acc[...])
                return carry

            lax.fori_loop(0, C, attend_step, 0)
            half_pass(p)
        else:
            for b in range(C):
                rs_block(p, b, attend(b))
        w_relay(1, l)

        @pl.when(more)
        def _():
            own_wa(l + 1).wait()
            for j in range(1, C):
                a2a_all(l + 1, j).wait_recv()
            w_send(0, l + 1)

        branch = (rs_halves_finish if SPLIT else rs_finish)(p)
        br[l] = branch
        nhat, unused = normalize(branch)
        middle = st[l] + nhat * gain(l, 2) + gain(l, 3)
        mid[l] = middle
        nhat, unused = normalize(middle)
        ag_start(p + 1, a3.at[l], (nhat * gain(l, 4) + gain(l, 5)).astype(BF))
        ag_drain(p, a1.at[l])
        ag_pass(p + 1, a3.at[l])
        w_arrive(1, l)


        def feed(x, core):
            up = wm[l, core, :, :, 0:D].reshape(N * US, D)
            down = wm[l, core, :, :, D : 2 * D].reshape(N * US, D)
            return dot_nn(gelu(dot_nt(x, up)).astype(BF), down)

        if SPLIT:
            for j in range(1, C):
                ag_wait(p + 1, a3.at[l], j)
            pre_s[...] = feed(a3[l].reshape(T, D), k)
            w_ready(1, l)

            def feed_step(i, carry):
                pair = (block(half_chip(2 * i)), block(half_chip(2 * i + 1)))
                value = feed(both(a3.at[l], pair), 1 - k)
                value = value + jnp.concatenate([pre_s[pl.ds(b * TB, TB), :] for b in pair], axis=0)
                half_put(p + 1, 2 * i, value[0:TB])
                half_put(p + 1, 2 * i + 1, value[TB:])
                return carry

            lax.fori_loop(0, 2, feed_step, 0)

            @pl.when(jnp.logical_not(more))
            def _():
                grad_move()

            half_pass(p + 1)
        else:
            @pl.when(jnp.logical_not(more))
            def _():
                grad_move()

            w_ready(1, l)
            arrivals(p + 1, a3.at[l], lambda i, pair: rs_pair(
                p + 1, i, feed(both(a3.at[l], pair), k) + feed(both(a3.at[l], pair), 1 - k)
            ))

        @pl.when(more)
        def _():
            w_relay(0, l + 1)
            own_wm(l + 1).wait()
            w_send(1, l + 1)

        mlp_out = (rs_halves_finish if SPLIT else rs_finish)(p + 1)
        mo[l] = mlp_out

        @pl.when(more)
        def _():
            nhat, unused = normalize(mlp_out)
            st[l + 1] = mid[l] + nhat * gain(l, 6) + gain(l, 7)

        ag_drain(p + 1, a3.at[l])
        return carry

    lax.fori_loop(0, LAYERS, forward, 0)
    grad_here()
    here = lax.broadcasted_iota(jnp.int32, (TB, TB), 0) == lax.broadcasted_iota(jnp.int32, (TB, TB), 1)
    column = jnp.sum(
        jnp.where(here, jnp.broadcast_to(sc_p[0:1, :], (TB, TB)), 0.0), axis=1, keepdims=True
    )
    g[...] = g_p[...].astype(F32) * column

    def add_norm(l, col, grad, nhat):
        ngrad[pl.ds(l * 8 + col, 1), :] = jnp.sum(grad * nhat, axis=0, keepdims=True)
        ngrad[pl.ds(l * 8 + col + 1, 1), :] = jnp.sum(grad, axis=0, keepdims=True)

    def gm_mate(l, at):
        return remote(wm.at[l + 1, 1 - k, at], gmr.at[at], mgm_s.at[l, at], mgm_r.at[l, at], mate)

    def ga_all(l):
        dst = wa.at[l + 1]
        rows = 2 * N * RW

        def chunk(i, carry):
            off = pl.multiple_of(i * rows, LANES)
            grad_a = dot_tn(a1[l, :, :, pl.ds(off, rows)].reshape(T, rows), dqkv[...])
            grad_p = dot_tn(db[:, :, pl.ds(off, rows)].reshape(T, rows), att[l].reshape(T, FQ))
            dst[i, :, :, :, 0 : 3 * FQ] = grad_a.astype(BF).reshape(2, N, RW, 3 * FQ)
            dst[i, :, :, :, 3 * FQ : 4 * FQ] = grad_p.astype(BF).reshape(2, N, RW, FQ)
            return carry

        lax.fori_loop(0, C, chunk, 0)

    def ga_mate(l):
        return remote(wa.at[l + 1, :, 1 - k], gar, mga_s.at[l], mga_r.at[l], mate)

    def zpart(kind, l, at):
        return wm.at[l + 1, k, at] if kind else wa.at[l + 1, :, k, at]

    def zbuf(kind, l, slot):
        return gmz.at[l, slot] if kind else gaz.at[l, slot]

    def zg_copy(kind, l, owner, device, send, recv):
        ssem, rsem = zg_s.at[2 * l + kind, send], zg_r.at[2 * l + kind, recv]
        return remote(zpart(kind, l, owner), zbuf(kind, l, recv), ssem, rsem, zdev(device))

    def z_direct(kind, l, d):
        return zg_copy(kind, l, n + d, n + d, d + N - 1, (-d) % N - 1)

    def z_beyond(kind, l, d):
        sign = 1 if d > 0 else -1
        return zg_copy(kind, l, n + d, n + d - sign * REACH, d + N - 1, N - 1 + abs(d) - REACH - 1)

    def z_spread(kind, l):
        for d in signed(1, N - 1):
            ready = inside(n + d)
            if abs(d) == REACH:
                ready = ready & jnp.logical_not(inside(n - d // REACH))

            @pl.when(ready)
            def _(d=d):
                (z_beyond if abs(d) > REACH else z_direct)(kind, l, d).start()

    def z_relay(kind, l):
        for sign in (1, -1):
            owner = n + sign * REACH

            @pl.when(inside(owner) & inside(n - sign))
            def _(sign=sign, owner=owner):
                part = zpart(kind, l, owner)
                for q in range(1, REACH):
                    @pl.when(inside(n - sign * q))
                    def _(q=q):
                        slot = N - 1 + q - 1
                        zg_copy(kind, l, n, n, 0, slot).wait_recv()
                        part[...] = (part[...].astype(F32) + zbuf(kind, l, slot)[...].astype(F32)).astype(BF)
                z_direct(kind, l, sign * REACH).start()

    def z_arrive(kind, l, add):
        for d in reversed(signed(1, REACH)):
            @pl.when(inside(n + d))
            def _(d=d):
                slot = d % N - 1
                zg_copy(kind, l, n, n, 0, slot).wait_recv()
                add(zbuf(kind, l, slot))

    def z_drain(kind, l):
        for d in signed(1, N - 1):
            @pl.when(inside(n + d))
            def _(d=d):
                (z_beyond if abs(d) > REACH else z_direct)(kind, l, d).wait_send()

    def gm_add(l, at):
        gm_mate(l, at).wait_recv()
        src = wm.at[l + 1]
        src[k, at] = (src[k, at].astype(F32) + gmr[at].astype(F32)).astype(BF)
        dist = jnp.where(at > n, at - n, n - at)
        sign = jnp.where(at > n, 1, -1)
        beyond = dist > REACH
        device = jnp.where(beyond, at - sign * REACH, at)
        slot = jnp.where(beyond, N - 2 + dist - REACH, lax.rem(n - at + N, N) - 1)

        @pl.when((dist != 0) & ((dist != REACH) | jnp.logical_not(inside(n - sign))))
        def _():
            zg_copy(1, l, at, device, at - n + N - 1, slot).start()

    def gm_all(l):
        dst = wm.at[l + 1]
        per = UNITS // US
        count = HALF // UNITS
        far = flipped(n, N - 1, N)

        def chunk(i, carry):
            core = jnp.where(i < count, 1 - k, k)
            at = flipped(far // per, lax.rem(i, count), count)
            off = pl.multiple_of(core * HALF + at * UNITS, LANES)
            up = dot_tn(dpre_s[:, pl.ds(off, UNITS)], a3[l].reshape(T, D))
            down = dot_tn(hid_s[:, pl.ds(off, UNITS)], dm[...].reshape(T, D))
            rows = pl.ds(at * per, per)
            dst[core, rows, :, 0:D] = up.astype(BF).reshape(per, US, D)
            dst[core, rows, :, D : 2 * D] = down.astype(BF).reshape(per, US, D)

            def owners(e, carry):
                owner = at * per + flipped(lax.rem(far, per), e, per)

                @pl.when(i < count)
                def _():
                    gm_mate(l, owner).start()

                @pl.when(i >= count)
                def _():
                    gm_add(l, owner)

                return carry

            lax.fori_loop(0, per, owners, 0)
            return carry

        lax.fori_loop(0, 2 * count, chunk, 0)

    def ga_spread(l):
        ga_mate(l).wait_recv()
        src = wa.at[l + 1]
        src[:, k] = (src[:, k].astype(F32) + gar[...].astype(F32)).astype(BF)
        z_spread(0, l)

    def gm_out(l):
        return local(stage, out_mlp.at[l], loc.at[2 * LAYERS + l])

    def gm_finish(l):
        stage[...] = wm[l + 1, k, n].astype(F32)

        def add(ref):
            stage[...] += ref[...].astype(F32)

        z_arrive(1, l, add)
        gm_out(l).start()
        z_drain(1, l)
        for at in range(N):
            gm_mate(l, at).wait_send()

    def xg(l, j):
        return remote(gax_s.at[j - 1], gax_r.at[l, j - 1], xg_s.at[l], xg_r.at[l], xy(j))

    def place(l, at, value):
        for part in range(3):
            cols = pl.ds(pl.multiple_of(part * D + at * FQ, LANES), FQ)
            held_qkv[:, cols] = value[:, part * FQ : (part + 1) * FQ]
        held_proj[:, pl.ds(pl.multiple_of(at * FQ, LANES), FQ)] = value[:, 3 * FQ : 4 * FQ]

    def ga_finish(l):
        stage_a[...] = wa[l + 1, :, k, n].astype(F32)

        def add(ref):
            stage_a[...] += ref[...].astype(F32)

        z_arrive(0, l, add)
        z_drain(0, l)
        ga_mate(l).wait_send()
        for j in range(1, C):
            gax_s[j - 1] = stage_a[chip(j)].astype(BF)
            xg(l, j).start()
        place(l, c, stage_a[c])

    def ga_out(l):
        return (
            local(held_qkv, out_qkv.at[l], fin.at[2 * l]),
            local(held_proj, out_proj.at[l], fin.at[2 * l + 1]),
        )

    def ga_place(l):
        remote(gax_s, gax_r.at[l], xg_s.at[l], xg_r.at[l], mate).wait()
        for j in range(1, C):
            place(l, chip(j), gax_r[l, j - 1].astype(F32))
        for copy in ga_out(l):
            copy.start()

    def backward(i, carry):
        l = LAYERS - 1 - i
        p = 2 * LAYERS + 2 * i
        grad = g[...]
        nhat, rstd = normalize(mo[l])
        ag_start(p, dm, norm_back(nhat, rstd, grad, gain(l, 6)).astype(BF))
        add_norm(l, 6, grad, nhat)

        @pl.when(i == 0)
        def _():
            outh_s[...] = (mid[l] + nhat * gain(l, 6) + gain(l, 7)).astype(BF)
            out_z("start")

        ag_pass(p, dm)

        @pl.when((i == 0) & holder)
        def _():
            grad_z("sent")


        def redo(i, carry):
            pre = dot_nt(a3[l, pl.ds(2 * i, 2)].reshape(2 * TB, D), w_up(l))
            rows = pl.ds(i * 2 * TB, 2 * TB)
            pre_s[rows, :] = pre
            hid_s[rows, :] = gelu(pre).astype(BF)
            return carry

        lax.fori_loop(0, C // 2, redo, 0)

        @pl.when(i > 0)
        def _():
            z_relay(0, l + 1)


        def feed_back(i, pair):
            where = [pl.ds(b * TB, TB) for b in pair]
            pre = jnp.concatenate([pre_s[rows, :] for rows in where], axis=0)
            slope = (dot_nt(both(dm, pair), w_down(l)) * gelu_slope(pre)).astype(BF)
            for e, rows in enumerate(where):
                dpre_s[rows, :] = slope[e * TB : (e + 1) * TB]
            value = dot_nn(slope, w_up(l))
            if SPLIT:
                half_put(p, jnp.where(i == 0, 3, 2), value[0:TB])
                half_put(p, jnp.where(i == 0, 1, 0), value[TB:])
            else:
                rs_pair(p, i, value)

        arrivals(p, dm, feed_back)

        @pl.when(i > 0)
        def _():
            pl.semaphore_wait(credit.at[1], 1)

        gm_all(l)
        if SPLIT:
            half_pass(p)

        @pl.when(l > 0)
        def _():
            pl.semaphore_signal(credit.at[1], inc=1, device_id=mate, device_id_type=MESH)

        d_a3 = (rs_halves_finish if SPLIT else rs_finish)(p)
        nhat, rstd = normalize(mid[l])
        d_mid = g[...] + norm_back(nhat, rstd, d_a3, gain(l, 4))
        g[...] = d_mid
        nhat_b, rstd_b = normalize(br[l])
        ag_start(p + 1, db, norm_back(nhat_b, rstd_b, d_mid, gain(l, 2)).astype(BF))
        add_norm(l, 4, d_a3, nhat)
        add_norm(l, 2, d_mid, nhat_b)
        ag_drain(p, dm)
        for b in range(C):
            weights, inverse = exp_scores(l, b)
            cols = pl.ds(TB * (b * (b + 1) // 2), (b + 1) * TB)
            p_s[:, cols] = (weights * inverse).astype(BF)
        dk_s[...] = jnp.zeros_like(dk_s)
        dv_s[...] = jnp.zeros_like(dv_s)
        ag_pass(p + 1, db)
        for j in range(1, C):
            ag_wait(p + 1, db, j)
        for b in reversed(range(C)):
            size = (b + 1) * TB
            rows = pl.ds(b * TB, TB)
            seen = pl.ds(0, size)
            d_att = by_head(dot_nn(db[b], w_proj(l)).astype(BF))
            d_probs = dot_nt(d_att, vs_[l, 0 : b + 1].reshape(size, FQ))
            low = p_s[:, pl.ds(TB * (b * (b + 1) // 2), size)]
            probs = low.astype(F32)
            delta = jnp.sum(probs * d_probs, axis=-1, keepdims=True)
            d_scores = (probs * (d_probs - delta)).astype(BF)
            d_query = of_heads(dot_nn(d_scores, ks_[l, 0 : b + 1].reshape(size, FQ)))
            d_query = d_query * HEAD_DIM ** (-0.5)
            dk_s[seen, :] += dot_tn(d_scores, by_head(qs_[l, b]))
            dv_s[seen, :] += dot_tn(low, d_att)
            d_key = dk_s[rows, :]
            cosine, sine = tables(b)
            dqkv[rows, 0:FQ] = (d_query * cosine - swapped(d_query) * sine).astype(BF)
            dqkv[rows, FQ : 2 * FQ] = (d_key * cosine - swapped(d_key) * sine).astype(BF)
            dqkv[rows, 2 * FQ : 3 * FQ] = dv_s[rows, :].astype(BF)
            value = dot_nt(dqkv[rows, :], w_qkv(l))
            if SPLIT:
                j = flipped(c, block(b), C)
                half_put(p + 1, jnp.where(j == 3, 0, jnp.where(j == 0, 3, j)), value)
            else:
                rs_block(p + 1, b, value)
        z_relay(1, l)

        @pl.when(i > 0)
        def _():
            pl.semaphore_wait(credit.at[0], 1)

        ga_all(l)
        ga_mate(l).start()
        if SPLIT:
            half_pass(p + 1)

        @pl.when(i > 0)
        def _():
            gm_finish(l + 1)
            ga_finish(l + 1)

        ga_spread(l)

        @pl.when(l > 0)
        def _():
            pl.semaphore_signal(credit.at[0], inc=1, device_id=mate, device_id_type=MESH)


        @pl.when((i == LAYERS - 1) & holder)
        def _():
            out_held()
            out_plane("start")

        d_a1 = (rs_halves_finish if SPLIT else rs_finish)(p + 1)
        nhat, rstd = normalize(st[l])
        g[...] = g[...] + norm_back(nhat, rstd, d_a1, gain(l, 0))
        add_norm(l, 0, d_a1, nhat)
        ag_drain(p + 1, db)

        @pl.when(i == 0)
        def _():
            for kind in range(2):
                for at in range(LAYERS):
                    w_drain(kind, at)
            perm(0, "sent")
            grad_plane("sent")


        return carry

    lax.fori_loop(0, LAYERS, backward, 0)

    g_p[...] = g[...].astype(BF)
    n_start(1, "m", ngrad[...])

    z_relay(0, 0)
    n_start(1, "x", n_finish(1, "m"))
    gm_out(1).wait()
    gm_finish(0)
    perm(1, "start")
    n_start(1, "z", n_finish(1, "x"))
    ga_place(1)

    for copy in ga_out(1):
        copy.wait()
    ga_finish(0)
    total = n_finish(1, "z")
    for l in range(LAYERS):
        out_n[l] = lax.dot_general(
            total[l * 8 : (l + 1) * 8], spot, (((1,), (1,)), ((), ())),
            preferred_element_type=F32, precision=lax.Precision.HIGHEST,
        )
    ga_place(0)
    gm_out(0).wait()

    for l in range(LAYERS):
        for j in range(1, C):
            a2a_all(l, j).wait_send()
    perm(1, "here")
    g[...] = hid_p[...].astype(F32)
    grad_out = local(g, out_g, fin.at[2 * LAYERS])
    grad_out.start()
    perm(1, "sent")
    out_z("sent")
    out_here()

    @pl.when(holder)
    def _():
        out_plane("sent")

    for copy in ga_out(0):
        copy.wait()
    grad_out.wait()


def copy_out(*refs):
    count = (len(refs) - 1) // 3
    sems = refs[-1]
    into, out = [], []
    for i in range(count):
        src, dst, held = refs[i], refs[count + i], refs[2 * count + i]
        cuts = [()]
        if len(held.shape) == 3:
            half = held.shape[1] // 2 if held.shape[1] >= 128 else held.shape[1]
            cuts = [(l, pl.ds(at, half)) for l in range(held.shape[0]) for at in range(0, held.shape[1], half)]
        for at in cuts:
            one, two, three = (ref.at[at] if at else ref for ref in (src, held, dst))
            into.append(pltpu.make_async_copy(one, two, sems.at[2 * len(into)]))
            out.append(pltpu.make_async_copy(two, three, sems.at[2 * len(out) + 1]))
    for copy in into:
        copy.start()
    for first, second in zip(into, out):
        first.wait()
        second.start()
    for copy in out:
        copy.wait()


def body(mesh, hidden_in, w_qkv, w_proj, w_mlp, norm_params, grad_output, corpus_id, corpus_weight):
    W, N = mesh.shape["wide"], mesh.shape["narrow"]
    C = W // 2
    TB, D = hidden_in.shape
    FQ, UQ, RW, US = D // C, FF // C, D // (W * N), FF // (W * N)
    AW = 4 * FQ
    T = C * TB
    REACH = N // 2
    assert C == N and w_mlp.shape[1] == US and w_qkv.shape[1] == RW

    half = HEAD_DIM // 2
    freqs = np.float32(ROPE_BASE) ** (-np.arange(half, dtype=np.float32) / np.float32(half))
    angles = (np.arange(T, dtype=np.float32)[:, None] * freqs[None, :]).astype(np.float32)
    cosine = np.tile(np.cos(angles), (1, LANES // half)).astype(np.float32)
    sine = np.sin(angles)
    sine = np.tile(np.concatenate([-sine, sine], axis=1), (1, LANES // HEAD_DIM)).astype(np.float32)

    NR = LAYERS * 8
    dma = pltpu.SemaphoreType.DMA
    vm = pltpu.VMEM
    L = LAYERS
    scratch = [
        vm((T, LANES), F32),
        vm((T, LANES), F32),
        vm((RW, 3 * D), F32),
        vm((RW, D), F32),
        vm((L + 1, C, 2, N, RW, AW), BF),
        vm((L + 1, 2, N, US, 2 * D), BF),
        vm((L, C, TB, D), BF),
        vm((L, C, TB, D), BF),
        vm((C, TB, D), BF),
        vm((C, TB, D), BF),
        vm((L, C, TB, FQ), BF),
        vm((L, C, TB, FQ), BF),
        vm((L, C, TB, FQ), BF),
        vm((L, C, TB, FQ), BF),
        vm((L, TB, D), F32),
        vm((L, TB, D), F32),
        vm((L, TB, D), F32),
        vm((L, TB, D), F32),
        vm((T, UQ), F32),
        vm((T, UQ), BF),
        vm((T, UQ), BF),
        vm((FQ // HEAD_DIM * TB, TB * C * (C + 1) // 2), BF),
        vm((T, FQ), F32),
        vm((T, FQ), F32),
        vm((T, 3 * FQ), BF),
        vm((C - 1, TB, D), BF),
        vm((C - 1, TB, D), BF),
        vm((2, TB // 2, D), BF),
        vm((TB, D), F32),
        vm((TB, D), BF),
        vm((TB, D), BF),
        vm((8, TB), F32),
        vm((C, 8, TB), F32),
        vm((8, TB), F32),
        vm((TB, D), BF),
        vm((N, TB, D), BF),
        vm((TB, D), F32),
        vm((N, US, 2 * D), BF),
        vm((L, N + REACH - 2, US, 2 * D), BF),
        vm((US, 2 * D), F32),
        vm((C, RW, AW), F32),
        vm((C, N, RW, AW), BF),
        vm((L, N + REACH - 2, C, RW, AW), BF),
        vm((C - 1, RW, AW), BF),
        vm((L, C - 1, RW, AW), BF),
        vm((NR, D), F32),
        vm((NR, D), F32),
        vm((3, NR, D), BF),
        vm((3, C - 1, NR, D), BF),
        vm((3, NR, D), F32),
        vm((3, C - 1, NR, D), F32),
        dma((2,)), dma((2,)),
        dma((2,)), dma((2, C)),
        dma((2, C)), dma((2,)),
        dma((1,)), dma((N,)),
        dma((N,)), dma((1,)),
        dma((3 * L,)),
        dma((L, C - 1)), dma((L, C - 1)),
        dma((2, max(C - 1, 6))), dma((2, max(C - 1, 6))),
        dma((2, max(C - 1, 6))), dma((2, max(C - 1, 6))),
        dma((2 * L, 4 * REACH)), dma((2 * L, N)),
        dma((2 * L,)), dma((2 * L,)),
        dma((2 * L, 2 * N - 1)), dma((2 * L, N + REACH - 2)),
        dma((L,)), dma((L,)),
        dma((L, N)), dma((L, N)),
        dma((L,)), dma((L,)),
        dma((2,)), dma((2,)),
        dma((2,)), dma((2,)),
        dma((2,)), dma((2,)),
        dma((2 * L + 3,)),
        pltpu.SemaphoreType.REGULAR((2,)),
    ]
    vspec = pl.BlockSpec(memory_space=pltpu.VMEM)
    anyspec = pl.BlockSpec(memory_space=pl.ANY)
    shapes = (
        jax.ShapeDtypeStruct((TB, D), BF),
        jax.ShapeDtypeStruct((TB, D), F32),
        jax.ShapeDtypeStruct((L, RW, 3 * D), F32),
        jax.ShapeDtypeStruct((L, RW, D), F32),
        jax.ShapeDtypeStruct((L, US, 2 * D), F32),
        jax.ShapeDtypeStruct((L, 8, RW), F32),
    )
    outs = pl.pallas_call(
        partial(kernel_body, (C, N, TB, D, FQ, UQ, RW, US, AW)),
        out_shape=shapes,
        in_specs=[anyspec] * 2 + [vspec] * 3 + [anyspec] * 5,
        out_specs=(anyspec,) * 5 + (vspec,),
        scratch_shapes=scratch,
        compiler_params=pltpu.CompilerParams(
            collective_id=0, has_side_effects=True, vmem_limit_bytes=127 << 19
        ),
    )(
        hidden_in, grad_output, corpus_id.reshape(1, TB), corpus_weight.reshape(1, -1), norm_params.transpose(0, 2, 1),
        jnp.asarray(cosine), jnp.asarray(sine), w_qkv, w_proj, w_mlp,
    )
    outs = pl.pallas_call(
        copy_out,
        out_shape=shapes,
        in_specs=[anyspec] * len(shapes),
        out_specs=(anyspec,) * len(shapes),
        scratch_shapes=[vm(one.shape, one.dtype) for one in shapes] + [dma((4 * len(shapes),))],
        compiler_params=pltpu.CompilerParams(vmem_limit_bytes=60 << 20),
    )(*outs)
    return (*outs[:5], outs[5].transpose(0, 2, 1))


def solution(mesh):
    rows = P(("wide", "narrow"), None)
    layered = P(None, ("wide", "narrow"), None)
    return jax.shard_map(
        partial(body, mesh),
        mesh=mesh,
        in_specs=(rows, layered, layered, layered, layered, rows, P(("wide", "narrow")), P()),
        out_specs=(rows, rows, layered, layered, layered, layered),
        check_vma=False,
    )
```

```python
from functools import partial

import jax
import jax.numpy as jnp
import numpy as np
from jax import lax
from jax.experimental import pallas as pl
from jax.experimental.pallas import tpu as pltpu
from jax.sharding import PartitionSpec as P

HEADS = 16
HEAD_DIM = 64
FF = 4096
LAYERS = 2
EPS = 1e-05
MASKED = -1e30
ROPE_BASE = 10000.0
MESH = pl.DeviceIdType.MESH
BF = jnp.bfloat16
F32 = jnp.float32
LANES = 128
UNITS = 256


def dot_nn(left, right):
    return lax.dot_general(left, right, (((1,), (0,)), ((), ())), preferred_element_type=F32)


def dot_nt(left, right):
    return lax.dot_general(left, right, (((1,), (1,)), ((), ())), preferred_element_type=F32)


def dot_tn(left, right):
    return lax.dot_general(left, right, (((0,), (0,)), ((), ())), preferred_element_type=F32)


def normalize(inputs):
    centre = jnp.mean(inputs, axis=-1, keepdims=True)
    centered = inputs - centre
    rstd = lax.rsqrt(jnp.mean(centered * centered, axis=-1, keepdims=True) + EPS)
    return centered * rstd, rstd


def norm_back(nhat, rstd, grad, gain):
    scaled = grad * gain
    mean_f = jnp.mean(scaled, axis=-1, keepdims=True)
    mean_fn = jnp.mean(scaled * nhat, axis=-1, keepdims=True)
    return rstd * (scaled - mean_f - nhat * mean_fn)


GELU_S = 0.7978845608028654
GELU_A = 0.044715


def gelu(pre):
    return 0.5 * pre * (1.0 + jnp.tanh(GELU_S * (pre + GELU_A * pre * pre * pre)))


def gelu_slope(pre):
    square = pre * pre
    turned = jnp.tanh(GELU_S * (pre + GELU_A * pre * square))
    inner = GELU_S * (1.0 + 3.0 * GELU_A * square)
    return 0.5 * (1.0 + turned) + 0.5 * pre * (1.0 - turned * turned) * inner


def kernel_body(
    dims,
    hid_ref, gout_ref, ids_ref, cw_ref, nrm_ref, cos_in, sin_in, wq_ref, wp_ref, wm_ref,
    out_h, out_g, out_qkv, out_proj, out_mlp, out_n,
    cos_ref, sin_ref, held_qkv, held_proj,
    wa, wm, a1, a3, dm, db, qs_, ks_, vs_, att, st, br, mid, mo,
    pre_s, hid_s, dpre_s, p_s, dk_s, dv_s, dqkv,
    rs_send, rs_recv, rs_mid, acc, hid_p, g_p, sc_own, sc_x, sc_p, outh_s, hx, g,
    gmr, gmz, stage, stage_a, gar, gaz, gax_s, gax_r,
    npar, ngrad, nf_send, nf_recv, nb_send, nb_recv,
    perm_s, perm_r, gp_s, gp_r, gz_s, gz_r, oz_s, oz_r, op_s, op_r, loc, a2a_s, a2a_r, ag_s, ag_r, rs_s, rs_r,
    zw_s, zw_r, mw_s, mw_r, zg_s, zg_r, mga_s, mga_r, mgm_s, mgm_r, xg_s, xg_r,
    nx_s, nx_r, nz_s, nz_r, nm_s, nm_r, fin, credit,
):
    C, N, TB, D, FQ, UQ, RW, US, AW = dims
    T = C * TB
    HPC = FQ // HEAD_DIM
    HALF = N * US
    REACH = N // 2
    w = lax.axis_index("wide")
    n = lax.axis_index("narrow")
    c = w // 2
    k = lax.rem(w, 2)
    mate = (2 * c + (1 - k), n)
    to_chip = n + k * (N - 1 - 2 * n)
    to_plane = c + k * (N - 1 - 2 * c)
    swap = (2 * to_chip + k, to_plane)
    moves = to_chip != c

    def block(at):
        return at + k * (C - 1 - 2 * at)

    mine = block(c)

    def flipped(base, j, count):
        out, bit = 0, 1
        while bit < count:
            ours = lax.rem(base // bit, 2)
            flip = (j // bit) % 2 if isinstance(j, int) else lax.rem(j // bit, 2)
            out = out + bit * (ours + flip - 2 * ours * flip)
            bit *= 2
        return out

    def chip(j):
        return flipped(c, j, C)

    def xy(j):
        return (2 * chip(j) + k, n)

    def zdev(at):
        return (w, at)

    def remote(src, dst, ssem, rsem, device):
        return pltpu.make_async_remote_copy(
            src_ref=src, dst_ref=dst, send_sem=ssem, recv_sem=rsem,
            device_id=device, device_id_type=MESH,
        )

    def local(src, dst, sem):
        return pltpu.make_async_copy(src, dst, sem)

    barrier = pltpu.get_barrier_semaphore()
    partners = [xy(j) for j in range(1, C)] + [mate]
    partners += [zdev(lax.rem(n + j, N)) for j in range(1, N)]
    for device in partners:
        pl.semaphore_signal(barrier, inc=1, device_id=device, device_id_type=MESH)

    @pl.when(moves)
    def _():
        pl.semaphore_signal(barrier, inc=1, device_id=swap, device_id_type=MESH)

    pl.semaphore_wait(barrier, len(partners) + jnp.where(moves, 1, 0))

    rope = (
        local(cos_in, cos_ref, fin.at[2 * LAYERS + 1]), local(sin_in, sin_ref, fin.at[2 * LAYERS + 2])
    )
    for copy in rope:
        copy.start()

    def either(far, src, dst, ssem, rsem, device, act):
        @pl.when(far)
        def _():
            getattr(remote(src, dst, ssem, rsem, device), {"here": "wait_recv", "sent": "wait_send"}.get(act, act))()

        if act != "sent":
            @pl.when(jnp.logical_not(far))
            def _():
                getattr(local(src, dst, rsem), {"here": "wait"}.get(act, act))()

    def perm(i, act):
        src, dst = ((hid_ref, hid_p), (g_p, hid_p))[i]
        either(moves, src, dst, perm_s.at[i], perm_r.at[i], swap, act)

    holder = c == to_chip

    def grad_plane(act):
        for e, (src, dst) in enumerate(((gout_ref, db.at[c]), (sc_own, sc_x.at[c]))):
            either(jnp.logical_not(holder), src, dst, gp_s.at[e], gp_r.at[e, c], (2 * to_chip + k, n), act)

    def grad_held():
        for at in range(C):
            for e, dst in enumerate((db.at[at], sc_x.at[at])):
                either(c != at, dst, dst, gp_s.at[e], gp_r.at[e, at], (2 * at + k, n), "here")

    def grad_z(act):
        for at in range(C):
            plane = at + k * (N - 1 - 2 * at)
            for e, (src, dst) in enumerate(((db.at[at], g_p), (sc_x.at[at], sc_p))):
                either(plane != n, src, dst, gz_s.at[e, at], gz_r.at[e], (w, plane), act)

    def grad_here():
        for e, dst in enumerate((g_p, sc_p)):
            either(to_plane != n, dst, dst, gz_s.at[e, 0], gz_r.at[e], (w, to_plane), "here")

    def out_z(act):
        either(to_plane != n, outh_s, hx.at[n], oz_s.at[0], oz_r.at[n], (w, to_plane), act)

    def out_held():
        for at in range(N):
            either(n != at, hx.at[at], hx.at[at], oz_s.at[0], oz_r.at[at], (w, at), "here")

    def out_plane(act):
        for at in range(N):
            dest = at + k * (N - 1 - 2 * at)
            either(dest != c, hx.at[at], out_h, op_s.at[at], op_r.at[0], (2 * dest + k, n), act)

    def out_here():
        either(jnp.logical_not(holder), hx.at[0], out_h, op_s.at[0], op_r.at[0], (2 * to_chip + k, n), "here")

    perm(0, "start")

    def n_copy(way, axis, j):
        send, heard = (nf_send, nf_recv) if way == 0 else (nb_send, nb_recv)
        slot = n_slot[axis]
        if axis == "x":
            return remote(send.at[slot], heard.at[slot, j - 1], nx_s.at[way], nx_r.at[way], xy(j))
        if axis == "z":
            there = zdev(lax.rem(n + j, N))
            return remote(send.at[slot], heard.at[slot, j - 1], nz_s.at[way], nz_r.at[way], there)
        return remote(send.at[slot], heard.at[slot, j - 1], nm_s.at[way], nm_r.at[way], mate)

    n_count = {"x": C, "z": N, "m": 2}
    n_slot = {"x": 0, "z": 1, "m": 2}

    def n_start(way, axis, value):
        send = nf_send if way == 0 else nb_send
        send[n_slot[axis]] = value.astype(send.dtype)
        for j in range(1, n_count[axis]):
            n_copy(way, axis, j).start()

    def n_finish(way, axis):
        send, heard = (nf_send, nf_recv) if way == 0 else (nb_send, nb_recv)
        total = send[n_slot[axis]].astype(F32)
        whole = heard.at[n_slot[axis], pl.ds(0, n_count[axis] - 1)]
        ssem, rsem = {"x": (nx_s, nx_r), "z": (nz_s, nz_r), "m": (nm_s, nm_r)}[axis]
        remote(whole, whole, ssem.at[way], rsem.at[way], mate).wait()
        for j in range(1, n_count[axis]):
            total = total + heard[n_slot[axis], j - 1].astype(F32)
        return total

    first = (w * N + n) * RW
    spot = lax.broadcasted_iota(jnp.int32, (RW, D), 1) == (
        lax.broadcasted_iota(jnp.int32, (RW, D), 0) + first
    )
    spot = spot.astype(F32)
    n_start(0, "x", jnp.concatenate(
        [dot_nn(nrm_ref[l], spot.astype(BF)) for l in range(LAYERS)], axis=0
    ))

    def pieces(l, at):
        for part in range(3):
            cols = pl.ds(pl.multiple_of(part * D + at * FQ, LANES), FQ)
            yield wq_ref.at[l, :, cols], wa.at[l, c, k, n, :, pl.ds(part * FQ, FQ)]
        cols = pl.ds(pl.multiple_of(at * FQ, LANES), FQ)
        yield wp_ref.at[l, :, cols], wa.at[l, c, k, n, :, pl.ds(3 * FQ, FQ)]

    def a2a_start(l):
        for j in range(1, C):
            for src, dst in pieces(l, chip(j)):
                remote(src, dst, a2a_s.at[l, j - 1], a2a_r.at[l, j - 1], xy(j)).start()

    def a2a_all(l, j):
        there = wa.at[l, chip(j), k, n]
        return remote(there, there, a2a_s.at[l, j - 1], a2a_r.at[l, j - 1], xy(j))

    def own_wa(l):
        mine = wa.at[l, c, k, n]
        return local(mine, mine, loc.at[l])

    def own_wm(l):
        return local(wm_ref.at[l], wm.at[l, k, n], loc.at[LAYERS + l])

    a2a_start(0)
    for l in range(LAYERS):
        for src, dst in pieces(l, c):
            local(src, dst, loc.at[l]).start()
        own_wm(l).start()

    def shard(kind, l, core, at):
        return wm.at[l, core, at] if kind else wa.at[l, :, core, at]

    def inside(at):
        return (at >= 0) & (at < N)

    def signed(least, most):
        return [sign * d for d in range(most, least - 1, -1) for sign in (1, -1)]

    def zw_copy(kind, l, origin, at, slot):
        rows = shard(kind, l, k, origin)
        return remote(rows, rows, zw_s.at[2 * l + kind, slot], zw_r.at[2 * l + kind, origin], zdev(at))

    def direct_slot(d):
        return d + REACH

    def relay_slot(sign, q):
        return 2 * REACH + (q if sign > 0 else q + REACH - 1)

    def to_mate(kind, l, at):
        rows = shard(kind, l, k, at)
        return remote(rows, rows, mw_s.at[2 * l + kind], mw_r.at[2 * l + kind], mate)

    def mate_half(kind, l, core):
        rows = wm.at[l, core] if kind else wa.at[l, :, core]
        return remote(rows, rows, mw_s.at[2 * l + kind], mw_r.at[2 * l + kind], mate)

    def w_send(kind, l):
        for d in signed(1, REACH):
            @pl.when(inside(n + d))
            def _(d=d):
                zw_copy(kind, l, n, n + d, direct_slot(d)).start()

        to_mate(kind, l, n).start()

    def w_relay(kind, l):
        for sign in (1, -1):
            origin = n - sign * REACH

            @pl.when(inside(origin) & inside(n + sign))
            def _(sign=sign, origin=origin):
                zw_copy(kind, l, origin, n, 0).wait_recv()
                for q in range(1, REACH):
                    @pl.when(inside(n + sign * q))
                    def _(q=q):
                        zw_copy(kind, l, origin, n + sign * q, relay_slot(sign, q)).start()

    def w_arrive(kind, l):
        for d in reversed(signed(1, N - 1)):
            origin = n + d

            @pl.when(inside(origin))
            def _(d=d, origin=origin):
                if abs(d) == REACH:
                    sign = -1 if d > 0 else 1

                    @pl.when(jnp.logical_not(inside(n + sign)))
                    def _():
                        zw_copy(kind, l, origin, n, 0).wait_recv()
                else:
                    zw_copy(kind, l, origin, n, 0).wait_recv()
                to_mate(kind, l, origin).start()

    def w_ready(kind, l):
        mate_half(kind, l, 1 - k).wait_recv()

    def w_drain(kind, l):
        for d in signed(1, REACH):
            @pl.when(inside(n + d))
            def _(d=d):
                zw_copy(kind, l, n, n + d, direct_slot(d)).wait_send()

        for sign in (1, -1):
            origin = n - sign * REACH
            for q in range(1, REACH):
                @pl.when(inside(origin) & inside(n + sign) & inside(n + sign * q))
                def _(sign=sign, origin=origin, q=q):
                    zw_copy(kind, l, origin, n + sign * q, relay_slot(sign, q)).wait_send()

        mate_half(kind, l, k).wait_send()

    n_start(0, "z", n_finish(0, "x"))
    own_wa(0).wait()
    for j in range(1, C):
        a2a_all(0, j).wait_recv()
    w_send(0, 0)
    n_start(0, "m", n_finish(0, "z"))
    npar[...] = n_finish(0, "m")
    ngrad[...] = jnp.zeros_like(ngrad)

    def gain(l, col):
        return npar[pl.ds(l * 8 + col, 1), :]

    SPLIT = C == 4
    hops = ((1, 0), (1, 1), (2, 1), (2, 0), (2, 0), (1, 1))

    def ag_copy(p, buf, source, slot):
        if not SPLIT:
            rows = buf.at[block(source)]
            return remote(rows, rows, ag_s.at[lax.rem(p, 2), slot], ag_r.at[lax.rem(p, 2), slot], xy(slot + 1))
        j, part = hops[slot]
        rows = buf.at[block(source), pl.ds(part * (TB // 2), TB // 2)]
        return remote(rows, rows, ag_s.at[lax.rem(p, 2), slot], ag_r.at[lax.rem(p, 2), slot], xy(j))

    def ag_start(p, buf, value):
        buf[mine] = value
        for slot in (0, 2, 1, 3) if SPLIT else range(C - 1):
            ag_copy(p, buf, c, slot).start()

    def ag_pass(p, buf):
        if SPLIT:
            ag_copy(p, buf, chip(1), 0).wait_recv()
            ag_copy(p, buf, chip(1), 4).start()
            ag_copy(p, buf, chip(2), 2).wait_recv()
            ag_copy(p, buf, chip(2), 5).start()

    def ag_wait(p, buf, j):
        for slot in ((), (1,), (3,), (4, 5))[j] if SPLIT else (j - 1,) * min(j, 1):
            ag_copy(p, buf, chip(j), slot).wait_recv()

    def ag_drain(p, buf):
        for slot in range(4) if SPLIT else range(C - 1):
            ag_copy(p, buf, c, slot).wait_send()
        if SPLIT:
            ag_copy(p, buf, chip(1), 4).wait_send()
            ag_copy(p, buf, chip(2), 5).wait_send()

    def rs_copy(p, j):
        return remote(rs_send.at[j - 1], rs_recv.at[j - 1], rs_s.at[lax.rem(p, 2), j - 1], rs_r.at[lax.rem(p, 2), j - 1], xy(j))

    def rs_put(p, j, value):
        @pl.when(j > 0)
        def _():
            rs_send[j - 1] = value.astype(BF)
            rs_copy(p, j).start()

        @pl.when(j == 0)
        def _():
            acc[...] = value

    def rs_block(p, b, value):
        rs_put(p, chip(block(b)), value)

    def rs_pair(p, i, value):
        rs_put(p, 2 * i, value[0:TB])
        rs_send[2 * i] = value[TB:].astype(BF)
        rs_copy(p, 2 * i + 1).start()

    def half_copy(p, slot):
        part = pl.ds((0, 1, 1, 0, 0, 1)[slot] * (TB // 2), TB // 2)
        src = rs_send.at[(0, 0, 1, 1, 2, 2)[slot], part]
        dst = rs_mid.at[slot - 4] if slot >= 4 else rs_recv.at[(0, 0, 1, 1)[slot], part]
        return remote(src, dst, rs_s.at[lax.rem(p, 2), slot], rs_r.at[lax.rem(p, 2), slot], xy((1, 1, 2, 2, 1, 2)[slot]))

    def half_put(p, i, value):
        @pl.when(i == 0)
        def _():
            rs_send[2] = value.astype(BF)
            half_copy(p, 4).start()
            half_copy(p, 5).start()

        @pl.when(i == 1)
        def _():
            rs_send[0] = value.astype(BF)
            half_copy(p, 0).start()

        @pl.when(i == 2)
        def _():
            rs_send[1] = value.astype(BF)
            half_copy(p, 2).start()

        @pl.when(i == 3)
        def _():
            acc[...] = value

    def half_chip(i):
        return chip(jnp.where(i == 0, 3, jnp.where(i == 3, 0, i)))

    def half_pass(p):
        for slot, at, rows, onward in ((4, 1, pl.ds(0, TB // 2), 3), (5, 0, pl.ds(TB // 2, TB // 2), 1)):
            half_copy(p, slot).wait_recv()
            rs_send[at, rows] = (rs_send[at, rows].astype(F32) + rs_mid[slot - 4].astype(F32)).astype(BF)
            half_copy(p, onward).start()

    def rs_halves_finish(p):
        for slot in range(4):
            half_copy(p, slot).wait()
        half_copy(p, 4).wait_send()
        half_copy(p, 5).wait_send()
        return acc[...] + rs_recv[0].astype(F32) + rs_recv[1].astype(F32)

    def arrivals(p, buf, use):
        def step(i, carry):
            for at in range(C // 2):
                @pl.when(i == at)
                def _(at=at):
                    ag_wait(p, buf, 2 * at)
                    ag_wait(p, buf, 2 * at + 1)

            use(i, (block(chip(2 * i)), block(chip(2 * i + 1))))
            return carry

        lax.fori_loop(0, C // 2, step, 0)

    def both(ref, pair):
        return jnp.concatenate([ref[b] for b in pair], axis=0)

    def rs_finish(p):
        total = acc[...]
        for j in range(1, C):
            rs_copy(p, j).wait()
            total = total + rs_recv[j - 1].astype(F32)
        return total

    lane = lax.broadcasted_iota(jnp.int32, (TB, FQ), 1)
    low_half = lax.rem(lane, HEAD_DIM) < HEAD_DIM // 2
    head_of = lane // HEAD_DIM
    causal = lax.broadcasted_iota(jnp.int32, (HPC * TB, TB), 1) <= lax.rem(
        lax.broadcasted_iota(jnp.int32, (HPC * TB, TB), 0), TB
    )

    def tables(b):
        rows = pl.ds(b * TB, TB)
        reps = FQ // LANES
        return (
            jnp.concatenate([cos_ref[rows, :]] * reps, axis=1),
            jnp.concatenate([sin_ref[rows, :]] * reps, axis=1),
        )

    def swapped(u):
        half_dim = HEAD_DIM // 2
        return jnp.where(
            low_half, pltpu.roll(u, FQ - half_dim, 1), pltpu.roll(u, half_dim, 1)
        )

    def w_qkv(l):
        return wa[l, :, :, :, :, 0 : 3 * FQ].reshape(D, 3 * FQ)

    def w_proj(l):
        return wa[l, :, :, :, :, 3 * FQ : 4 * FQ].reshape(D, FQ)

    def w_up(l):
        return wm[l, :, :, :, 0:D].reshape(UQ, D)

    def w_down(l):
        return wm[l, :, :, :, D : 2 * D].reshape(UQ, D)

    def by_head(rows):
        return jnp.concatenate(
            [jnp.where(head_of == h, rows, jnp.zeros((), rows.dtype)) for h in range(HPC)], axis=0
        )

    def of_heads(stacked):
        out = stacked[0:TB]
        for h in range(1, HPC):
            out = jnp.where(head_of == h, stacked[h * TB : (h + 1) * TB], out)
        return out

    def exp_scores(l, b):
        scores = dot_nt(by_head(qs_[l, b]), ks_[l, 0 : b + 1].reshape((b + 1) * TB, FQ))
        last = jnp.where(causal, scores[:, b * TB :], MASKED)
        scores = jnp.concatenate([scores[:, : b * TB], last], axis=1) if b else last
        weights = jnp.exp(scores - jnp.max(scores, axis=-1, keepdims=True))
        return weights, 1.0 / jnp.sum(weights, axis=-1, keepdims=True)

    w_relay(0, 0)
    own_wm(0).wait()
    w_send(1, 0)
    perm(0, "here")
    st[0] = hid_p[...].astype(F32)
    ids = jnp.broadcast_to(ids_ref[...], (8, TB))
    scale = jnp.zeros((8, TB), F32)
    for i in range(cw_ref.shape[1]):
        scale = jnp.where(ids == i, cw_ref[:, i : i + 1], scale)
    sc_own[...] = scale
    for copy in rope:
        copy.wait()

    def grad_move():
        @pl.when(holder)
        def _():
            grad_held()
            grad_z("start")

    def forward(l, carry):
        p = 2 * l
        more = l + 1 < LAYERS
        nhat, unused = normalize(st[l])
        ag_start(p, a1.at[l], (nhat * gain(l, 0) + gain(l, 1)).astype(BF))

        @pl.when(l == 0)
        def _():
            a2a_start(1)

        ag_pass(p, a1.at[l])

        @pl.when(l == 0)
        def _():
            grad_plane("start")

        w_arrive(0, l)
        w_ready(0, l)

        def qkv_step(i, pair):
            u = dot_nn(both(a1.at[l], pair), w_qkv(l))
            for e, b in enumerate(pair):
                cosine, sine = tables(b)
                uq = u[e * TB : (e + 1) * TB, 0:FQ]
                uk = u[e * TB : (e + 1) * TB, FQ : 2 * FQ]
                uq = (uq * cosine + swapped(uq) * sine).astype(BF)
                qs_[l, b] = (uq * HEAD_DIM ** (-0.5)).astype(BF)
                ks_[l, b] = (uk * cosine + swapped(uk) * sine).astype(BF)
                vs_[l, b] = u[e * TB : (e + 1) * TB, 2 * FQ :].astype(BF)

        arrivals(p, a1.at[l], qkv_step)
        def attend(b):
            weights, inverse = exp_scores(l, b)
            mixed = dot_nn(weights.astype(BF), vs_[l, 0 : b + 1].reshape((b + 1) * TB, FQ))
            low = of_heads(mixed * inverse).astype(BF)
            att[l, b] = low
            return dot_nt(low, w_proj(l))

        if SPLIT:

            def attend_step(i, carry):
                for b in range(C):
                    @pl.when(block(half_chip(i)) == b)
                    def _(b=b):
                        acc[...] = attend(b)

                half_put(p, i, acc[...])
                return carry

            lax.fori_loop(0, C, attend_step, 0)
            half_pass(p)
        else:
            for b in range(C):
                rs_block(p, b, attend(b))
        w_relay(1, l)

        @pl.when(more)
        def _():
            own_wa(l + 1).wait()
            for j in range(1, C):
                a2a_all(l + 1, j).wait_recv()
            w_send(0, l + 1)

        branch = (rs_halves_finish if SPLIT else rs_finish)(p)
        br[l] = branch
        nhat, unused = normalize(branch)
        middle = st[l] + nhat * gain(l, 2) + gain(l, 3)
        mid[l] = middle
        nhat, unused = normalize(middle)
        ag_start(p + 1, a3.at[l], (nhat * gain(l, 4) + gain(l, 5)).astype(BF))
        ag_drain(p, a1.at[l])
        ag_pass(p + 1, a3.at[l])
        w_arrive(1, l)


        def feed(x, core):
            up = wm[l, core, :, :, 0:D].reshape(N * US, D)
            down = wm[l, core, :, :, D : 2 * D].reshape(N * US, D)
            return dot_nn(gelu(dot_nt(x, up)).astype(BF), down)

        if SPLIT:
            for j in range(1, C):
                ag_wait(p + 1, a3.at[l], j)
            pre_s[...] = feed(a3[l].reshape(T, D), k)
            w_ready(1, l)

            def feed_step(i, carry):
                pair = (block(half_chip(2 * i)), block(half_chip(2 * i + 1)))
                value = feed(both(a3.at[l], pair), 1 - k)
                value = value + jnp.concatenate([pre_s[pl.ds(b * TB, TB), :] for b in pair], axis=0)
                half_put(p + 1, 2 * i, value[0:TB])
                half_put(p + 1, 2 * i + 1, value[TB:])
                return carry

            lax.fori_loop(0, 2, feed_step, 0)

            @pl.when(jnp.logical_not(more))
            def _():
                grad_move()

            half_pass(p + 1)
        else:
            @pl.when(jnp.logical_not(more))
            def _():
                grad_move()

            w_ready(1, l)
            arrivals(p + 1, a3.at[l], lambda i, pair: rs_pair(
                p + 1, i, feed(both(a3.at[l], pair), k) + feed(both(a3.at[l], pair), 1 - k)
            ))

        @pl.when(more)
        def _():
            w_relay(0, l + 1)
            own_wm(l + 1).wait()
            w_send(1, l + 1)

        mlp_out = (rs_halves_finish if SPLIT else rs_finish)(p + 1)
        mo[l] = mlp_out

        @pl.when(more)
        def _():
            nhat, unused = normalize(mlp_out)
            st[l + 1] = mid[l] + nhat * gain(l, 6) + gain(l, 7)

        ag_drain(p + 1, a3.at[l])
        return carry

    lax.fori_loop(0, LAYERS, forward, 0)
    def add_norm(l, col, grad, nhat):
        ngrad[pl.ds(l * 8 + col, 1), :] = jnp.sum(grad * nhat, axis=0, keepdims=True)
        ngrad[pl.ds(l * 8 + col + 1, 1), :] = jnp.sum(grad, axis=0, keepdims=True)

    def gm_mate(l, at):
        return remote(wm.at[l + 1, 1 - k, at], gmr.at[at], mgm_s.at[l, at], mgm_r.at[l, at], mate)

    def ga_all(l):
        dst = wa.at[l + 1]
        rows = 2 * N * RW

        def chunk(i, carry):
            off = pl.multiple_of(i * rows, LANES)
            grad_a = dot_tn(a1[l, :, :, pl.ds(off, rows)].reshape(T, rows), dqkv[...])
            grad_p = dot_tn(db[:, :, pl.ds(off, rows)].reshape(T, rows), att[l].reshape(T, FQ))
            dst[i, :, :, :, 0 : 3 * FQ] = grad_a.astype(BF).reshape(2, N, RW, 3 * FQ)
            dst[i, :, :, :, 3 * FQ : 4 * FQ] = grad_p.astype(BF).reshape(2, N, RW, FQ)
            return carry

        lax.fori_loop(0, C, chunk, 0)

    def ga_mate(l):
        return remote(wa.at[l + 1, :, 1 - k], gar, mga_s.at[l], mga_r.at[l], mate)

    def zpart(kind, l, at):
        return wm.at[l + 1, k, at] if kind else wa.at[l + 1, :, k, at]

    def zbuf(kind, l, slot):
        return gmz.at[l, slot] if kind else gaz.at[l, slot]

    def zg_copy(kind, l, owner, device, send, recv):
        ssem, rsem = zg_s.at[2 * l + kind, send], zg_r.at[2 * l + kind, recv]
        return remote(zpart(kind, l, owner), zbuf(kind, l, recv), ssem, rsem, zdev(device))

    def z_direct(kind, l, d):
        return zg_copy(kind, l, n + d, n + d, d + N - 1, (-d) % N - 1)

    def z_beyond(kind, l, d):
        sign = 1 if d > 0 else -1
        return zg_copy(kind, l, n + d, n + d - sign * REACH, d + N - 1, N - 1 + abs(d) - REACH - 1)

    def z_spread(kind, l):
        for d in signed(1, N - 1):
            ready = inside(n + d)
            if abs(d) == REACH:
                ready = ready & jnp.logical_not(inside(n - d // REACH))

            @pl.when(ready)
            def _(d=d):
                (z_beyond if abs(d) > REACH else z_direct)(kind, l, d).start()

    def z_relay(kind, l):
        for sign in (1, -1):
            owner = n + sign * REACH

            @pl.when(inside(owner) & inside(n - sign))
            def _(sign=sign, owner=owner):
                part = zpart(kind, l, owner)
                for q in range(1, REACH):
                    @pl.when(inside(n - sign * q))
                    def _(q=q):
                        slot = N - 1 + q - 1
                        zg_copy(kind, l, n, n, 0, slot).wait_recv()
                        part[...] = (part[...].astype(F32) + zbuf(kind, l, slot)[...].astype(F32)).astype(BF)
                z_direct(kind, l, sign * REACH).start()

    def z_arrive(kind, l, add):
        for d in reversed(signed(1, REACH)):
            @pl.when(inside(n + d))
            def _(d=d):
                slot = d % N - 1
                zg_copy(kind, l, n, n, 0, slot).wait_recv()
                add(zbuf(kind, l, slot))

    def z_drain(kind, l):
        for d in signed(1, N - 1):
            @pl.when(inside(n + d))
            def _(d=d):
                (z_beyond if abs(d) > REACH else z_direct)(kind, l, d).wait_send()

    def gm_add(l, at):
        gm_mate(l, at).wait_recv()
        src = wm.at[l + 1]
        src[k, at] = (src[k, at].astype(F32) + gmr[at].astype(F32)).astype(BF)
        dist = jnp.where(at > n, at - n, n - at)
        sign = jnp.where(at > n, 1, -1)
        beyond = dist > REACH
        device = jnp.where(beyond, at - sign * REACH, at)
        slot = jnp.where(beyond, N - 2 + dist - REACH, lax.rem(n - at + N, N) - 1)

        @pl.when((dist != 0) & ((dist != REACH) | jnp.logical_not(inside(n - sign))))
        def _():
            zg_copy(1, l, at, device, at - n + N - 1, slot).start()

    def gm_all(l):
        dst = wm.at[l + 1]
        per = UNITS // US
        count = HALF // UNITS
        far = flipped(n, N - 1, N)

        def chunk(i, carry):
            core = jnp.where(i < count, 1 - k, k)
            at = flipped(far // per, lax.rem(i, count), count)
            off = pl.multiple_of(core * HALF + at * UNITS, LANES)
            up = dot_tn(dpre_s[:, pl.ds(off, UNITS)], a3[l].reshape(T, D))
            down = dot_tn(hid_s[:, pl.ds(off, UNITS)], dm[...].reshape(T, D))
            rows = pl.ds(at * per, per)
            dst[core, rows, :, 0:D] = up.astype(BF).reshape(per, US, D)
            dst[core, rows, :, D : 2 * D] = down.astype(BF).reshape(per, US, D)

            def owners(e, carry):
                owner = at * per + flipped(lax.rem(far, per), e, per)

                @pl.when(i < count)
                def _():
                    gm_mate(l, owner).start()

                @pl.when(i >= count)
                def _():
                    gm_add(l, owner)

                return carry

            lax.fori_loop(0, per, owners, 0)
            return carry

        lax.fori_loop(0, 2 * count, chunk, 0)

    def ga_spread(l):
        ga_mate(l).wait_recv()
        src = wa.at[l + 1]
        src[:, k] = (src[:, k].astype(F32) + gar[...].astype(F32)).astype(BF)
        z_spread(0, l)

    def gm_out(l):
        return local(stage, out_mlp.at[l], loc.at[2 * LAYERS + l])

    def gm_finish(l):
        stage[...] = wm[l + 1, k, n].astype(F32)

        def add(ref):
            stage[...] += ref[...].astype(F32)

        z_arrive(1, l, add)
        gm_out(l).start()
        z_drain(1, l)
        for at in range(N):
            gm_mate(l, at).wait_send()

    def xg(l, j):
        return remote(gax_s.at[j - 1], gax_r.at[l, j - 1], xg_s.at[l], xg_r.at[l], xy(j))

    def place(l, at, value):
        for part in range(3):
            cols = pl.ds(pl.multiple_of(part * D + at * FQ, LANES), FQ)
            held_qkv[:, cols] = value[:, part * FQ : (part + 1) * FQ]
        held_proj[:, pl.ds(pl.multiple_of(at * FQ, LANES), FQ)] = value[:, 3 * FQ : 4 * FQ]

    def ga_finish(l):
        stage_a[...] = wa[l + 1, :, k, n].astype(F32)

        def add(ref):
            stage_a[...] += ref[...].astype(F32)

        z_arrive(0, l, add)
        z_drain(0, l)
        ga_mate(l).wait_send()
        for j in range(1, C):
            gax_s[j - 1] = stage_a[chip(j)].astype(BF)
            xg(l, j).start()
        place(l, c, stage_a[c])

    def ga_out(l):
        return (
            local(held_qkv, out_qkv.at[l], fin.at[2 * l]),
            local(held_proj, out_proj.at[l], fin.at[2 * l + 1]),
        )

    def ga_place(l):
        remote(gax_s, gax_r.at[l], xg_s.at[l], xg_r.at[l], mate).wait()
        for j in range(1, C):
            place(l, chip(j), gax_r[l, j - 1].astype(F32))
        for copy in ga_out(l):
            copy.start()

    def backward(i, carry):
        l = LAYERS - 1 - i
        p = 2 * LAYERS + 2 * i
        nhat, rstd = normalize(mo[l])

        @pl.when(i == 0)
        def _():
            grad_here()
            here = lax.broadcasted_iota(jnp.int32, (TB, TB), 0) == lax.broadcasted_iota(jnp.int32, (TB, TB), 1)
            column = jnp.sum(
                jnp.where(here, jnp.broadcast_to(sc_p[0:1, :], (TB, TB)), 0.0), axis=1, keepdims=True
            )
            g[...] = g_p[...].astype(F32) * column

        grad = g[...]
        ag_start(p, dm, norm_back(nhat, rstd, grad, gain(l, 6)).astype(BF))
        add_norm(l, 6, grad, nhat)

        @pl.when(i == 0)
        def _():
            outh_s[...] = (mid[l] + nhat * gain(l, 6) + gain(l, 7)).astype(BF)
            out_z("start")

        ag_pass(p, dm)

        @pl.when((i == 0) & holder)
        def _():
            grad_z("sent")


        def redo(i, carry):
            pre = dot_nt(a3[l, pl.ds(2 * i, 2)].reshape(2 * TB, D), w_up(l))
            rows = pl.ds(i * 2 * TB, 2 * TB)
            pre_s[rows, :] = pre
            hid_s[rows, :] = gelu(pre).astype(BF)
            return carry

        lax.fori_loop(0, C // 2, redo, 0)

        @pl.when(i > 0)
        def _():
            z_relay(0, l + 1)


        def feed_back(i, pair):
            where = [pl.ds(b * TB, TB) for b in pair]
            pre = jnp.concatenate([pre_s[rows, :] for rows in where], axis=0)
            slope = (dot_nt(both(dm, pair), w_down(l)) * gelu_slope(pre)).astype(BF)
            for e, rows in enumerate(where):
                dpre_s[rows, :] = slope[e * TB : (e + 1) * TB]
            value = dot_nn(slope, w_up(l))
            if SPLIT:
                half_put(p, jnp.where(i == 0, 3, 2), value[0:TB])
                half_put(p, jnp.where(i == 0, 1, 0), value[TB:])
            else:
                rs_pair(p, i, value)

        arrivals(p, dm, feed_back)

        @pl.when(i > 0)
        def _():
            pl.semaphore_wait(credit.at[1], 1)

        gm_all(l)
        if SPLIT:
            half_pass(p)

        @pl.when(l > 0)
        def _():
            pl.semaphore_signal(credit.at[1], inc=1, device_id=mate, device_id_type=MESH)

        d_a3 = (rs_halves_finish if SPLIT else rs_finish)(p)
        nhat, rstd = normalize(mid[l])
        d_mid = g[...] + norm_back(nhat, rstd, d_a3, gain(l, 4))
        g[...] = d_mid
        nhat_b, rstd_b = normalize(br[l])
        ag_start(p + 1, db, norm_back(nhat_b, rstd_b, d_mid, gain(l, 2)).astype(BF))
        add_norm(l, 4, d_a3, nhat)
        add_norm(l, 2, d_mid, nhat_b)
        ag_drain(p, dm)
        for b in range(C):
            weights, inverse = exp_scores(l, b)
            cols = pl.ds(TB * (b * (b + 1) // 2), (b + 1) * TB)
            p_s[:, cols] = (weights * inverse).astype(BF)
        dk_s[...] = jnp.zeros_like(dk_s)
        dv_s[...] = jnp.zeros_like(dv_s)
        ag_pass(p + 1, db)
        for j in range(1, C):
            ag_wait(p + 1, db, j)
        for b in reversed(range(C)):
            size = (b + 1) * TB
            rows = pl.ds(b * TB, TB)
            seen = pl.ds(0, size)
            d_att = by_head(dot_nn(db[b], w_proj(l)).astype(BF))
            d_probs = dot_nt(d_att, vs_[l, 0 : b + 1].reshape(size, FQ))
            low = p_s[:, pl.ds(TB * (b * (b + 1) // 2), size)]
            probs = low.astype(F32)
            delta = jnp.sum(probs * d_probs, axis=-1, keepdims=True)
            d_scores = (probs * (d_probs - delta)).astype(BF)
            d_query = of_heads(dot_nn(d_scores, ks_[l, 0 : b + 1].reshape(size, FQ)))
            d_query = d_query * HEAD_DIM ** (-0.5)
            dk_s[seen, :] += dot_tn(d_scores, by_head(qs_[l, b]))
            dv_s[seen, :] += dot_tn(low, d_att)
            d_key = dk_s[rows, :]
            cosine, sine = tables(b)
            dqkv[rows, 0:FQ] = (d_query * cosine - swapped(d_query) * sine).astype(BF)
            dqkv[rows, FQ : 2 * FQ] = (d_key * cosine - swapped(d_key) * sine).astype(BF)
            dqkv[rows, 2 * FQ : 3 * FQ] = dv_s[rows, :].astype(BF)
            value = dot_nt(dqkv[rows, :], w_qkv(l))
            if SPLIT:
                j = flipped(c, block(b), C)
                half_put(p + 1, jnp.where(j == 3, 0, jnp.where(j == 0, 3, j)), value)
            else:
                rs_block(p + 1, b, value)
        z_relay(1, l)

        @pl.when(i > 0)
        def _():
            pl.semaphore_wait(credit.at[0], 1)

        ga_all(l)
        ga_mate(l).start()
        if SPLIT:
            half_pass(p + 1)

        @pl.when(i > 0)
        def _():
            gm_finish(l + 1)
            ga_finish(l + 1)

        ga_spread(l)

        @pl.when(l > 0)
        def _():
            pl.semaphore_signal(credit.at[0], inc=1, device_id=mate, device_id_type=MESH)


        @pl.when((i == LAYERS - 1) & holder)
        def _():
            out_held()
            out_plane("start")

        d_a1 = (rs_halves_finish if SPLIT else rs_finish)(p + 1)
        nhat, rstd = normalize(st[l])
        g[...] = g[...] + norm_back(nhat, rstd, d_a1, gain(l, 0))
        add_norm(l, 0, d_a1, nhat)
        ag_drain(p + 1, db)

        @pl.when(i == 0)
        def _():
            for kind in range(2):
                for at in range(LAYERS):
                    w_drain(kind, at)
            perm(0, "sent")
            grad_plane("sent")


        return carry

    lax.fori_loop(0, LAYERS, backward, 0)

    g_p[...] = g[...].astype(BF)
    n_start(1, "m", ngrad[...])

    z_relay(0, 0)
    n_start(1, "x", n_finish(1, "m"))
    gm_out(1).wait()
    gm_finish(0)
    perm(1, "start")
    n_start(1, "z", n_finish(1, "x"))
    ga_place(1)

    for copy in ga_out(1):
        copy.wait()
    ga_finish(0)
    total = n_finish(1, "z")
    for l in range(LAYERS):
        out_n[l] = lax.dot_general(
            total[l * 8 : (l + 1) * 8], spot, (((1,), (1,)), ((), ())),
            preferred_element_type=F32, precision=lax.Precision.HIGHEST,
        )
    ga_place(0)
    gm_out(0).wait()

    for l in range(LAYERS):
        for j in range(1, C):
            a2a_all(l, j).wait_send()
    perm(1, "here")
    g[...] = hid_p[...].astype(F32)
    grad_out = local(g, out_g, fin.at[2 * LAYERS])
    grad_out.start()
    perm(1, "sent")
    out_z("sent")
    out_here()

    @pl.when(holder)
    def _():
        out_plane("sent")

    for copy in ga_out(0):
        copy.wait()
    grad_out.wait()


def copy_out(*refs):
    count = (len(refs) - 1) // 3
    sems = refs[-1]
    into, out = [], []
    for i in sorted(range(count), key=lambda i: -refs[i].size):
        src, dst, held = refs[i], refs[count + i], refs[2 * count + i]
        cuts = [()]
        if len(held.shape) == 3:
            half = held.shape[1] // 2 if held.shape[1] >= 128 else held.shape[1]
            cuts = [(l, pl.ds(at, half)) for l in range(held.shape[0]) for at in range(0, held.shape[1], half)]
        for at in cuts:
            one, two, three = (ref.at[at] if at else ref for ref in (src, held, dst))
            into.append(pltpu.make_async_copy(one, two, sems.at[2 * len(into)]))
            out.append(pltpu.make_async_copy(two, three, sems.at[2 * len(out) + 1]))
    for copy in into:
        copy.start()
    for first, second in zip(into, out):
        first.wait()
        second.start()
    for copy in out:
        copy.wait()


def body(mesh, hidden_in, w_qkv, w_proj, w_mlp, norm_params, grad_output, corpus_id, corpus_weight):
    W, N = mesh.shape["wide"], mesh.shape["narrow"]
    C = W // 2
    TB, D = hidden_in.shape
    FQ, UQ, RW, US = D // C, FF // C, D // (W * N), FF // (W * N)
    AW = 4 * FQ
    T = C * TB
    REACH = N // 2
    assert C == N and w_mlp.shape[1] == US and w_qkv.shape[1] == RW

    half = HEAD_DIM // 2
    freqs = np.float32(ROPE_BASE) ** (-np.arange(half, dtype=np.float32) / np.float32(half))
    angles = (np.arange(T, dtype=np.float32)[:, None] * freqs[None, :]).astype(np.float32)
    cosine = np.tile(np.cos(angles), (1, LANES // half)).astype(np.float32)
    sine = np.sin(angles)
    sine = np.tile(np.concatenate([-sine, sine], axis=1), (1, LANES // HEAD_DIM)).astype(np.float32)

    NR = LAYERS * 8
    dma = pltpu.SemaphoreType.DMA
    vm = pltpu.VMEM
    L = LAYERS
    scratch = [
        vm((T, LANES), F32),
        vm((T, LANES), F32),
        vm((RW, 3 * D), F32),
        vm((RW, D), F32),
        vm((L + 1, C, 2, N, RW, AW), BF),
        vm((L + 1, 2, N, US, 2 * D), BF),
        vm((L, C, TB, D), BF),
        vm((L, C, TB, D), BF),
        vm((C, TB, D), BF),
        vm((C, TB, D), BF),
        vm((L, C, TB, FQ), BF),
        vm((L, C, TB, FQ), BF),
        vm((L, C, TB, FQ), BF),
        vm((L, C, TB, FQ), BF),
        vm((L, TB, D), F32),
        vm((L, TB, D), F32),
        vm((L, TB, D), F32),
        vm((L, TB, D), F32),
        vm((T, UQ), F32),
        vm((T, UQ), BF),
        vm((T, UQ), BF),
        vm((FQ // HEAD_DIM * TB, TB * C * (C + 1) // 2), BF),
        vm((T, FQ), F32),
        vm((T, FQ), F32),
        vm((T, 3 * FQ), BF),
        vm((C - 1, TB, D), BF),
        vm((C - 1, TB, D), BF),
        vm((2, TB // 2, D), BF),
        vm((TB, D), F32),
        vm((TB, D), BF),
        vm((TB, D), BF),
        vm((8, TB), F32),
        vm((C, 8, TB), F32),
        vm((8, TB), F32),
        vm((TB, D), BF),
        vm((N, TB, D), BF),
        vm((TB, D), F32),
        vm((N, US, 2 * D), BF),
        vm((L, N + REACH - 2, US, 2 * D), BF),
        vm((US, 2 * D), F32),
        vm((C, RW, AW), F32),
        vm((C, N, RW, AW), BF),
        vm((L, N + REACH - 2, C, RW, AW), BF),
        vm((C - 1, RW, AW), BF),
        vm((L, C - 1, RW, AW), BF),
        vm((NR, D), F32),
        vm((NR, D), F32),
        vm((3, NR, D), BF),
        vm((3, C - 1, NR, D), BF),
        vm((3, NR, D), F32),
        vm((3, C - 1, NR, D), F32),
        dma((2,)), dma((2,)),
        dma((2,)), dma((2, C)),
        dma((2, C)), dma((2,)),
        dma((1,)), dma((N,)),
        dma((N,)), dma((1,)),
        dma((3 * L,)),
        dma((L, C - 1)), dma((L, C - 1)),
        dma((2, max(C - 1, 6))), dma((2, max(C - 1, 6))),
        dma((2, max(C - 1, 6))), dma((2, max(C - 1, 6))),
        dma((2 * L, 4 * REACH)), dma((2 * L, N)),
        dma((2 * L,)), dma((2 * L,)),
        dma((2 * L, 2 * N - 1)), dma((2 * L, N + REACH - 2)),
        dma((L,)), dma((L,)),
        dma((L, N)), dma((L, N)),
        dma((L,)), dma((L,)),
        dma((2,)), dma((2,)),
        dma((2,)), dma((2,)),
        dma((2,)), dma((2,)),
        dma((2 * L + 3,)),
        pltpu.SemaphoreType.REGULAR((2,)),
    ]
    vspec = pl.BlockSpec(memory_space=pltpu.VMEM)
    anyspec = pl.BlockSpec(memory_space=pl.ANY)
    shapes = (
        jax.ShapeDtypeStruct((TB, D), BF),
        jax.ShapeDtypeStruct((TB, D), F32),
        jax.ShapeDtypeStruct((L, RW, 3 * D), F32),
        jax.ShapeDtypeStruct((L, RW, D), F32),
        jax.ShapeDtypeStruct((L, US, 2 * D), F32),
        jax.ShapeDtypeStruct((L, 8, RW), F32),
    )
    outs = pl.pallas_call(
        partial(kernel_body, (C, N, TB, D, FQ, UQ, RW, US, AW)),
        out_shape=shapes,
        in_specs=[anyspec] * 2 + [vspec] * 3 + [anyspec] * 5,
        out_specs=(anyspec,) * 5 + (vspec,),
        scratch_shapes=scratch,
        compiler_params=pltpu.CompilerParams(
            collective_id=0, has_side_effects=True, vmem_limit_bytes=127 << 19
        ),
    )(
        hidden_in, grad_output, corpus_id.reshape(1, TB), corpus_weight.reshape(1, -1), norm_params.transpose(0, 2, 1),
        jnp.asarray(cosine), jnp.asarray(sine), w_qkv, w_proj, w_mlp,
    )
    outs = pl.pallas_call(
        copy_out,
        out_shape=shapes,
        in_specs=[anyspec] * len(shapes),
        out_specs=(anyspec,) * len(shapes),
        scratch_shapes=[vm(one.shape, one.dtype) for one in shapes] + [dma((4 * len(shapes),))],
        compiler_params=pltpu.CompilerParams(vmem_limit_bytes=60 << 20),
    )(*outs)
    return (*outs[:5], outs[5].transpose(0, 2, 1))


def solution(mesh):
    rows = P(("wide", "narrow"), None)
    layered = P(None, ("wide", "narrow"), None)
    return jax.shard_map(
        partial(body, mesh),
        mesh=mesh,
        in_specs=(rows, layered, layered, layered, layered, rows, P(("wide", "narrow")), P()),
        out_specs=(rows, rows, layered, layered, layered, layered),
        check_vma=False,
    )
```

```python
from functools import partial

import jax
import jax.numpy as jnp
import numpy as np
from jax import lax
from jax.experimental import pallas as pl
from jax.experimental.pallas import tpu as pltpu
from jax.sharding import PartitionSpec as P

HEADS = 16
HEAD_DIM = 64
FF = 4096
LAYERS = 2
EPS = 1e-05
MASKED = -1e30
ROPE_BASE = 10000.0
MESH = pl.DeviceIdType.MESH
BF = jnp.bfloat16
F32 = jnp.float32
LANES = 128
UNITS = 256


def dot_nn(left, right):
    return lax.dot_general(left, right, (((1,), (0,)), ((), ())), preferred_element_type=F32)


def dot_nt(left, right):
    return lax.dot_general(left, right, (((1,), (1,)), ((), ())), preferred_element_type=F32)


def dot_tn(left, right):
    return lax.dot_general(left, right, (((0,), (0,)), ((), ())), preferred_element_type=F32)


def normalize(inputs):
    centre = jnp.mean(inputs, axis=-1, keepdims=True)
    centered = inputs - centre
    rstd = lax.rsqrt(jnp.mean(centered * centered, axis=-1, keepdims=True) + EPS)
    return centered * rstd, rstd


def norm_back(nhat, rstd, grad, gain):
    scaled = grad * gain
    mean_f = jnp.mean(scaled, axis=-1, keepdims=True)
    mean_fn = jnp.mean(scaled * nhat, axis=-1, keepdims=True)
    return rstd * (scaled - mean_f - nhat * mean_fn)


GELU_S = 0.7978845608028654
GELU_A = 0.044715


def gelu(pre):
    return 0.5 * pre * (1.0 + jnp.tanh(GELU_S * (pre + GELU_A * pre * pre * pre)))


def gelu_slope(pre):
    square = pre * pre
    turned = jnp.tanh(GELU_S * (pre + GELU_A * pre * square))
    inner = GELU_S * (1.0 + 3.0 * GELU_A * square)
    return 0.5 * (1.0 + turned) + 0.5 * pre * (1.0 - turned * turned) * inner


def kernel_body(
    dims,
    hid_ref, gout_ref, ids_ref, cw_ref, nrm_ref, cos_in, sin_in, wq_ref, wp_ref, wm_ref,
    out_h, out_g, out_qkv, out_proj, out_mlp, out_n,
    cos_ref, sin_ref, held_qkv, held_proj,
    wa, wm, a1, a3, dm, db, qs_, ks_, vs_, att, st, br, mid, mo,
    pre_s, hid_s, dpre_s, p_s, dk_s, dv_s, dqkv,
    rs_send, rs_recv, rs_mid, acc, hid_p, g_p, sc_own, sc_x, sc_p, outh_s, hx, g,
    gmr, gmz, stage, stage_a, gar, gaz, gax_s, gax_r,
    npar, ngrad, nf_send, nf_recv, nb_send, nb_recv,
    perm_s, perm_r, gp_s, gp_r, gz_s, gz_r, oz_s, oz_r, op_s, op_r, loc, a2a_s, a2a_r, ag_s, ag_r, rs_s, rs_r,
    zw_s, zw_r, mw_s, mw_r, zg_s, zg_r, mga_s, mga_r, mgm_s, mgm_r, xg_s, xg_r,
    nx_s, nx_r, nz_s, nz_r, nm_s, nm_r, fin, credit,
):
    C, N, TB, D, FQ, UQ, RW, US, AW = dims
    T = C * TB
    HPC = FQ // HEAD_DIM
    HALF = N * US
    REACH = N // 2
    w = lax.axis_index("wide")
    n = lax.axis_index("narrow")
    c = w // 2
    k = lax.rem(w, 2)
    mate = (2 * c + (1 - k), n)
    to_chip = n + k * (N - 1 - 2 * n)
    to_plane = c + k * (N - 1 - 2 * c)
    swap = (2 * to_chip + k, to_plane)
    moves = to_chip != c

    def block(at):
        return at + k * (C - 1 - 2 * at)

    mine = block(c)

    def flipped(base, j, count):
        out, bit = 0, 1
        while bit < count:
            ours = lax.rem(base // bit, 2)
            flip = (j // bit) % 2 if isinstance(j, int) else lax.rem(j // bit, 2)
            out = out + bit * (ours + flip - 2 * ours * flip)
            bit *= 2
        return out

    def chip(j):
        return flipped(c, j, C)

    def xy(j):
        return (2 * chip(j) + k, n)

    def zdev(at):
        return (w, at)

    def remote(src, dst, ssem, rsem, device):
        return pltpu.make_async_remote_copy(
            src_ref=src, dst_ref=dst, send_sem=ssem, recv_sem=rsem,
            device_id=device, device_id_type=MESH,
        )

    def local(src, dst, sem):
        return pltpu.make_async_copy(src, dst, sem)

    barrier = pltpu.get_barrier_semaphore()
    partners = [xy(j) for j in range(1, C)] + [mate]
    partners += [zdev(lax.rem(n + j, N)) for j in range(1, N)]
    for device in partners:
        pl.semaphore_signal(barrier, inc=1, device_id=device, device_id_type=MESH)

    @pl.when(moves)
    def _():
        pl.semaphore_signal(barrier, inc=1, device_id=swap, device_id_type=MESH)

    pl.semaphore_wait(barrier, len(partners) + jnp.where(moves, 1, 0))

    rope = (
        local(cos_in, cos_ref, fin.at[2 * LAYERS + 1]), local(sin_in, sin_ref, fin.at[2 * LAYERS + 2])
    )
    for copy in rope:
        copy.start()

    def either(far, src, dst, ssem, rsem, device, act):
        @pl.when(far)
        def _():
            getattr(remote(src, dst, ssem, rsem, device), {"here": "wait_recv", "sent": "wait_send"}.get(act, act))()

        if act != "sent":
            @pl.when(jnp.logical_not(far))
            def _():
                getattr(local(src, dst, rsem), {"here": "wait"}.get(act, act))()

    def perm(i, act):
        src, dst = ((hid_ref, hid_p), (g_p, hid_p))[i]
        either(moves, src, dst, perm_s.at[i], perm_r.at[i], swap, act)

    holder = c == to_chip

    def grad_plane(act):
        for e, (src, dst) in enumerate(((gout_ref, db.at[c]), (sc_own, sc_x.at[c]))):
            either(jnp.logical_not(holder), src, dst, gp_s.at[e], gp_r.at[e, c], (2 * to_chip + k, n), act)

    def grad_held():
        for at in range(C):
            for e, dst in enumerate((db.at[at], sc_x.at[at])):
                either(c != at, dst, dst, gp_s.at[e], gp_r.at[e, at], (2 * at + k, n), "here")

    def grad_z(act):
        for at in range(C):
            plane = at + k * (N - 1 - 2 * at)
            for e, (src, dst) in enumerate(((db.at[at], g_p), (sc_x.at[at], sc_p))):
                either(plane != n, src, dst, gz_s.at[e, at], gz_r.at[e], (w, plane), act)

    def grad_here():
        for e, dst in enumerate((g_p, sc_p)):
            either(to_plane != n, dst, dst, gz_s.at[e, 0], gz_r.at[e], (w, to_plane), "here")

    def out_z(act):
        either(to_plane != n, outh_s, hx.at[n], oz_s.at[0], oz_r.at[n], (w, to_plane), act)

    def out_held():
        for at in range(N):
            either(n != at, hx.at[at], hx.at[at], oz_s.at[0], oz_r.at[at], (w, at), "here")

    def out_plane(act):
        for at in range(N):
            dest = at + k * (N - 1 - 2 * at)
            either(dest != c, hx.at[at], out_h, op_s.at[at], op_r.at[0], (2 * dest + k, n), act)

    def out_here():
        either(jnp.logical_not(holder), hx.at[0], out_h, op_s.at[0], op_r.at[0], (2 * to_chip + k, n), "here")

    perm(0, "start")

    def n_copy(way, axis, j):
        send, heard = (nf_send, nf_recv) if way == 0 else (nb_send, nb_recv)
        slot = n_slot[axis]
        if axis == "x":
            return remote(send.at[slot], heard.at[slot, j - 1], nx_s.at[way], nx_r.at[way], xy(j))
        if axis == "z":
            there = zdev(lax.rem(n + j, N))
            return remote(send.at[slot], heard.at[slot, j - 1], nz_s.at[way], nz_r.at[way], there)
        return remote(send.at[slot], heard.at[slot, j - 1], nm_s.at[way], nm_r.at[way], mate)

    n_count = {"x": C, "z": N, "m": 2}
    n_slot = {"x": 0, "z": 1, "m": 2}

    def n_start(way, axis, value):
        send = nf_send if way == 0 else nb_send
        send[n_slot[axis]] = value.astype(send.dtype)
        for j in range(1, n_count[axis]):
            n_copy(way, axis, j).start()

    def n_finish(way, axis):
        send, heard = (nf_send, nf_recv) if way == 0 else (nb_send, nb_recv)
        total = send[n_slot[axis]].astype(F32)
        whole = heard.at[n_slot[axis], pl.ds(0, n_count[axis] - 1)]
        ssem, rsem = {"x": (nx_s, nx_r), "z": (nz_s, nz_r), "m": (nm_s, nm_r)}[axis]
        remote(whole, whole, ssem.at[way], rsem.at[way], mate).wait()
        for j in range(1, n_count[axis]):
            total = total + heard[n_slot[axis], j - 1].astype(F32)
        return total

    first = (w * N + n) * RW
    spot = lax.broadcasted_iota(jnp.int32, (RW, D), 1) == (
        lax.broadcasted_iota(jnp.int32, (RW, D), 0) + first
    )
    spot = spot.astype(F32)
    n_start(0, "x", jnp.concatenate(
        [dot_nn(nrm_ref[l], spot.astype(BF)) for l in range(LAYERS)], axis=0
    ))

    def pieces(l, at):
        for part in range(3):
            cols = pl.ds(pl.multiple_of(part * D + at * FQ, LANES), FQ)
            yield wq_ref.at[l, :, cols], wa.at[l, c, k, n, :, pl.ds(part * FQ, FQ)]
        cols = pl.ds(pl.multiple_of(at * FQ, LANES), FQ)
        yield wp_ref.at[l, :, cols], wa.at[l, c, k, n, :, pl.ds(3 * FQ, FQ)]

    def a2a_start(l):
        for j in range(1, C):
            for src, dst in pieces(l, chip(j)):
                remote(src, dst, a2a_s.at[l, j - 1], a2a_r.at[l, j - 1], xy(j)).start()

    def a2a_all(l, j):
        there = wa.at[l, chip(j), k, n]
        return remote(there, there, a2a_s.at[l, j - 1], a2a_r.at[l, j - 1], xy(j))

    def own_wa(l):
        mine = wa.at[l, c, k, n]
        return local(mine, mine, loc.at[l])

    def own_wm(l):
        return local(wm_ref.at[l], wm.at[l, k, n], loc.at[LAYERS + l])

    a2a_start(0)
    for l in range(LAYERS):
        for src, dst in pieces(l, c):
            local(src, dst, loc.at[l]).start()
        own_wm(l).start()

    def shard(kind, l, core, at):
        return wm.at[l, core, at] if kind else wa.at[l, :, core, at]

    def inside(at):
        return (at >= 0) & (at < N)

    def signed(least, most):
        return [sign * d for d in range(most, least - 1, -1) for sign in (1, -1)]

    def zw_copy(kind, l, origin, at, slot):
        rows = shard(kind, l, k, origin)
        return remote(rows, rows, zw_s.at[2 * l + kind, slot], zw_r.at[2 * l + kind, origin], zdev(at))

    def direct_slot(d):
        return d + REACH

    def relay_slot(sign, q):
        return 2 * REACH + (q if sign > 0 else q + REACH - 1)

    def to_mate(kind, l, at):
        rows = shard(kind, l, k, at)
        return remote(rows, rows, mw_s.at[2 * l + kind], mw_r.at[2 * l + kind], mate)

    def mate_half(kind, l, core):
        rows = wm.at[l, core] if kind else wa.at[l, :, core]
        return remote(rows, rows, mw_s.at[2 * l + kind], mw_r.at[2 * l + kind], mate)

    def w_send(kind, l):
        for d in signed(1, REACH):
            @pl.when(inside(n + d))
            def _(d=d):
                zw_copy(kind, l, n, n + d, direct_slot(d)).start()

        to_mate(kind, l, n).start()

    def w_relay(kind, l):
        for sign in (1, -1):
            origin = n - sign * REACH

            @pl.when(inside(origin) & inside(n + sign))
            def _(sign=sign, origin=origin):
                zw_copy(kind, l, origin, n, 0).wait_recv()
                for q in range(1, REACH):
                    @pl.when(inside(n + sign * q))
                    def _(q=q):
                        zw_copy(kind, l, origin, n + sign * q, relay_slot(sign, q)).start()

    def w_arrive(kind, l):
        for d in reversed(signed(1, N - 1)):
            origin = n + d

            @pl.when(inside(origin))
            def _(d=d, origin=origin):
                if abs(d) == REACH:
                    sign = -1 if d > 0 else 1

                    @pl.when(jnp.logical_not(inside(n + sign)))
                    def _():
                        zw_copy(kind, l, origin, n, 0).wait_recv()
                else:
                    zw_copy(kind, l, origin, n, 0).wait_recv()
                to_mate(kind, l, origin).start()

    def w_ready(kind, l):
        mate_half(kind, l, 1 - k).wait_recv()

    def w_drain(kind, l):
        for d in signed(1, REACH):
            @pl.when(inside(n + d))
            def _(d=d):
                zw_copy(kind, l, n, n + d, direct_slot(d)).wait_send()

        for sign in (1, -1):
            origin = n - sign * REACH
            for q in range(1, REACH):
                @pl.when(inside(origin) & inside(n + sign) & inside(n + sign * q))
                def _(sign=sign, origin=origin, q=q):
                    zw_copy(kind, l, origin, n + sign * q, relay_slot(sign, q)).wait_send()

        mate_half(kind, l, k).wait_send()

    n_start(0, "z", n_finish(0, "x"))
    own_wa(0).wait()
    for j in range(1, C):
        a2a_all(0, j).wait_recv()
    w_send(0, 0)
    n_start(0, "m", n_finish(0, "z"))
    npar[...] = n_finish(0, "m")
    ngrad[...] = jnp.zeros_like(ngrad)

    def gain(l, col):
        return npar[pl.ds(l * 8 + col, 1), :]

    SPLIT = C == 4
    hops = ((1, 0), (1, 1), (2, 1), (2, 0), (2, 0), (1, 1))

    def ag_copy(p, buf, source, slot):
        if not SPLIT:
            rows = buf.at[block(source)]
            return remote(rows, rows, ag_s.at[lax.rem(p, 2), slot], ag_r.at[lax.rem(p, 2), slot], xy(slot + 1))
        j, part = hops[slot]
        rows = buf.at[block(source), pl.ds(part * (TB // 2), TB // 2)]
        return remote(rows, rows, ag_s.at[lax.rem(p, 2), slot], ag_r.at[lax.rem(p, 2), slot], xy(j))

    def ag_start(p, buf, value):
        buf[mine] = value
        for slot in (0, 2, 1, 3) if SPLIT else range(C - 1):
            ag_copy(p, buf, c, slot).start()

    def ag_pass(p, buf):
        if SPLIT:
            ag_copy(p, buf, chip(1), 0).wait_recv()
            ag_copy(p, buf, chip(1), 4).start()
            ag_copy(p, buf, chip(2), 2).wait_recv()
            ag_copy(p, buf, chip(2), 5).start()

    def ag_wait(p, buf, j):
        for slot in ((), (1,), (3,), (4, 5))[j] if SPLIT else (j - 1,) * min(j, 1):
            ag_copy(p, buf, chip(j), slot).wait_recv()

    def ag_drain(p, buf):
        for slot in range(4) if SPLIT else range(C - 1):
            ag_copy(p, buf, c, slot).wait_send()
        if SPLIT:
            ag_copy(p, buf, chip(1), 4).wait_send()
            ag_copy(p, buf, chip(2), 5).wait_send()

    def rs_copy(p, j):
        return remote(rs_send.at[j - 1], rs_recv.at[j - 1], rs_s.at[lax.rem(p, 2), j - 1], rs_r.at[lax.rem(p, 2), j - 1], xy(j))

    def rs_put(p, j, value):
        @pl.when(j > 0)
        def _():
            rs_send[j - 1] = value.astype(BF)
            rs_copy(p, j).start()

        @pl.when(j == 0)
        def _():
            acc[...] = value

    def rs_block(p, b, value):
        rs_put(p, chip(block(b)), value)

    def rs_pair(p, i, value):
        rs_put(p, 2 * i, value[0:TB])
        rs_send[2 * i] = value[TB:].astype(BF)
        rs_copy(p, 2 * i + 1).start()

    def half_copy(p, slot):
        part = pl.ds((0, 1, 1, 0, 0, 1)[slot] * (TB // 2), TB // 2)
        src = rs_send.at[(0, 0, 1, 1, 2, 2)[slot], part]
        dst = rs_mid.at[slot - 4] if slot >= 4 else rs_recv.at[(0, 0, 1, 1)[slot], part]
        return remote(src, dst, rs_s.at[lax.rem(p, 2), slot], rs_r.at[lax.rem(p, 2), slot], xy((1, 1, 2, 2, 1, 2)[slot]))

    def half_put(p, i, value):
        @pl.when(i == 0)
        def _():
            rs_send[2] = value.astype(BF)
            half_copy(p, 4).start()
            half_copy(p, 5).start()

        @pl.when(i == 1)
        def _():
            rs_send[0] = value.astype(BF)
            half_copy(p, 0).start()

        @pl.when(i == 2)
        def _():
            rs_send[1] = value.astype(BF)
            half_copy(p, 2).start()

        @pl.when(i == 3)
        def _():
            acc[...] = value

    def half_chip(i):
        return chip(jnp.where(i == 0, 3, jnp.where(i == 3, 0, i)))

    def half_pass(p):
        for slot, at, rows, onward in ((4, 1, pl.ds(0, TB // 2), 3), (5, 0, pl.ds(TB // 2, TB // 2), 1)):
            half_copy(p, slot).wait_recv()
            rs_send[at, rows] = (rs_send[at, rows].astype(F32) + rs_mid[slot - 4].astype(F32)).astype(BF)
            half_copy(p, onward).start()

    def rs_halves_finish(p):
        for slot in range(4):
            half_copy(p, slot).wait()
        half_copy(p, 4).wait_send()
        half_copy(p, 5).wait_send()
        return acc[...] + rs_recv[0].astype(F32) + rs_recv[1].astype(F32)

    def arrivals(p, buf, use):
        def step(i, carry):
            for at in range(C // 2):
                @pl.when(i == at)
                def _(at=at):
                    ag_wait(p, buf, 2 * at)
                    ag_wait(p, buf, 2 * at + 1)

            use(i, (block(chip(2 * i)), block(chip(2 * i + 1))))
            return carry

        lax.fori_loop(0, C // 2, step, 0)

    def both(ref, pair):
        return jnp.concatenate([ref[b] for b in pair], axis=0)

    def rs_finish(p):
        total = acc[...]
        for j in range(1, C):
            rs_copy(p, j).wait()
            total = total + rs_recv[j - 1].astype(F32)
        return total

    lane = lax.broadcasted_iota(jnp.int32, (TB, FQ), 1)
    low_half = lax.rem(lane, HEAD_DIM) < HEAD_DIM // 2
    head_of = lane // HEAD_DIM
    causal = lax.broadcasted_iota(jnp.int32, (HPC * TB, TB), 1) <= lax.rem(
        lax.broadcasted_iota(jnp.int32, (HPC * TB, TB), 0), TB
    )

    def tables(b):
        rows = pl.ds(b * TB, TB)
        reps = FQ // LANES
        return (
            jnp.concatenate([cos_ref[rows, :]] * reps, axis=1),
            jnp.concatenate([sin_ref[rows, :]] * reps, axis=1),
        )

    def swapped(u):
        half_dim = HEAD_DIM // 2
        return jnp.where(
            low_half, pltpu.roll(u, FQ - half_dim, 1), pltpu.roll(u, half_dim, 1)
        )

    def w_qkv(l):
        return wa[l, :, :, :, :, 0 : 3 * FQ].reshape(D, 3 * FQ)

    def w_proj(l):
        return wa[l, :, :, :, :, 3 * FQ : 4 * FQ].reshape(D, FQ)

    def w_up(l):
        return wm[l, :, :, :, 0:D].reshape(UQ, D)

    def w_down(l):
        return wm[l, :, :, :, D : 2 * D].reshape(UQ, D)

    def by_head(rows):
        return jnp.concatenate(
            [jnp.where(head_of == h, rows, jnp.zeros((), rows.dtype)) for h in range(HPC)], axis=0
        )

    def of_heads(stacked):
        out = stacked[0:TB]
        for h in range(1, HPC):
            out = jnp.where(head_of == h, stacked[h * TB : (h + 1) * TB], out)
        return out

    def exp_scores(l, b):
        scores = dot_nt(by_head(qs_[l, b]), ks_[l, 0 : b + 1].reshape((b + 1) * TB, FQ))
        last = jnp.where(causal, scores[:, b * TB :], MASKED)
        scores = jnp.concatenate([scores[:, : b * TB], last], axis=1) if b else last
        weights = jnp.exp(scores - jnp.max(scores, axis=-1, keepdims=True))
        return weights, 1.0 / jnp.sum(weights, axis=-1, keepdims=True)

    w_relay(0, 0)
    own_wm(0).wait()
    w_send(1, 0)
    perm(0, "here")
    st[0] = hid_p[...].astype(F32)
    ids = jnp.broadcast_to(ids_ref[...], (8, TB))
    scale = jnp.zeros((8, TB), F32)
    for i in range(cw_ref.shape[1]):
        scale = jnp.where(ids == i, cw_ref[:, i : i + 1], scale)
    sc_own[...] = scale
    for copy in rope:
        copy.wait()

    def grad_move():
        @pl.when(holder)
        def _():
            grad_held()
            grad_z("start")

    def forward(l, carry):
        p = 2 * l
        more = l + 1 < LAYERS
        nhat, unused = normalize(st[l])
        ag_start(p, a1.at[l], (nhat * gain(l, 0) + gain(l, 1)).astype(BF))

        @pl.when(l == 0)
        def _():
            a2a_start(1)

        ag_pass(p, a1.at[l])

        @pl.when(l == 0)
        def _():
            grad_plane("start")

        w_arrive(0, l)
        w_ready(0, l)

        def qkv_step(i, pair):
            u = dot_nn(both(a1.at[l], pair), w_qkv(l))
            for e, b in enumerate(pair):
                cosine, sine = tables(b)
                uq = u[e * TB : (e + 1) * TB, 0:FQ]
                uk = u[e * TB : (e + 1) * TB, FQ : 2 * FQ]
                uq = (uq * cosine + swapped(uq) * sine).astype(BF)
                qs_[l, b] = (uq * HEAD_DIM ** (-0.5)).astype(BF)
                ks_[l, b] = (uk * cosine + swapped(uk) * sine).astype(BF)
                vs_[l, b] = u[e * TB : (e + 1) * TB, 2 * FQ :].astype(BF)

        arrivals(p, a1.at[l], qkv_step)
        def attend(b):
            weights, inverse = exp_scores(l, b)
            mixed = dot_nn(weights.astype(BF), vs_[l, 0 : b + 1].reshape((b + 1) * TB, FQ))
            low = of_heads(mixed * inverse).astype(BF)
            att[l, b] = low
            return dot_nt(low, w_proj(l))

        if SPLIT:

            def attend_step(i, carry):
                for b in range(C):
                    @pl.when(block(half_chip(i)) == b)
                    def _(b=b):
                        acc[...] = attend(b)

                half_put(p, i, acc[...])
                return carry

            lax.fori_loop(0, C, attend_step, 0)
            half_pass(p)
        else:
            for b in range(C):
                rs_block(p, b, attend(b))
        w_relay(1, l)

        @pl.when(more)
        def _():
            own_wa(l + 1).wait()
            for j in range(1, C):
                a2a_all(l + 1, j).wait_recv()
            w_send(0, l + 1)

        branch = (rs_halves_finish if SPLIT else rs_finish)(p)
        br[l] = branch
        nhat, unused = normalize(branch)
        middle = st[l] + nhat * gain(l, 2) + gain(l, 3)
        mid[l] = middle
        nhat, unused = normalize(middle)
        ag_start(p + 1, a3.at[l], (nhat * gain(l, 4) + gain(l, 5)).astype(BF))
        ag_drain(p, a1.at[l])
        ag_pass(p + 1, a3.at[l])
        w_arrive(1, l)


        def feed(x, core):
            up = wm[l, core, :, :, 0:D].reshape(N * US, D)
            down = wm[l, core, :, :, D : 2 * D].reshape(N * US, D)
            return dot_nn(gelu(dot_nt(x, up)).astype(BF), down)

        if SPLIT:
            for j in range(1, C):
                ag_wait(p + 1, a3.at[l], j)
            pre_s[...] = feed(a3[l].reshape(T, D), k)
            w_ready(1, l)

            def feed_step(i, carry):
                pair = (block(half_chip(2 * i)), block(half_chip(2 * i + 1)))
                value = feed(both(a3.at[l], pair), 1 - k)
                value = value + jnp.concatenate([pre_s[pl.ds(b * TB, TB), :] for b in pair], axis=0)
                half_put(p + 1, 2 * i, value[0:TB])
                half_put(p + 1, 2 * i + 1, value[TB:])
                return carry

            lax.fori_loop(0, 2, feed_step, 0)

            @pl.when(jnp.logical_not(more))
            def _():
                grad_move()

            half_pass(p + 1)
        else:
            @pl.when(jnp.logical_not(more))
            def _():
                grad_move()

            w_ready(1, l)
            arrivals(p + 1, a3.at[l], lambda i, pair: rs_pair(
                p + 1, i, feed(both(a3.at[l], pair), k) + feed(both(a3.at[l], pair), 1 - k)
            ))

        @pl.when(more)
        def _():
            w_relay(0, l + 1)
            own_wm(l + 1).wait()
            w_send(1, l + 1)

        mlp_out = (rs_halves_finish if SPLIT else rs_finish)(p + 1)
        mo[l] = mlp_out

        @pl.when(more)
        def _():
            nhat, unused = normalize(mlp_out)
            st[l + 1] = mid[l] + nhat * gain(l, 6) + gain(l, 7)

        ag_drain(p + 1, a3.at[l])
        return carry

    lax.fori_loop(0, LAYERS, forward, 0)
    def add_norm(l, col, grad, nhat):
        ngrad[pl.ds(l * 8 + col, 1), :] = jnp.sum(grad * nhat, axis=0, keepdims=True)
        ngrad[pl.ds(l * 8 + col + 1, 1), :] = jnp.sum(grad, axis=0, keepdims=True)

    def gm_mate(l, at):
        return remote(wm.at[l + 1, 1 - k, at], gmr.at[at], mgm_s.at[l, at], mgm_r.at[l, at], mate)

    def ga_all(l):
        dst = wa.at[l + 1]
        rows = 2 * N * RW

        def chunk(i, carry):
            off = pl.multiple_of(i * rows, LANES)
            grad_a = dot_tn(a1[l, :, :, pl.ds(off, rows)].reshape(T, rows), dqkv[...])
            grad_p = dot_tn(db[:, :, pl.ds(off, rows)].reshape(T, rows), att[l].reshape(T, FQ))
            dst[i, :, :, :, 0 : 3 * FQ] = grad_a.astype(BF).reshape(2, N, RW, 3 * FQ)
            dst[i, :, :, :, 3 * FQ : 4 * FQ] = grad_p.astype(BF).reshape(2, N, RW, FQ)
            return carry

        lax.fori_loop(0, C, chunk, 0)

    def ga_mate(l):
        return remote(wa.at[l + 1, :, 1 - k], gar, mga_s.at[l], mga_r.at[l], mate)

    def zpart(kind, l, at):
        return wm.at[l + 1, k, at] if kind else wa.at[l + 1, :, k, at]

    def zbuf(kind, l, slot):
        return gmz.at[l, slot] if kind else gaz.at[l, slot]

    def zg_copy(kind, l, owner, device, send, recv):
        ssem, rsem = zg_s.at[2 * l + kind, send], zg_r.at[2 * l + kind, recv]
        return remote(zpart(kind, l, owner), zbuf(kind, l, recv), ssem, rsem, zdev(device))

    def z_direct(kind, l, d):
        return zg_copy(kind, l, n + d, n + d, d + N - 1, (-d) % N - 1)

    def z_beyond(kind, l, d):
        sign = 1 if d > 0 else -1
        return zg_copy(kind, l, n + d, n + d - sign * REACH, d + N - 1, N - 1 + abs(d) - REACH - 1)

    def z_spread(kind, l):
        for d in signed(1, N - 1):
            ready = inside(n + d)
            if abs(d) == REACH:
                ready = ready & jnp.logical_not(inside(n - d // REACH))

            @pl.when(ready)
            def _(d=d):
                (z_beyond if abs(d) > REACH else z_direct)(kind, l, d).start()

    def z_relay(kind, l):
        for sign in (1, -1):
            owner = n + sign * REACH

            @pl.when(inside(owner) & inside(n - sign))
            def _(sign=sign, owner=owner):
                part = zpart(kind, l, owner)
                for q in range(1, REACH):
                    @pl.when(inside(n - sign * q))
                    def _(q=q):
                        slot = N - 1 + q - 1
                        zg_copy(kind, l, n, n, 0, slot).wait_recv()
                        part[...] = (part[...].astype(F32) + zbuf(kind, l, slot)[...].astype(F32)).astype(BF)
                z_direct(kind, l, sign * REACH).start()

    def z_arrive(kind, l, add):
        for d in reversed(signed(1, REACH)):
            @pl.when(inside(n + d))
            def _(d=d):
                slot = d % N - 1
                zg_copy(kind, l, n, n, 0, slot).wait_recv()
                add(zbuf(kind, l, slot))

    def z_drain(kind, l):
        for d in signed(1, N - 1):
            @pl.when(inside(n + d))
            def _(d=d):
                (z_beyond if abs(d) > REACH else z_direct)(kind, l, d).wait_send()

    def gm_add(l, at):
        gm_mate(l, at).wait_recv()
        src = wm.at[l + 1]
        src[k, at] = (src[k, at].astype(F32) + gmr[at].astype(F32)).astype(BF)
        dist = jnp.where(at > n, at - n, n - at)
        sign = jnp.where(at > n, 1, -1)
        beyond = dist > REACH
        device = jnp.where(beyond, at - sign * REACH, at)
        slot = jnp.where(beyond, N - 2 + dist - REACH, lax.rem(n - at + N, N) - 1)

        @pl.when((dist != 0) & ((dist != REACH) | jnp.logical_not(inside(n - sign))))
        def _():
            zg_copy(1, l, at, device, at - n + N - 1, slot).start()

    def gm_all(l):
        dst = wm.at[l + 1]
        per = UNITS // US
        count = HALF // UNITS
        far = flipped(n, N - 1, N)

        def chunk(i, carry):
            core = jnp.where(i < count, 1 - k, k)
            at = flipped(far // per, lax.rem(i, count), count)
            off = pl.multiple_of(core * HALF + at * UNITS, LANES)
            up = dot_tn(dpre_s[:, pl.ds(off, UNITS)], a3[l].reshape(T, D))
            down = dot_tn(hid_s[:, pl.ds(off, UNITS)], dm[...].reshape(T, D))
            rows = pl.ds(at * per, per)
            dst[core, rows, :, 0:D] = up.astype(BF).reshape(per, US, D)
            dst[core, rows, :, D : 2 * D] = down.astype(BF).reshape(per, US, D)

            def owners(e, carry):
                owner = at * per + flipped(lax.rem(far, per), e, per)

                @pl.when(i < count)
                def _():
                    gm_mate(l, owner).start()

                @pl.when(i >= count)
                def _():
                    gm_add(l, owner)

                return carry

            lax.fori_loop(0, per, owners, 0)
            return carry

        lax.fori_loop(0, 2 * count, chunk, 0)

    def ga_spread(l):
        ga_mate(l).wait_recv()
        src = wa.at[l + 1]
        src[:, k] = (src[:, k].astype(F32) + gar[...].astype(F32)).astype(BF)
        z_spread(0, l)

    def gm_out(l):
        return local(stage, out_mlp.at[l], loc.at[2 * LAYERS + l])

    def gm_finish(l):
        stage[...] = wm[l + 1, k, n].astype(F32)

        def add(ref):
            stage[...] += ref[...].astype(F32)

        z_arrive(1, l, add)
        gm_out(l).start()
        z_drain(1, l)
        for at in range(N):
            gm_mate(l, at).wait_send()

    def xg(l, j):
        return remote(gax_s.at[j - 1], gax_r.at[l, j - 1], xg_s.at[l], xg_r.at[l], xy(j))

    def place(l, at, value):
        for part in range(3):
            cols = pl.ds(pl.multiple_of(part * D + at * FQ, LANES), FQ)
            held_qkv[:, cols] = value[:, part * FQ : (part + 1) * FQ]
        held_proj[:, pl.ds(pl.multiple_of(at * FQ, LANES), FQ)] = value[:, 3 * FQ : 4 * FQ]

    def ga_finish(l):
        stage_a[...] = wa[l + 1, :, k, n].astype(F32)

        def add(ref):
            stage_a[...] += ref[...].astype(F32)

        z_arrive(0, l, add)
        z_drain(0, l)
        ga_mate(l).wait_send()
        for j in range(1, C):
            gax_s[j - 1] = stage_a[chip(j)].astype(BF)
            xg(l, j).start()
        place(l, c, stage_a[c])

    def ga_out(l):
        return (
            local(held_qkv, out_qkv.at[l], fin.at[2 * l]),
            local(held_proj, out_proj.at[l], fin.at[2 * l + 1]),
        )

    def ga_place(l):
        remote(gax_s, gax_r.at[l], xg_s.at[l], xg_r.at[l], mate).wait()
        for j in range(1, C):
            place(l, chip(j), gax_r[l, j - 1].astype(F32))
        for copy in ga_out(l):
            copy.start()

    def backward(i, carry):
        l = LAYERS - 1 - i
        p = 2 * LAYERS + 2 * i
        nhat, rstd = normalize(mo[l])

        @pl.when(i == 0)
        def _():
            grad_here()
            here = lax.broadcasted_iota(jnp.int32, (TB, TB), 0) == lax.broadcasted_iota(jnp.int32, (TB, TB), 1)
            column = jnp.sum(
                jnp.where(here, jnp.broadcast_to(sc_p[0:1, :], (TB, TB)), 0.0), axis=1, keepdims=True
            )
            g[...] = g_p[...].astype(F32) * column

        grad = g[...]
        ag_start(p, dm, norm_back(nhat, rstd, grad, gain(l, 6)).astype(BF))
        add_norm(l, 6, grad, nhat)

        @pl.when(i == 0)
        def _():
            outh_s[...] = (mid[l] + nhat * gain(l, 6) + gain(l, 7)).astype(BF)
            out_z("start")

        ag_pass(p, dm)

        @pl.when((i == 0) & holder)
        def _():
            grad_z("sent")


        def redo(i, carry):
            pre = dot_nt(a3[l, pl.ds(2 * i, 2)].reshape(2 * TB, D), w_up(l))
            rows = pl.ds(i * 2 * TB, 2 * TB)
            pre_s[rows, :] = pre
            hid_s[rows, :] = gelu(pre).astype(BF)
            return carry

        lax.fori_loop(0, C // 2, redo, 0)

        @pl.when(i > 0)
        def _():
            z_relay(0, l + 1)


        def feed_back(i, pair):
            where = [pl.ds(b * TB, TB) for b in pair]
            pre = jnp.concatenate([pre_s[rows, :] for rows in where], axis=0)
            slope = (dot_nt(both(dm, pair), w_down(l)) * gelu_slope(pre)).astype(BF)
            for e, rows in enumerate(where):
                dpre_s[rows, :] = slope[e * TB : (e + 1) * TB]
            value = dot_nn(slope, w_up(l))
            if SPLIT:
                half_put(p, jnp.where(i == 0, 3, 2), value[0:TB])
                half_put(p, jnp.where(i == 0, 1, 0), value[TB:])
            else:
                rs_pair(p, i, value)

        arrivals(p, dm, feed_back)

        @pl.when(i > 0)
        def _():
            pl.semaphore_wait(credit.at[1], 1)

        gm_all(l)
        if SPLIT:
            half_pass(p)

        @pl.when(l > 0)
        def _():
            pl.semaphore_signal(credit.at[1], inc=1, device_id=mate, device_id_type=MESH)

        d_a3 = (rs_halves_finish if SPLIT else rs_finish)(p)
        nhat, rstd = normalize(mid[l])
        d_mid = g[...] + norm_back(nhat, rstd, d_a3, gain(l, 4))
        g[...] = d_mid
        nhat_b, rstd_b = normalize(br[l])
        ag_start(p + 1, db, norm_back(nhat_b, rstd_b, d_mid, gain(l, 2)).astype(BF))
        add_norm(l, 4, d_a3, nhat)
        add_norm(l, 2, d_mid, nhat_b)
        ag_drain(p, dm)
        for b in range(C):
            weights, inverse = exp_scores(l, b)
            cols = pl.ds(TB * (b * (b + 1) // 2), (b + 1) * TB)
            p_s[:, cols] = (weights * inverse).astype(BF)
        dk_s[...] = jnp.zeros_like(dk_s)
        dv_s[...] = jnp.zeros_like(dv_s)
        ag_pass(p + 1, db)
        for j in range(1, C):
            ag_wait(p + 1, db, j)
        for b in reversed(range(C)):
            size = (b + 1) * TB
            rows = pl.ds(b * TB, TB)
            seen = pl.ds(0, size)
            d_att = by_head(dot_nn(db[b], w_proj(l)).astype(BF))
            d_probs = dot_nt(d_att, vs_[l, 0 : b + 1].reshape(size, FQ))
            low = p_s[:, pl.ds(TB * (b * (b + 1) // 2), size)]
            probs = low.astype(F32)
            delta = jnp.sum(probs * d_probs, axis=-1, keepdims=True)
            d_scores = (probs * (d_probs - delta)).astype(BF)
            d_query = of_heads(dot_nn(d_scores, ks_[l, 0 : b + 1].reshape(size, FQ)))
            d_query = d_query * HEAD_DIM ** (-0.5)
            dk_s[seen, :] += dot_tn(d_scores, by_head(qs_[l, b]))
            dv_s[seen, :] += dot_tn(low, d_att)
            d_key = dk_s[rows, :]
            cosine, sine = tables(b)
            dqkv[rows, 0:FQ] = (d_query * cosine - swapped(d_query) * sine).astype(BF)
            dqkv[rows, FQ : 2 * FQ] = (d_key * cosine - swapped(d_key) * sine).astype(BF)
            dqkv[rows, 2 * FQ : 3 * FQ] = dv_s[rows, :].astype(BF)
            value = dot_nt(dqkv[rows, :], w_qkv(l))
            if SPLIT:
                j = flipped(c, block(b), C)
                half_put(p + 1, jnp.where(j == 3, 0, jnp.where(j == 0, 3, j)), value)
            else:
                rs_block(p + 1, b, value)
        z_relay(1, l)

        @pl.when(i > 0)
        def _():
            pl.semaphore_wait(credit.at[0], 1)

        ga_all(l)
        ga_mate(l).start()
        if SPLIT:
            half_pass(p + 1)

        @pl.when(i > 0)
        def _():
            gm_finish(l + 1)
            ga_finish(l + 1)

        ga_spread(l)

        @pl.when(l > 0)
        def _():
            pl.semaphore_signal(credit.at[0], inc=1, device_id=mate, device_id_type=MESH)


        @pl.when((i == LAYERS - 1) & holder)
        def _():
            out_held()
            out_plane("start")

        d_a1 = (rs_halves_finish if SPLIT else rs_finish)(p + 1)
        nhat, rstd = normalize(st[l])
        g[...] = g[...] + norm_back(nhat, rstd, d_a1, gain(l, 0))
        add_norm(l, 0, d_a1, nhat)
        ag_drain(p + 1, db)

        @pl.when(i == 0)
        def _():
            for kind in range(2):
                for at in range(LAYERS):
                    w_drain(kind, at)
            perm(0, "sent")
            grad_plane("sent")


        return carry

    lax.fori_loop(0, LAYERS, backward, 0)

    g_p[...] = g[...].astype(BF)
    n_start(1, "m", ngrad[...])

    z_relay(0, 0)
    n_start(1, "x", n_finish(1, "m"))
    gm_out(1).wait()
    gm_finish(0)
    perm(1, "start")
    n_start(1, "z", n_finish(1, "x"))
    ga_place(1)

    for copy in ga_out(1):
        copy.wait()
    ga_finish(0)
    total = n_finish(1, "z")
    for l in range(LAYERS):
        out_n[l] = lax.dot_general(
            total[l * 8 : (l + 1) * 8], spot, (((1,), (1,)), ((), ())),
            preferred_element_type=F32, precision=lax.Precision.HIGHEST,
        )
    ga_place(0)
    gm_out(0).wait()

    for l in range(LAYERS):
        for j in range(1, C):
            a2a_all(l, j).wait_send()
    perm(1, "here")
    g[...] = hid_p[...].astype(F32)
    grad_out = local(g, out_g, fin.at[2 * LAYERS])
    grad_out.start()
    perm(1, "sent")
    out_z("sent")
    out_here()

    @pl.when(holder)
    def _():
        out_plane("sent")

    for copy in ga_out(0):
        copy.wait()
    grad_out.wait()


def copy_out(*refs):
    count = (len(refs) - 1) // 3
    sems = refs[-1]
    into, out = [], []
    for i in sorted(range(count), key=lambda i: -refs[i].size):
        src, dst, held = refs[i], refs[count + i], refs[2 * count + i]
        cuts = [()]
        if len(held.shape) == 3:
            half = held.shape[1] // 4 if held.shape[1] >= 128 else held.shape[1]
            cuts = [(l, pl.ds(at, half)) for l in range(held.shape[0]) for at in range(0, held.shape[1], half)]
        for at in cuts:
            one, two, three = (ref.at[at] if at else ref for ref in (src, held, dst))
            into.append(pltpu.make_async_copy(one, two, sems.at[2 * len(into)]))
            out.append(pltpu.make_async_copy(two, three, sems.at[2 * len(out) + 1]))
    for copy in into:
        copy.start()
    for first, second in zip(into, out):
        first.wait()
        second.start()
    for copy in out:
        copy.wait()


def body(mesh, hidden_in, w_qkv, w_proj, w_mlp, norm_params, grad_output, corpus_id, corpus_weight):
    W, N = mesh.shape["wide"], mesh.shape["narrow"]
    C = W // 2
    TB, D = hidden_in.shape
    FQ, UQ, RW, US = D // C, FF // C, D // (W * N), FF // (W * N)
    AW = 4 * FQ
    T = C * TB
    REACH = N // 2
    assert C == N and w_mlp.shape[1] == US and w_qkv.shape[1] == RW

    half = HEAD_DIM // 2
    freqs = np.float32(ROPE_BASE) ** (-np.arange(half, dtype=np.float32) / np.float32(half))
    angles = (np.arange(T, dtype=np.float32)[:, None] * freqs[None, :]).astype(np.float32)
    cosine = np.tile(np.cos(angles), (1, LANES // half)).astype(np.float32)
    sine = np.sin(angles)
    sine = np.tile(np.concatenate([-sine, sine], axis=1), (1, LANES // HEAD_DIM)).astype(np.float32)

    NR = LAYERS * 8
    dma = pltpu.SemaphoreType.DMA
    vm = pltpu.VMEM
    L = LAYERS
    scratch = [
        vm((T, LANES), F32),
        vm((T, LANES), F32),
        vm((RW, 3 * D), F32),
        vm((RW, D), F32),
        vm((L + 1, C, 2, N, RW, AW), BF),
        vm((L + 1, 2, N, US, 2 * D), BF),
        vm((L, C, TB, D), BF),
        vm((L, C, TB, D), BF),
        vm((C, TB, D), BF),
        vm((C, TB, D), BF),
        vm((L, C, TB, FQ), BF),
        vm((L, C, TB, FQ), BF),
        vm((L, C, TB, FQ), BF),
        vm((L, C, TB, FQ), BF),
        vm((L, TB, D), F32),
        vm((L, TB, D), F32),
        vm((L, TB, D), F32),
        vm((L, TB, D), F32),
        vm((T, UQ), F32),
        vm((T, UQ), BF),
        vm((T, UQ), BF),
        vm((FQ // HEAD_DIM * TB, TB * C * (C + 1) // 2), BF),
        vm((T, FQ), F32),
        vm((T, FQ), F32),
        vm((T, 3 * FQ), BF),
        vm((C - 1, TB, D), BF),
        vm((C - 1, TB, D), BF),
        vm((2, TB // 2, D), BF),
        vm((TB, D), F32),
        vm((TB, D), BF),
        vm((TB, D), BF),
        vm((8, TB), F32),
        vm((C, 8, TB), F32),
        vm((8, TB), F32),
        vm((TB, D), BF),
        vm((N, TB, D), BF),
        vm((TB, D), F32),
        vm((N, US, 2 * D), BF),
        vm((L, N + REACH - 2, US, 2 * D), BF),
        vm((US, 2 * D), F32),
        vm((C, RW, AW), F32),
        vm((C, N, RW, AW), BF),
        vm((L, N + REACH - 2, C, RW, AW), BF),
        vm((C - 1, RW, AW), BF),
        vm((L, C - 1, RW, AW), BF),
        vm((NR, D), F32),
        vm((NR, D), F32),
        vm((3, NR, D), BF),
        vm((3, C - 1, NR, D), BF),
        vm((3, NR, D), F32),
        vm((3, C - 1, NR, D), F32),
        dma((2,)), dma((2,)),
        dma((2,)), dma((2, C)),
        dma((2, C)), dma((2,)),
        dma((1,)), dma((N,)),
        dma((N,)), dma((1,)),
        dma((3 * L,)),
        dma((L, C - 1)), dma((L, C - 1)),
        dma((2, max(C - 1, 6))), dma((2, max(C - 1, 6))),
        dma((2, max(C - 1, 6))), dma((2, max(C - 1, 6))),
        dma((2 * L, 4 * REACH)), dma((2 * L, N)),
        dma((2 * L,)), dma((2 * L,)),
        dma((2 * L, 2 * N - 1)), dma((2 * L, N + REACH - 2)),
        dma((L,)), dma((L,)),
        dma((L, N)), dma((L, N)),
        dma((L,)), dma((L,)),
        dma((2,)), dma((2,)),
        dma((2,)), dma((2,)),
        dma((2,)), dma((2,)),
        dma((2 * L + 3,)),
        pltpu.SemaphoreType.REGULAR((2,)),
    ]
    vspec = pl.BlockSpec(memory_space=pltpu.VMEM)
    anyspec = pl.BlockSpec(memory_space=pl.ANY)
    shapes = (
        jax.ShapeDtypeStruct((TB, D), BF),
        jax.ShapeDtypeStruct((TB, D), F32),
        jax.ShapeDtypeStruct((L, RW, 3 * D), F32),
        jax.ShapeDtypeStruct((L, RW, D), F32),
        jax.ShapeDtypeStruct((L, US, 2 * D), F32),
        jax.ShapeDtypeStruct((L, 8, RW), F32),
    )
    outs = pl.pallas_call(
        partial(kernel_body, (C, N, TB, D, FQ, UQ, RW, US, AW)),
        out_shape=shapes,
        in_specs=[anyspec] * 2 + [vspec] * 3 + [anyspec] * 5,
        out_specs=(anyspec,) * 5 + (vspec,),
        scratch_shapes=scratch,
        compiler_params=pltpu.CompilerParams(
            collective_id=0, has_side_effects=True, vmem_limit_bytes=127 << 19
        ),
    )(
        hidden_in, grad_output, corpus_id.reshape(1, TB), corpus_weight.reshape(1, -1), norm_params.transpose(0, 2, 1),
        jnp.asarray(cosine), jnp.asarray(sine), w_qkv, w_proj, w_mlp,
    )
    outs = pl.pallas_call(
        copy_out,
        out_shape=shapes,
        in_specs=[anyspec] * len(shapes),
        out_specs=(anyspec,) * len(shapes),
        scratch_shapes=[vm(one.shape, one.dtype) for one in shapes] + [dma((6 * len(shapes),))],
        compiler_params=pltpu.CompilerParams(vmem_limit_bytes=60 << 20),
    )(*outs)
    return (*outs[:5], outs[5].transpose(0, 2, 1))


def solution(mesh):
    rows = P(("wide", "narrow"), None)
    layered = P(None, ("wide", "narrow"), None)
    return jax.shard_map(
        partial(body, mesh),
        mesh=mesh,
        in_specs=(rows, layered, layered, layered, layered, rows, P(("wide", "narrow")), P()),
        out_specs=(rows, rows, layered, layered, layered, layered),
        check_vma=False,
    )
```
